256 devices in a mesh: gx: 32 (over z, x), gy: 8 (over y, core).
Axes of the slice: x: 4, y: 4, z: 8, core: 2. Of those that a mesh axis runs over, the one named last changes fastest.
Arguments:
- field: float32 [36, 128, 4096], P(None, 'gx', 'gy'), may hold values from -6 to 6
- mix_weights: float32 [2, 36, 36, 32, 1024], P(None, None, None, 'gx', 'gy'), may hold values from -0.75 to 0.75
- kept_z: int32 [1024], P('gy'), may hold values from 1 to 32, as said below
- conv_kernels: float32 [3, 27, 36, 36], replicated, may hold values from -0.1875 to 0.1875
Outputs:
- layer_out: float32 [36, 128, 4096], P(None, 'gx', 'gy')
The draws below stay inside these ranges and needn't reach their ends.
Inputs may be any that keep to these rules, and one draw needn't show every extreme that they name: kept_z[j * 32 + l] counts the lowest z modes kept for the j-th kept x mode and the l-th kept y mode; one entry equals 32.
All inputs are finite; a program needn't handle non-finite values.
Results may differ from the reference program's by a relative error of at most 0.0001.
Values sent between devices are 32-bit elements; how exact they have to be, the bound alone decides.
No kernel may reach another device: no remote copies, remote signals or barrier semaphores. Data moves between devices by JAX's collectives and lax.ppermute only.
A program may use at most 128 MiB of HBM per device.

```python
import math
import jax
import jax.numpy as jnp
from jax import lax

C = 36
NZ = 64
KY = 32
NX = 128
NY = 64
MZ = 32
KX = 32


def draw_kept_z(key, part):
    key_counts, key_chosen = jax.random.split(jax.random.fold_in(key, 17))
    counts = jax.random.randint(key_counts, (KX * KY,), 1, MZ + 1)
    chosen = jax.random.randint(key_chosen, (), 0, KX * KY)
    return jnp.where(jnp.arange(KX * KY) == chosen, MZ, counts).astype(jnp.int32)


def levels(stream_key, extent, cuts, low, top_value):
    level = 1.0
    for position, parts in cuts:
        draws = jax.random.uniform(jax.random.fold_in(jax.random.fold_in(stream_key, 6), position), (parts,), jnp.float32, low / len(cuts), top_value / len(cuts))
        level = level * jnp.repeat(jnp.exp(draws), extent[position] // parts).reshape((-1,) + (1,) * (len(extent) - 1 - position))
    return level


def noise(rng, extent, width, bound, pieces=(), kind=jnp.bfloat16):
    values = width * jax.random.normal(rng, extent, jnp.float32)
    if pieces:
        values = values * levels(rng, extent, pieces, -0.22, 0.18)
    return jnp.clip(values, -bound, bound).astype(kind)


def setup_inputs(seed: int = 0) -> dict:
    key_list = jax.random.split(jax.random.key(seed), 5)
    field = noise(key_list[0], (C, NX, NY * NZ), 1.0, 6.0, ((1, 32), (2, 8)), jnp.float32)
    mix_weights = noise(key_list[1], (2, C, C, MZ, KX * KY), (2 * C) ** -0.5, 0.75, ((3, 32), (4, 8)), jnp.float32)
    kept_z = draw_kept_z(jax.random.fold_in(key_list[4], 71), 0)
    conv_kernels = noise(key_list[3], (3, 27, C, C), (27 * C) ** -0.5, 0.1875, (), jnp.float32)
    return {"field": field, "mix_weights": mix_weights, "kept_z": kept_z, "conv_kernels": conv_kernels}


precise = lax.Precision.HIGHEST

def kept_frequencies(count, length):
    index = jnp.arange(count, dtype=jnp.int32)
    return jnp.where(index < count // 2, index, length - count + index).astype(jnp.int32)

def inverse_table(frequencies, length):
    positions = jnp.arange(length, dtype=jnp.int32)
    product = frequencies[:, None] * positions[None, :] % length
    angles = product.astype(jnp.float32) * (2.0 * math.pi / length)
    return jnp.cos(angles) + 1j * jnp.sin(angles)

def convolve(padded, kernel):
    width_x = padded.shape[1] - 2
    width_y = padded.shape[2] - 2
    depth_z = padded.shape[3]
    channels = padded.shape[0]
    shifted = jnp.pad(padded, ((0, 0), (0, 0), (0, 0), (1, 1)))
    result = None
    for shift_x in range(3):
        for shift_y in range(3):
            stacked = jnp.concatenate([shifted[:, shift_x:shift_x + width_x, shift_y:shift_y + width_y, shift_z:shift_z + depth_z] for shift_z in range(3)], axis=0)
            first_tap = 9 * shift_x + 3 * shift_y
            tap_block = kernel[first_tap:first_tap + 3].reshape(3 * channels, kernel.shape[2])
            partial_sum = jnp.einsum('cxyz,co->oxyz', stacked, tap_block, precision=precise)
            result = partial_sum if result is None else result + partial_sum
    return result

def with_rim(values):
    return jnp.pad(values, ((0, 0), (1, 1), (1, 1), (0, 0)))

def reference(field, mix_weights, kept_z, conv_kernels):
    volume = field.reshape(C, NX, NY, NZ)
    scale_in = 1.0 / math.sqrt(NX * NY * NZ)
    scale_out = 1.0 / math.sqrt(KX * KY * MZ)
    freq_x = kept_frequencies(KX, NX)
    freq_y = kept_frequencies(KY, NY)
    z_modes = jnp.fft.rfft(volume, axis=3)[..., :MZ] * scale_in
    x_modes = jnp.take(jnp.fft.fft(z_modes, axis=1), freq_x, axis=1)
    y_modes = jnp.take(jnp.fft.fft(x_modes, axis=2), freq_y, axis=2)
    weights = (mix_weights[0] + 1j * mix_weights[1]).reshape(C, C, MZ, KX, KY)
    mixed = jnp.einsum('cokjl,cjlk->ojlk', weights, y_modes, precision=precise)
    keep_mask = jnp.arange(MZ, dtype=jnp.int32)[None, None, :] < kept_z.reshape(KX, KY)[:, :, None]
    mixed = jnp.where(keep_mask[None], mixed, jnp.zeros_like(mixed))
    in_y = jnp.einsum('ojlk,ly->ojyk', mixed, inverse_table(freq_y, NY), precision=precise)
    in_x = jnp.einsum('ojyk,jx->oxyk', in_y, inverse_table(freq_x, NX), precision=precise)
    padded_modes = jnp.pad(in_x, ((0, 0), (0, 0), (0, 0), (0, NZ // 2 + 1 - MZ)))
    spectral = jnp.fft.irfft(padded_modes, n=NZ, axis=3) * (NZ * scale_out)
    first = jax.nn.gelu(convolve(with_rim(volume), conv_kernels[0]), approximate=False)
    second = jax.nn.gelu(convolve(with_rim(first), conv_kernels[1]), approximate=False)
    third = convolve(with_rim(second), conv_kernels[2])
    return jax.nn.gelu(spectral + third, approximate=False).reshape(C, NX, NY * NZ)
```

```python
import math

import jax
import jax.numpy as jnp
import ml_dtypes
import numpy as np
from jax import lax
from jax.experimental import pallas as pl
from jax.experimental.pallas import tpu as pltpu
from jax.sharding import PartitionSpec as P

NZ = 64
KY = 32
CP = 40
LANES = 128
F32 = jnp.float32
BF16 = jnp.bfloat16


def split_table(table):
    high = table.astype(np.float32).astype(ml_dtypes.bfloat16)
    low = (table - high.astype(np.float64)).astype(np.float32).astype(ml_dtypes.bfloat16)
    return np.stack([high, low])


def split(values):
    high = values.astype(BF16)
    return high, (values - high.astype(F32)).astype(BF16)


def product(table, values, dims):
    high, low = split(values)
    numbers = (dims, ((), ()))

    def dot(left, right):
        return lax.dot_general(left, right, numbers, preferred_element_type=F32)

    return dot(table[0], high) + dot(table[0], low) + dot(table[1], high)


def frequencies(count, length):
    index = np.arange(count)
    return np.where(index < count // 2, index, length - count + index)


def tables(size_x, size_y, cells_x, cells_y, modes_x, modes_z):
    full_x, full_y = size_x * cells_x, size_y * cells_y
    scale_in = 1.0 / math.sqrt(full_x * full_y * NZ)
    scale_out = 1.0 / math.sqrt(modes_x * KY * modes_z)
    kx_local = modes_x // size_y
    z = np.arange(NZ)
    k = np.arange(modes_z)
    turn = 2.0 * np.pi * (np.outer(k, z) % NZ) / NZ
    eye_x = np.eye(cells_x)
    parts = np.stack([np.cos(turn), -np.sin(turn)], 1)
    z_in = np.einsum("kpz,xw->kpxwz", parts, eye_x).reshape(modes_z * 2 * cells_x, -1) * scale_in
    weight = np.where(k == 0, 1.0, 2.0)[:, None, None] * scale_out
    z_out = np.einsum("kpz,xw->kpxwz", parts * weight, eye_x).reshape(modes_z * 2 * cells_x, -1)

    def rotation(freq, positions, length):
        angle = 2.0 * np.pi * (np.outer(freq, positions) % length) / length
        cos, sin = np.cos(angle), np.sin(angle)
        return np.stack([np.stack([cos, -sin]), np.stack([sin, cos])])

    plus_x = rotation(frequencies(modes_x, full_x), np.arange(full_x), full_x)
    minus_x = plus_x.transpose(1, 0, 2, 3)
    x_in = minus_x.reshape(2, 2, modes_x, size_x, cells_x).transpose(2, 0, 3, 1, 4)
    x_in = x_in.reshape(modes_x * 2, -1)
    x_out = plus_x.reshape(2, 2, modes_x, size_x, cells_x).transpose(3, 0, 4, 2, 1)
    x_out = x_out.reshape(size_x * 2 * cells_x, -1)
    plus_y = rotation(frequencies(KY, full_y), np.arange(full_y), full_y)
    minus_y = plus_y.transpose(1, 0, 2, 3)
    eye_j = np.eye(kx_local)
    shape = (2, 2, KY, size_y, cells_y)
    y_in = np.einsum("pqlsy,jk->pjlyskq", minus_y.reshape(shape), eye_j)
    y_in = y_in.reshape(2 * kx_local * KY, -1)
    y_out = np.einsum("pqlsy,jk->ysjpqkl", plus_y.reshape(shape), eye_j)
    y_out = y_out.reshape(cells_y * size_y * kx_local * 2, -1)
    return [split_table(t) for t in (z_in, x_in, y_in, y_out, x_out, z_out)]


def params(vmem=16 << 20):
    return pltpu.CompilerParams(vmem_limit_bytes=vmem)


def call(body, out_shape, *args, scratch=(), flops=0, smem=()):
    space = [pl.BlockSpec(memory_space=pltpu.SMEM if i in smem else pltpu.VMEM) for i in range(len(args))]
    size = sum(a.size * a.dtype.itemsize for a in args)
    return pl.pallas_call(
        body,
        out_shape=out_shape,
        in_specs=space,
        out_specs=jax.tree.map(lambda _: pl.BlockSpec(memory_space=pltpu.VMEM), out_shape),
        scratch_shapes=list(scratch),
        compiler_params=params(),
        cost_estimate=pl.CostEstimate(flops=flops, bytes_accessed=size, transcendentals=0),
    )(*args)


def store_payload(ref, rows):
    count = ref.shape[0]
    for tile in range(3):
        width = min(LANES, rows.shape[1] - LANES * tile)
        block = rows[:, LANES * tile : LANES * tile + width]
        ref[:, 8 * tile : 8 * tile + 8, :width] = block.reshape(count, 8, width)
        if width < LANES:
            ref[:, 8 * tile : 8 * tile + 8, width:] = jnp.zeros((count, 8, LANES - width), F32)


def load_payload(ref):
    count = ref.shape[0]
    tiles = [ref[:, 8 * t : 8 * t + 8, :].reshape(count * 8, LANES) for t in range(3)]
    return jnp.concatenate(tiles, axis=1)


def z_in_body(grid_ref, table, out_ref):
    cells = grid_ref[...].reshape(-1, grid_ref.shape[2])
    store_payload(out_ref, product(table, cells, ((1,), (1,))))


def rows_body(received, table, out_ref):
    rows = product(table, load_payload(received), ((1,), (0,)))
    for tile in range(3):
        block = rows[:, LANES * tile : LANES * tile + LANES]
        out_ref[:, 8 * tile : 8 * tile + 8, :] = block.reshape(out_ref.shape[0], 8, LANES)


def mix_body(received, weights, kept, place, y_in, y_out, out_ref, stacked, s_re, s_im):
    cells_y = received.shape[0]
    rows = load_payload(received)
    block = rows.shape[0]
    for y in range(cells_y):
        stacked[y * block : (y + 1) * block, :CP] = rows[:, CP * y : CP * y + CP]
        stacked[y * block : (y + 1) * block, CP:] = jnp.zeros((block, LANES - CP), F32)
    modes = product(y_in, stacked[...], ((1,), (0,)))
    count = modes.shape[0] // 2
    s_re[...] = modes[:count].T
    s_im[...] = modes[count:].T
    channels = 36
    pair = 2 * channels
    row = lax.broadcasted_iota(jnp.int32, (8, count), 0)

    def spread(ref, c):
        first = jnp.broadcast_to(ref[c : c + 1, :], (8, count))
        second = jnp.broadcast_to(ref[c + 1 : c + 2, :], (8, count))
        middle = jnp.where(row < 4, first, second)
        return jnp.concatenate([first] * 4 + [middle] + [second] * 4, axis=0)

    total_re = jnp.zeros((pair, count), F32)
    total_im = jnp.zeros((pair, count), F32)
    for c in range(0, channels, 2):
        w_re = weights[0, channels * c : channels * c + pair, :]
        w_im = weights[1, channels * c : channels * c + pair, :]
        f_re, f_im = spread(s_re, c), spread(s_im, c)
        total_re += w_re * f_re - w_im * f_im
        total_im += w_re * f_im + w_im * f_re
    keep = place[0] < kept[...]

    def fold(total):
        total = total[:channels] + total[channels:]
        return jnp.concatenate([jnp.where(keep, total, 0.0), jnp.zeros((CP - channels, count), F32)], axis=0)

    mixed = jnp.concatenate([fold(total_re), fold(total_im)], axis=1)
    back = product(y_out, mixed, ((1,), (1,)))
    lanes = jnp.concatenate([back[y * block : (y + 1) * block] for y in range(cells_y)], axis=1)
    store_payload(out_ref, lanes)


def gelu_exact(values):
    return 0.5 * values * (1.0 + lax.erf(values * math.sqrt(0.5)))


ROW = 368


def taps_body(kernels, out_ref, scratch):
    channels = kernels.shape[2]
    for r in range(3):
        scratch[...] = jnp.zeros(scratch.shape, F32)
        for tap in range(27):
            row, lane = CP * (tap % 3), CP * (tap // 3)
            scratch[row : row + channels, lane : lane + channels] = kernels[r, tap]
        high, low = split(scratch[...].T[:ROW])
        out_ref[r, :ROW, :128] = high
        out_ref[r, :ROW, 128:] = high
        out_ref[r, ROW:, :128] = low
        out_ref[r, ROW:, 128:] = jnp.zeros((ROW, 128), BF16)


def convolve_rows(load_row, rows_in, width, taps, refs, finish):
    stack_a, stack_b, first_sum, second_sum, whole = refs
    z_position = lax.broadcasted_iota(jnp.int32, (CP, LANES), 1) % NZ
    has_lower = z_position >= 1
    has_upper = z_position <= NZ - 2
    low_half = lax.broadcasted_iota(jnp.int32, (CP, LANES), 1) < NZ
    tiles = width // LANES

    def prepare(index, stack):
        cells = load_row(index)
        for t in range(tiles):
            piece = cells[:, LANES * t : LANES * t + LANES]
            lower = jnp.where(has_lower, pltpu.roll(piece, 1, 1), 0.0)
            upper = jnp.where(has_upper, pltpu.roll(piece, LANES - 1, 1), 0.0)
            rows = jnp.concatenate([lower, piece, upper, jnp.zeros((8, LANES), F32)], axis=0)
            high, low = split(rows)
            stack[:128, LANES * t : LANES * t + LANES] = high
            stack[128:, LANES * t : LANES * t + LANES] = low

    def emit(row):
        sums = [[whole[CP * a : CP * a + CP, LANES * t : LANES * t + LANES] for t in range(tiles)] for a in range(3)]
        out = []
        for t in range(tiles):
            low_part = sums[0][t]
            if t + 1 < tiles:
                low_part = low_part + sums[2][t + 1]
            high_part = sums[2][t]
            if t > 0:
                high_part = high_part + sums[0][t - 1]
            turned = pltpu.roll(jnp.where(low_half, low_part, high_part), NZ, 1)
            out.append(sums[1][t] + turned)
        finish(row, out)

    def step(index, here, there):
        prepare(jnp.minimum(index + 1, rows_in - 1), there)
        emit(jnp.maximum(index - 3, 0))
        for t in range(tiles // 2):
            lanes = slice(2 * LANES * t, 2 * LANES * t + 2 * LANES)
            terms = lax.dot_general(
                taps[...], here[:, lanes], (((1,), (0,)), ((), ())), preferred_element_type=F32
            )
            for a in range(3):
                rows = slice(CP * a, CP * a + CP)
                piece = []
                for b in range(3):
                    first = CP * (3 * a + b)
                    piece.append(terms[first : first + CP] + terms[ROW + first : ROW + first + CP])
                whole[rows, lanes] = second_sum[rows, lanes] + piece[2]
                second_sum[rows, lanes] = first_sum[rows, lanes] + piece[1]
                first_sum[rows, lanes] = piece[0]

    def pair(j, carry):
        step(2 * j, stack_a, stack_b)
        step(2 * j + 1, stack_b, stack_a)
        return carry

    prepare(0, stack_a)
    lax.fori_loop(0, rows_in // 2, pair, 0)
    emit(rows_in - 3)


def conv_scratch(width):
    return [pltpu.VMEM((256, width), BF16)] * 2 + [pltpu.VMEM((3 * CP, width), F32)] * 3


def inside(place, first_x, first_y, sizes, width):
    cells_x, cells_y, full_x, full_y = sizes
    x = place[0] * cells_x + first_x + lax.broadcasted_iota(jnp.int32, (CP, width), 1) // NZ
    in_x = (x >= 0) & (x < full_x)

    def at(row):
        y = place[1] * cells_y + first_y + row
        return in_x & ((y >= 0) & (y < full_y))

    return at


def first_body(sizes, wide, before, after, place, taps, out_ref, rows, *refs):
    cells_y = wide.shape[0]
    rows[0:3] = before[...]
    rows[3 : 3 + cells_y] = wide[...]
    rows[3 + cells_y :] = after[...]
    keep = inside(place, -2, -2, sizes, 512)

    def finish(row, tiles):
        values = jnp.concatenate(tiles[1:5], axis=1)
        out_ref[row] = jnp.where(keep(row), gelu_exact(values), 0.0)

    convolve_rows(lambda i: rows[i], cells_y + 6, 768, taps, refs, finish)


def second_body(sizes, cells, place, taps, out_ref, *refs):
    keep = inside(place, -2, -1, sizes, 512)

    def finish(row, tiles):
        values = jnp.concatenate(tiles, axis=1)
        out_ref[row] = jnp.where(keep(row), gelu_exact(values), 0.0)

    convolve_rows(lambda i: cells[i], cells.shape[0], 512, taps, refs, finish)


def third_body(cells, taps, out_ref, *refs):
    def finish(row, tiles):
        out_ref[row] = jnp.concatenate(tiles[1:3], axis=1)

    convolve_rows(lambda i: cells[i], cells.shape[0], 512, taps, refs, finish)


def last_body(received, third, table, out_ref):
    spectrum = load_payload(received)[:, : third.shape[0] * CP]
    high, low = split(spectrum)

    def dot(left, right):
        return lax.dot_general(left, right, (((0,), (0,)), ((), ())), preferred_element_type=F32)

    spectral = dot(high, table[0]) + dot(low, table[0]) + dot(high, table[1])
    out_ref[...] = gelu_exact(spectral.reshape(third.shape) + third[...])


def shift(values, axis, step):
    count = lax.axis_size(axis)
    pairs = [(i, i + step) for i in range(count) if 0 <= i + step < count]
    return lax.ppermute(values, axis, pairs)


def shards(field, mix_weights, kept_z, conv_kernels):
    channels = field.shape[0]
    cells_x = field.shape[1]
    cells_y = field.shape[2] // NZ
    size_x = lax.axis_size("gx")
    size_y = lax.axis_size("gy")
    full_x, full_y = cells_x * size_x, cells_y * size_y
    modes_z = mix_weights.shape[3] * size_x
    kx_local = mix_weights.shape[4] // KY
    modes_x = kx_local * size_y
    place = jnp.stack([lax.axis_index("gx"), lax.axis_index("gy")]).astype(jnp.int32)
    z_in, x_in, y_in, y_out, x_out, z_out = [
        jnp.asarray(t) for t in tables(size_x, size_y, cells_x, cells_y, modes_x, modes_z)
    ]

    grid = field.reshape(channels, cells_x, cells_y, NZ).transpose(2, 0, 1, 3)
    grid = jnp.pad(grid.reshape(cells_y, channels, cells_x * NZ), ((0, 0), (0, CP - channels), (0, 0)))

    from_left = shift(grid, "gx", 1)
    from_right = shift(grid, "gx", -1)
    sent = call(z_in_body, jax.ShapeDtypeStruct((size_x, 24, LANES), F32), grid, z_in)
    taps = call(
        taps_body, jax.ShapeDtypeStruct((3, 2 * ROW, 256), BF16), conv_kernels,
        scratch=[pltpu.VMEM((128, 384), F32)],
    )
    received = lax.all_to_all(sent, "gx", 0, 0, tiled=True)
    wide = jnp.concatenate([from_left, grid, from_right], axis=2)
    before = shift(wide[cells_y - 3 :], "gy", 1)
    after = shift(wide[:3], "gy", -1)
    sent = call(rows_body, jax.ShapeDtypeStruct((size_y, 24, LANES), F32), received, x_in)

    sizes = (cells_x, cells_y, full_x, full_y)
    wide, sent = lax.optimization_barrier((wide, sent))
    received = lax.all_to_all(sent, "gy", 0, 0, tiled=True)
    first = call(
        lambda *refs: first_body(sizes, *refs),
        jax.ShapeDtypeStruct((cells_y + 4, CP, 512), F32),
        wide, before, after, place, taps[0],
        scratch=[pltpu.VMEM((cells_y + 6, CP, 768), F32)] + conv_scratch(768),
        smem=(3,), flops=6 << 30,
    )
    first, received = lax.optimization_barrier((first, received))
    weights = mix_weights.reshape(2, channels * channels, kx_local * KY)
    sent = call(
        mix_body,
        jax.ShapeDtypeStruct((size_y, 24, LANES), F32),
        received, weights, kept_z.reshape(1, -1), place, y_in, y_out,
        scratch=[pltpu.VMEM((cells_y * size_y * kx_local * 2, LANES), F32)]
        + [pltpu.VMEM((LANES, kx_local * KY), F32)] * 2,
        smem=(3,),
    )
    first, sent = lax.optimization_barrier((first, sent))
    received = lax.all_to_all(sent, "gy", 0, 0, tiled=True)
    second = call(
        lambda *refs: second_body(sizes, *refs),
        jax.ShapeDtypeStruct((cells_y + 2, CP, 512), F32),
        first, place, taps[1], scratch=conv_scratch(512), smem=(1,), flops=4 << 30,
    )
    second, received = lax.optimization_barrier((second, received))
    sent = call(rows_body, jax.ShapeDtypeStruct((size_x, 24, LANES), F32), received, x_out)
    second, sent = lax.optimization_barrier((second, sent))
    received = lax.all_to_all(sent, "gx", 0, 0, tiled=True)
    third = call(
        third_body,
        jax.ShapeDtypeStruct((cells_y, CP, cells_x * NZ), F32),
        second, taps[2], scratch=conv_scratch(512), flops=3 << 30,
    )
    out = call(last_body, jax.ShapeDtypeStruct(third.shape, F32), received, third, z_out)
    out = out[:, :channels].reshape(cells_y, channels, cells_x, NZ).transpose(1, 2, 0, 3)
    return out.reshape(channels, cells_x, cells_y * NZ)


def solution(mesh):
    placed = (P(None, "gx", "gy"), P(None, None, None, "gx", "gy"), P("gy"), P())
    return jax.shard_map(
        shards, mesh=mesh, in_specs=placed, out_specs=P(None, "gx", "gy"), check_vma=False
    )
```

```python
import math

import jax
import jax.numpy as jnp
import ml_dtypes
import numpy as np
from jax import lax
from jax.experimental import pallas as pl
from jax.experimental.pallas import tpu as pltpu
from jax.sharding import PartitionSpec as P

NZ = 64
KY = 32
CP = 40
LANES = 128
F32 = jnp.float32
BF16 = jnp.bfloat16


def split_table(table):
    high = table.astype(np.float32).astype(ml_dtypes.bfloat16)
    low = (table - high.astype(np.float64)).astype(np.float32).astype(ml_dtypes.bfloat16)
    return np.stack([high, low])


def split(values):
    high = values.astype(BF16)
    return high, (values - high.astype(F32)).astype(BF16)


def product(table, values, dims):
    high, low = split(values)
    numbers = (dims, ((), ()))

    def dot(left, right):
        return lax.dot_general(left, right, numbers, preferred_element_type=F32)

    return dot(table[0], high) + dot(table[0], low) + dot(table[1], high)


def frequencies(count, length):
    index = np.arange(count)
    return np.where(index < count // 2, index, length - count + index)


def tables(size_x, size_y, cells_x, cells_y, modes_x, modes_z):
    full_x, full_y = size_x * cells_x, size_y * cells_y
    scale_in = 1.0 / math.sqrt(full_x * full_y * NZ)
    scale_out = 1.0 / math.sqrt(modes_x * KY * modes_z)
    kx_local = modes_x // size_y
    z = np.arange(NZ)
    k = np.arange(modes_z)
    turn = 2.0 * np.pi * (np.outer(k, z) % NZ) / NZ
    eye_x = np.eye(cells_x)
    parts = np.stack([np.cos(turn), -np.sin(turn)], 1)
    z_in = np.einsum("kpz,xw->kpxwz", parts, eye_x).reshape(modes_z * 2 * cells_x, -1) * scale_in
    weight = np.where(k == 0, 1.0, 2.0)[:, None, None] * scale_out
    z_out = np.einsum("kpz,xw->kpxwz", parts * weight, eye_x).reshape(modes_z * 2 * cells_x, -1)

    def rotation(freq, positions, length):
        angle = 2.0 * np.pi * (np.outer(freq, positions) % length) / length
        cos, sin = np.cos(angle), np.sin(angle)
        return np.stack([np.stack([cos, -sin]), np.stack([sin, cos])])

    plus_x = rotation(frequencies(modes_x, full_x), np.arange(full_x), full_x)
    minus_x = plus_x.transpose(1, 0, 2, 3)
    x_in = minus_x.reshape(2, 2, modes_x, size_x, cells_x).transpose(2, 0, 3, 1, 4)
    x_in = x_in.reshape(modes_x * 2, -1)
    x_out = plus_x.reshape(2, 2, modes_x, size_x, cells_x).transpose(3, 0, 4, 2, 1)
    x_out = x_out.reshape(size_x * 2 * cells_x, -1)
    plus_y = rotation(frequencies(KY, full_y), np.arange(full_y), full_y)
    minus_y = plus_y.transpose(1, 0, 2, 3)
    eye_j = np.eye(kx_local)
    shape = (2, 2, KY, size_y, cells_y)
    y_in = np.einsum("pqlsy,jk->pjlyskq", minus_y.reshape(shape), eye_j)
    y_in = y_in.reshape(2 * kx_local * KY, -1)
    y_out = np.einsum("pqlsy,jk->ysjpqkl", plus_y.reshape(shape), eye_j)
    y_out = y_out.reshape(cells_y * size_y * kx_local * 2, -1)
    return [split_table(t) for t in (z_in, x_in, y_in, y_out, x_out, z_out)]


def call(body, out_shape, *args, scratch=(), flops=0, smem=(), hbm=(), out_hbm=(), vmem=24):
    def spec(index, kept):
        return pl.BlockSpec(memory_space=pl.ANY if index in kept else pltpu.VMEM)

    in_specs = [pl.BlockSpec(memory_space=pltpu.SMEM) if i in smem else spec(i, hbm) for i in range(len(args))]
    size = sum(a.size * a.dtype.itemsize for a in args)
    many = isinstance(out_shape, tuple)
    return pl.pallas_call(
        body,
        out_shape=out_shape,
        in_specs=in_specs,
        out_specs=tuple(spec(i, out_hbm) for i in range(len(out_shape))) if many else spec(0, out_hbm),
        scratch_shapes=list(scratch),
        compiler_params=pltpu.CompilerParams(vmem_limit_bytes=vmem << 20),
        cost_estimate=pl.CostEstimate(flops=flops, bytes_accessed=size, transcendentals=0),
    )(*args)


def copies(pairs, semaphores, first=0):
    started = [pltpu.make_async_copy(a, b, semaphores.at[first + i]) for i, (a, b) in enumerate(pairs)]
    for copy in started:
        copy.start()
    return started


def wait(started):
    for copy in started:
        copy.wait()


def store_payload(ref, rows):
    count = ref.shape[0]
    for tile in range(3):
        width = min(LANES, rows.shape[1] - LANES * tile)
        block = rows[:, LANES * tile : LANES * tile + width]
        ref[:, 8 * tile : 8 * tile + 8, :width] = block.reshape(count, 8, width)
        if width < LANES:
            ref[:, 8 * tile : 8 * tile + 8, width:] = jnp.zeros((count, 8, LANES - width), F32)


def load_payload(ref):
    count = ref.shape[0]
    tiles = [ref[:, 8 * t : 8 * t + 8, :].reshape(count * 8, LANES) for t in range(3)]
    return jnp.concatenate(tiles, axis=1)


def z_in_body(field, table, grid_ref, out_ref):
    channels, cells_x, width = field.shape
    for x in range(cells_x):
        piece = field[:, x, :]
        piece = jnp.concatenate([piece, jnp.zeros((CP - channels, width), F32)], axis=0)
        for y in range(width // NZ):
            grid_ref[y, :, NZ * x : NZ * x + NZ] = piece[:, NZ * y : NZ * y + NZ]
    cells = grid_ref[...].reshape(-1, grid_ref.shape[2])
    store_payload(out_ref, product(table, cells, ((1,), (1,))))


def rows_body(received, table, out_ref):
    rows = product(table, load_payload(received), ((1,), (0,)))
    for tile in range(3):
        block = rows[:, LANES * tile : LANES * tile + LANES]
        out_ref[:, 8 * tile : 8 * tile + 8, :] = block.reshape(out_ref.shape[0], 8, LANES)


def mix_body(received_hbm, weights_hbm, kept, place, y_in, y_out, out_ref, stacked, s_re, s_im, received, weights, sems):
    arrived = copies([(received_hbm, received)], sems, 2)
    started = copies([(weights_hbm.at[0], weights.at[0]), (weights_hbm.at[1], weights.at[1])], sems)
    wait(arrived)
    cells_y = received.shape[0]
    rows = load_payload(received)
    block = rows.shape[0]
    for y in range(cells_y):
        stacked[y * block : (y + 1) * block, :CP] = rows[:, CP * y : CP * y + CP]
        stacked[y * block : (y + 1) * block, CP:] = jnp.zeros((block, LANES - CP), F32)
    modes = product(y_in, stacked[...], ((1,), (0,)))
    count = modes.shape[0] // 2
    s_re[...] = modes[:count].T
    s_im[...] = modes[count:].T
    channels = 36
    pair = 2 * channels
    row = lax.broadcasted_iota(jnp.int32, (8, count), 0)

    def spread(ref, c):
        first = jnp.broadcast_to(ref[c : c + 1, :], (8, count))
        second = jnp.broadcast_to(ref[c + 1 : c + 2, :], (8, count))
        middle = jnp.where(row < 4, first, second)
        return jnp.concatenate([first] * 4 + [middle] + [second] * 4, axis=0)

    wait(started)
    total_re = jnp.zeros((pair, count), F32)
    total_im = jnp.zeros((pair, count), F32)
    for c in range(0, channels, 2):
        w_re = weights[0, channels * c : channels * c + pair, :]
        w_im = weights[1, channels * c : channels * c + pair, :]
        f_re, f_im = spread(s_re, c), spread(s_im, c)
        total_re += w_re * f_re - w_im * f_im
        total_im += w_re * f_im + w_im * f_re
    keep = place[0] < kept[...]

    def fold(total):
        total = total[:channels] + total[channels:]
        return jnp.concatenate([jnp.where(keep, total, 0.0), jnp.zeros((CP - channels, count), F32)], axis=0)

    mixed = jnp.concatenate([fold(total_re), fold(total_im)], axis=1)
    back = product(y_out, mixed, ((1,), (1,)))
    lanes = jnp.concatenate([back[y * block : (y + 1) * block] for y in range(cells_y)], axis=1)
    store_payload(out_ref, lanes)


def gelu_exact(values):
    return 0.5 * values * (1.0 + lax.erf(values * math.sqrt(0.5)))


ROW = 368


def taps_body(kernels, *refs):
    channels = kernels.shape[2]
    scratch = refs[3]
    for r in range(3):
        out_ref = refs[r]
        scratch[...] = jnp.zeros(scratch.shape, F32)
        for tap in range(27):
            row, lane = CP * (tap % 3), CP * (tap // 3)
            scratch[row : row + channels, lane : lane + channels] = kernels[r, tap]
        high, low = split(scratch[...].T[:ROW])
        out_ref[:ROW, :128] = high
        out_ref[:ROW, 128:] = high
        out_ref[ROW:, :128] = low
        out_ref[ROW:, 128:] = jnp.zeros((ROW, 128), BF16)


def convolve_rows(load_row, rows_in, width, taps, refs, finish, rest=()):
    stack_a, stack_b, first_sum, second_sum, whole = refs
    z_position = lax.broadcasted_iota(jnp.int32, (CP, LANES), 1) % NZ
    has_lower = z_position >= 1
    has_upper = z_position <= NZ - 2
    low_half = lax.broadcasted_iota(jnp.int32, (CP, LANES), 1) < NZ
    tiles = width // LANES

    def prepare(index, stack):
        cells = load_row(index)
        for t in range(tiles):
            piece = cells[:, LANES * t : LANES * t + LANES]
            lower = jnp.where(has_lower, pltpu.roll(piece, 1, 1), 0.0)
            upper = jnp.where(has_upper, pltpu.roll(piece, LANES - 1, 1), 0.0)
            rows = jnp.concatenate([lower, piece, upper, jnp.zeros((8, LANES), F32)], axis=0)
            high, low = split(rows)
            stack[:128, LANES * t : LANES * t + LANES] = high
            stack[128:, LANES * t : LANES * t + LANES] = low

    def emit(row):
        sums = [[whole[CP * a : CP * a + CP, LANES * t : LANES * t + LANES] for t in range(tiles)] for a in range(3)]
        out = []
        for t in range(tiles):
            low_part = sums[0][t]
            if t + 1 < tiles:
                low_part = low_part + sums[2][t + 1]
            high_part = sums[2][t]
            if t > 0:
                high_part = high_part + sums[0][t - 1]
            turned = pltpu.roll(jnp.where(low_half, low_part, high_part), NZ, 1)
            out.append(sums[1][t] + turned)
        finish(row, out)

    def step(index, here, there):
        prepare(jnp.minimum(index + 1, rows_in - 1), there)
        emit(jnp.maximum(index - 3, 0))
        for t in range(tiles // 2):
            lanes = slice(2 * LANES * t, 2 * LANES * t + 2 * LANES)
            terms = lax.dot_general(
                taps[...], here[:, lanes], (((1,), (0,)), ((), ())), preferred_element_type=F32
            )
            for a in range(3):
                rows = slice(CP * a, CP * a + CP)
                piece = []
                for b in range(3):
                    first = CP * (3 * a + b)
                    piece.append(terms[first : first + CP] + terms[ROW + first : ROW + first + CP])
                whole[rows, lanes] = second_sum[rows, lanes] + piece[2]
                second_sum[rows, lanes] = first_sum[rows, lanes] + piece[1]
                first_sum[rows, lanes] = piece[0]

    def pair(j, carry):
        step(2 * j, stack_a, stack_b)
        step(2 * j + 1, stack_b, stack_a)
        return carry

    prepare(0, stack_a)
    pair(0, 0)
    wait(rest)
    lax.fori_loop(1, rows_in // 2, pair, 0)
    emit(rows_in - 3)


def conv_scratch(width):
    return [pltpu.VMEM((256, width), BF16)] * 2 + [pltpu.VMEM((3 * CP, width), F32)] * 3


def inside(place, first_x, sizes, width):
    cells_x, cells_y, full_x, full_y = sizes
    x = place[0] * cells_x + first_x + lax.broadcasted_iota(jnp.int32, (CP, width), 1) // NZ
    in_x = (x >= 0) & (x < full_x)

    def at(local_y):
        y = place[1] * cells_y + local_y
        return in_x & ((y >= 0) & (y < full_y))

    return at


def gather(sources, rows, target, first):
    width = sources[0].shape[2]
    count = rows.stop - rows.start
    return [
        (s.at[rows], target.at[slice(first, first + count), :, slice(width * i, width * i + width)])
        for i, s in enumerate(sources)
    ]


def inner_body(sizes, left, own, right, place, taps, out_ref, rows, staged, sems, *refs):
    taps_ref, refs = refs[0], refs[1:]
    count = own.shape[0]
    sides = (left, own, right)
    head = copies([(taps, taps_ref)] + gather(sides, slice(0, 3), rows, 0), sems)
    rest = copies(gather(sides, slice(3, count), rows, 3), sems, 4)
    wait(head)
    keep = inside(place, -2, sizes, 512)

    def finish(row, tiles):
        values = jnp.concatenate(tiles[1:5], axis=1)
        staged[row] = jnp.where(keep(row + 1), gelu_exact(values), 0.0)

    convolve_rows(lambda i: rows[i], count, 768, taps_ref, refs, finish, rest)
    wait(copies([(staged, out_ref)], sems))


def outer_body(sizes, before, left, own, right, after, place, taps, out_ref, rows, staged, sems, *refs):
    taps_ref, refs = refs[0], refs[1:]
    count = own.shape[0]
    sides = (left, own, right)
    head = copies([(taps, taps_ref), (before, rows.at[0:3])], sems)
    pairs = gather(sides, slice(0, 2), rows, 3) + gather(sides, slice(count - 2, count), rows, 5)
    rest = copies(pairs + [(after, rows.at[7:10])], sems, 2)
    wait(head)
    keep = inside(place, -2, sizes, 512)

    def finish(row, tiles):
        values = jnp.concatenate(tiles[1:5], axis=1)
        local_y = jnp.where(row < 4, row - 2, row + count - 6)
        staged[row] = jnp.where(keep(local_y), gelu_exact(values), 0.0)

    convolve_rows(lambda i: rows[i], 10, 768, taps_ref, refs, finish, rest)
    wait(copies([(staged, out_ref)], sems))


def later_body(sizes, inner, outer, place, taps_1, taps_2, out_ref, rows, second, staged, sems, *refs):
    taps_ref_1, taps_ref_2, refs = refs[0], refs[1], refs[2:]
    count = inner.shape[0]
    head = copies([(taps_1, taps_ref_1), (outer.at[0:3], rows.at[0:3])], sems)
    pairs = [(inner, rows.at[3 : 3 + count]), (outer.at[5:8], rows.at[3 + count : 6 + count]), (taps_2, taps_ref_2)]
    rest = copies(pairs, sems, 2)
    wait(head)
    keep = inside(place, -2, sizes, 512)

    def finish_second(row, tiles):
        values = jnp.concatenate(tiles, axis=1)
        second[row] = jnp.where(keep(row - 1), gelu_exact(values), 0.0)

    def finish_third(row, tiles):
        staged[row] = jnp.concatenate(tiles[1:3], axis=1)

    convolve_rows(lambda i: rows[i], count + 6, 512, taps_ref_1, refs, finish_second, rest)
    convolve_rows(lambda i: second[i], count + 4, 512, taps_ref_2, refs, finish_third)
    wait(copies([(staged, out_ref)], sems))


def last_body(received_hbm, third_hbm, table, out_ref, received, third, sems):
    arrived = copies([(received_hbm, received), (third_hbm, third)], sems)
    wait(arrived)
    spectrum = load_payload(received)[:, : third.shape[0] * CP]
    high, low = split(spectrum)

    def dot(left, right):
        return lax.dot_general(left, right, (((0,), (0,)), ((), ())), preferred_element_type=F32)

    spectral = dot(high, table[0]) + dot(low, table[0]) + dot(high, table[1])
    out = gelu_exact(spectral.reshape(third.shape) + third[...])
    channels, cells_x, width = out_ref.shape
    for x in range(cells_x):
        piece = [out[y, :channels, NZ * x : NZ * x + NZ] for y in range(width // NZ)]
        out_ref[:, x, :] = jnp.concatenate(piece, axis=1)


def shift(values, axis, step):
    count = lax.axis_size(axis)
    pairs = [(i, i + step) for i in range(count) if 0 <= i + step < count]
    return lax.ppermute(values, axis, pairs)


def shards(field, mix_weights, kept_z, conv_kernels):
    channels = field.shape[0]
    cells_x = field.shape[1]
    cells_y = field.shape[2] // NZ
    size_x = lax.axis_size("gx")
    size_y = lax.axis_size("gy")
    full_x, full_y = cells_x * size_x, cells_y * size_y
    modes_z = mix_weights.shape[3] * size_x
    kx_local = mix_weights.shape[4] // KY
    modes_x = kx_local * size_y
    place = jnp.stack([lax.axis_index("gx"), lax.axis_index("gy")]).astype(jnp.int32)
    z_in, x_in, y_in, y_out, x_out, z_out = [
        jnp.asarray(t) for t in tables(size_x, size_y, cells_x, cells_y, modes_x, modes_z)
    ]

    sizes = (cells_x, cells_y, full_x, full_y)
    row_scratch = [pltpu.SemaphoreType.DMA((9,)), pltpu.VMEM((2 * ROW, 256), BF16)]
    taps_shape = jax.ShapeDtypeStruct((2 * ROW, 256), BF16)

    grid, sent = call(
        z_in_body,
        (
            jax.ShapeDtypeStruct((cells_y, CP, cells_x * NZ), F32),
            jax.ShapeDtypeStruct((size_x, 24, LANES), F32),
        ),
        field, z_in,
    )
    left = shift(grid, "gx", 1)
    right = shift(grid, "gx", -1)
    taps = call(taps_body, (taps_shape,) * 3, conv_kernels, scratch=[pltpu.VMEM((128, 384), F32)])
    received = lax.all_to_all(sent, "gx", 0, 0, tiled=True)

    def edge(rows):
        return jnp.concatenate([left[rows], grid[rows], right[rows]], axis=2)

    before = shift(edge(slice(cells_y - 3, cells_y)), "gy", 1)
    after = shift(edge(slice(0, 3)), "gy", -1)
    sent = call(rows_body, jax.ShapeDtypeStruct((size_y, 24, LANES), F32), received, x_in)

    left, sent = lax.optimization_barrier((left, sent))
    received = lax.all_to_all(sent, "gy", 0, 0, tiled=True)
    inner = call(
        lambda *refs: inner_body(sizes, *refs),
        jax.ShapeDtypeStruct((cells_y - 2, CP, 512), F32),
        left, grid, right, place, taps[0],
        scratch=[pltpu.VMEM((cells_y, CP, 768), F32), pltpu.VMEM((cells_y - 2, CP, 512), F32)]
        + row_scratch + conv_scratch(768),
        smem=(3,), hbm=(0, 1, 2, 4), out_hbm=(0,), vmem=60, flops=3 << 30,
    )
    inner, received = lax.optimization_barrier((inner, received))
    weights = mix_weights.reshape(2, channels * channels, kx_local * KY)
    sent = call(
        mix_body,
        jax.ShapeDtypeStruct((size_y, 24, LANES), F32),
        received, weights, kept_z.reshape(1, -1), place, y_in, y_out,
        scratch=[pltpu.VMEM((cells_y * size_y * kx_local * 2, LANES), F32)]
        + [pltpu.VMEM((LANES, kx_local * KY), F32)] * 2
        + [pltpu.VMEM(received.shape, F32), pltpu.VMEM(weights.shape, F32), pltpu.SemaphoreType.DMA((3,))],
        smem=(3,), hbm=(0, 1), vmem=60,
    )
    before, sent = lax.optimization_barrier((before, sent))
    received = lax.all_to_all(sent, "gy", 0, 0, tiled=True)
    outer = call(
        lambda *refs: outer_body(sizes, *refs),
        jax.ShapeDtypeStruct((8, CP, 512), F32),
        before, left, grid, right, after, place, taps[0],
        scratch=[pltpu.VMEM((10, CP, 768), F32), pltpu.VMEM((8, CP, 512), F32)] + row_scratch + conv_scratch(768),
        smem=(5,), hbm=(0, 1, 2, 3, 4, 6), out_hbm=(0,), vmem=60, flops=4 << 30,
    )
    outer, received = lax.optimization_barrier((outer, received))
    sent = call(rows_body, jax.ShapeDtypeStruct((size_x, 24, LANES), F32), received, x_out)
    outer, sent = lax.optimization_barrier((outer, sent))
    received = lax.all_to_all(sent, "gx", 0, 0, tiled=True)
    third = call(
        lambda *refs: later_body(sizes, *refs),
        jax.ShapeDtypeStruct((cells_y, CP, cells_x * NZ), F32),
        inner, outer, place, taps[1], taps[2],
        scratch=[
            pltpu.VMEM((cells_y + 4, CP, 512), F32),
            pltpu.VMEM((cells_y + 2, CP, 512), F32),
            pltpu.VMEM((cells_y, CP, cells_x * NZ), F32),
        ]
        + row_scratch + [pltpu.VMEM((2 * ROW, 256), BF16)] + conv_scratch(512),
        smem=(2,), hbm=(0, 1, 3, 4), out_hbm=(0,), vmem=60, flops=8 << 30,
    )
    return call(
        last_body, jax.ShapeDtypeStruct(field.shape, F32), received, third, z_out,
        scratch=[pltpu.VMEM(received.shape, F32), pltpu.VMEM(third.shape, F32), pltpu.SemaphoreType.DMA((2,))],
        hbm=(0, 1), vmem=60,
    )


def solution(mesh):
    placed = (P(None, "gx", "gy"), P(None, None, None, "gx", "gy"), P("gy"), P())
    return jax.shard_map(
        shards, mesh=mesh, in_specs=placed, out_specs=P(None, "gx", "gy"), check_vma=False
    )
```

```python
import functools
import math

import jax
import jax.numpy as jnp
import ml_dtypes
import numpy as np
from jax import lax
from jax.experimental import pallas as pl
from jax.experimental.pallas import tpu as pltpu
from jax.sharding import PartitionSpec as P

NZ = 64
KY = 32
INNER = 1024
FULL = 60
CP = 40
LANES = 128
F32 = jnp.float32
BF16 = jnp.bfloat16


def split_table(table):
    high = table.astype(np.float32).astype(ml_dtypes.bfloat16)
    low = (table - high.astype(np.float64)).astype(np.float32).astype(ml_dtypes.bfloat16)
    return np.stack([high, low])


def split(values):
    high = values.astype(BF16)
    return high, (values - high.astype(F32)).astype(BF16)


def product(table, values, dims):
    high, low = split(values)
    numbers = (dims, ((), ()))

    def dot(left, right):
        return lax.dot_general(left, right, numbers, preferred_element_type=F32)

    return dot(table[0], high) + dot(table[0], low) + dot(table[1], high)


def frequencies(count, length):
    index = np.arange(count)
    return np.where(index < count // 2, index, length - count + index)


def tables(size_x, size_y, cells_x, cells_y, modes_x, modes_z):
    full_x, full_y = size_x * cells_x, size_y * cells_y
    scale_in = 1.0 / math.sqrt(full_x * full_y * NZ)
    scale_out = 1.0 / math.sqrt(modes_x * KY * modes_z)
    kx_local = modes_x // size_y
    z = np.arange(NZ)
    k = np.arange(modes_z)
    turn = 2.0 * np.pi * (np.outer(k, z) % NZ) / NZ
    eye_x = np.eye(cells_x)
    parts = np.stack([np.cos(turn), -np.sin(turn)], 1)
    z_in = np.einsum("kpz,xw->kpxwz", parts, eye_x).reshape(modes_z * 2 * cells_x, -1) * scale_in
    weight = np.where(k == 0, 1.0, 2.0)[:, None, None] * scale_out
    z_out = np.einsum("kpz,xw->kpxwz", parts * weight, eye_x).reshape(modes_z * 2 * cells_x, -1)

    def rotation(freq, positions, length):
        angle = 2.0 * np.pi * (np.outer(freq, positions) % length) / length
        cos, sin = np.cos(angle), np.sin(angle)
        return np.stack([np.stack([cos, -sin]), np.stack([sin, cos])])

    plus_x = rotation(frequencies(modes_x, full_x), np.arange(full_x), full_x)
    minus_x = plus_x.transpose(1, 0, 2, 3)
    x_in = minus_x.reshape(2, 2, modes_x, size_x, cells_x).transpose(2, 0, 3, 1, 4)
    x_in = x_in.reshape(modes_x * 2, -1)
    x_out = plus_x.reshape(2, 2, modes_x, size_x, cells_x).transpose(3, 0, 4, 2, 1)
    x_out = x_out.reshape(size_x * 2 * cells_x, -1)
    plus_y = rotation(frequencies(KY, full_y), np.arange(full_y), full_y)
    minus_y = plus_y.transpose(1, 0, 2, 3)
    eye_j = np.eye(kx_local)
    shape = (2, 2, KY, size_y, cells_y)
    y_in = np.einsum("pqlsy,jk->pjlyskq", minus_y.reshape(shape), eye_j)
    y_in = y_in.reshape(2 * kx_local * KY, -1)
    y_out = np.einsum("pqlsy,jk->ysjpqkl", plus_y.reshape(shape), eye_j)
    y_out = y_out.reshape(cells_y * size_y * kx_local * 2, -1)
    return [split_table(t) for t in (z_in, x_in, y_in, y_out, x_out, z_out)]


def call(body, out_shape, *args, scratch=(), flops=0, smem=(), hbm=(), out_hbm=(), vmem=24, light=False):
    def spec(index, kept):
        return pl.BlockSpec(memory_space=pl.ANY if index in kept else pltpu.VMEM)

    in_specs = [pl.BlockSpec(memory_space=pltpu.SMEM) if i in smem else spec(i, hbm) for i in range(len(args))]
    size = 0 if light else sum(a.size * a.dtype.itemsize for a in args)
    many = isinstance(out_shape, tuple)
    return pl.pallas_call(
        body,
        out_shape=out_shape,
        in_specs=in_specs,
        out_specs=tuple(spec(i, out_hbm) for i in range(len(out_shape))) if many else spec(0, out_hbm),
        scratch_shapes=list(scratch),
        compiler_params=pltpu.CompilerParams(vmem_limit_bytes=vmem << 20),
        cost_estimate=pl.CostEstimate(flops=flops, bytes_accessed=size, transcendentals=0),
    )(*args)


def copies(pairs, semaphores, first=0):
    started = [pltpu.make_async_copy(a, b, semaphores.at[first + i]) for i, (a, b) in enumerate(pairs)]
    for copy in started:
        copy.start()
    return started


def wait(started):
    for copy in started:
        copy.wait()


def store_payload(ref, rows):
    count = ref.shape[0]
    for tile in range(3):
        width = min(LANES, rows.shape[1] - LANES * tile)
        block = rows[:, LANES * tile : LANES * tile + width]
        ref[:, 8 * tile : 8 * tile + 8, :width] = block.reshape(count, 8, width)
        if width < LANES:
            ref[:, 8 * tile : 8 * tile + 8, width:] = jnp.zeros((count, 8, LANES - width), F32)


def load_payload(ref):
    count = ref.shape[0]
    tiles = [ref[:, 8 * t : 8 * t + 8, :].reshape(count * 8, LANES) for t in range(3)]
    return jnp.concatenate(tiles, axis=1)


def z_in_body(field_hbm, table_hbm, grid_ref, out_ref, field, table, sems):
    arrived = copies([(field_hbm, field), (table_hbm, table)], sems)
    wait(arrived[:1])
    channels, cells_x, width = field.shape
    for x in range(cells_x):
        piece = field[:, x, :]
        piece = jnp.concatenate([piece, jnp.zeros((CP - channels, width), F32)], axis=0)
        for y in range(width // NZ):
            grid_ref[y, :, NZ * x : NZ * x + NZ] = piece[:, NZ * y : NZ * y + NZ]
    cells = grid_ref[...].reshape(-1, grid_ref.shape[2])
    wait(arrived[1:])
    store_payload(out_ref, product(table, cells, ((1,), (1,))))


def rows_body(received, table, out_ref):
    rows = product(table, load_payload(received), ((1,), (0,)))
    for tile in range(3):
        block = rows[:, LANES * tile : LANES * tile + LANES]
        out_ref[:, 8 * tile : 8 * tile + 8, :] = block.reshape(out_ref.shape[0], 8, LANES)


def mix_body(received, weights, kept, place, y_in, y_out, out_ref, stacked, s_re, s_im):
    cells_y = received.shape[0]
    rows = load_payload(received)
    block = rows.shape[0]
    for y in range(cells_y):
        stacked[y * block : (y + 1) * block, :CP] = rows[:, CP * y : CP * y + CP]
        stacked[y * block : (y + 1) * block, CP:] = jnp.zeros((block, LANES - CP), F32)
    modes = product(y_in, stacked[...], ((1,), (0,)))
    count = modes.shape[0] // 2
    s_re[...] = modes[:count].T
    s_im[...] = modes[count:].T
    channels = 36
    pair = 2 * channels
    row = lax.broadcasted_iota(jnp.int32, (8, count), 0)

    def spread(ref, c):
        first = jnp.broadcast_to(ref[c : c + 1, :], (8, count))
        second = jnp.broadcast_to(ref[c + 1 : c + 2, :], (8, count))
        middle = jnp.where(row < 4, first, second)
        return jnp.concatenate([first] * 4 + [middle] + [second] * 4, axis=0)

    total_re = jnp.zeros((pair, count), F32)
    total_im = jnp.zeros((pair, count), F32)
    for c in range(0, channels, 2):
        w_re = weights[0, channels * c : channels * c + pair, :]
        w_im = weights[1, channels * c : channels * c + pair, :]
        f_re, f_im = spread(s_re, c), spread(s_im, c)
        total_re += w_re * f_re - w_im * f_im
        total_im += w_re * f_im + w_im * f_re
    keep = place[0] < kept[...]

    def fold(total):
        total = total[:channels] + total[channels:]
        return jnp.concatenate([jnp.where(keep, total, 0.0), jnp.zeros((CP - channels, count), F32)], axis=0)

    mixed = jnp.concatenate([fold(total_re), fold(total_im)], axis=1)
    back = product(y_out, mixed, ((1,), (1,)))
    lanes = jnp.concatenate([back[y * block : (y + 1) * block] for y in range(cells_y)], axis=1)
    store_payload(out_ref, lanes)


def gelu_exact(values):
    return 0.5 * values * (1.0 + lax.erf(values * math.sqrt(0.5)))


ROW = 368


def taps_body(first, kernels, *refs):
    channels = kernels.shape[2]
    *outs, scratch = refs
    for r, out_ref in enumerate(outs):
        scratch[...] = jnp.zeros(scratch.shape, F32)
        for tap in range(27):
            row, lane = CP * (tap % 3), CP * (tap // 3)
            scratch[row : row + channels, lane : lane + channels] = kernels[first + r, tap]
        high, low = split(scratch[...].T[:ROW])
        out_ref[:ROW, :128] = high
        out_ref[:ROW, 128:] = high
        out_ref[ROW:, :128] = low
        out_ref[ROW:, 128:] = jnp.zeros((ROW, 128), BF16)


def convolve_rows(load_row, rows_in, width, taps, refs, finish, rest=()):
    stack_a, stack_b, first_sum, second_sum, whole = refs
    z_position = lax.broadcasted_iota(jnp.int32, (CP, LANES), 1) % NZ
    has_lower = z_position >= 1
    has_upper = z_position <= NZ - 2
    low_half = lax.broadcasted_iota(jnp.int32, (CP, LANES), 1) < NZ
    tiles = width // LANES

    def prepare(index, stack):
        cells = load_row(index)
        for t in range(tiles):
            piece = cells[:, LANES * t : LANES * t + LANES]
            lower = jnp.where(has_lower, pltpu.roll(piece, 1, 1), 0.0)
            upper = jnp.where(has_upper, pltpu.roll(piece, LANES - 1, 1), 0.0)
            rows = jnp.concatenate([lower, piece, upper, jnp.zeros((8, LANES), F32)], axis=0)
            high, low = split(rows)
            stack[:128, LANES * t : LANES * t + LANES] = high
            stack[128:, LANES * t : LANES * t + LANES] = low

    def emit(row):
        sums = [[whole[CP * a : CP * a + CP, LANES * t : LANES * t + LANES] for t in range(tiles)] for a in range(3)]
        out = []
        for t in range(tiles):
            low_part = sums[0][t]
            if t + 1 < tiles:
                low_part = low_part + sums[2][t + 1]
            high_part = sums[2][t]
            if t > 0:
                high_part = high_part + sums[0][t - 1]
            turned = pltpu.roll(jnp.where(low_half, low_part, high_part), NZ, 1)
            out.append(sums[1][t] + turned)
        finish(row, out)

    def step(index, here, there):
        prepare(jnp.minimum(index + 1, rows_in - 1), there)
        emit(jnp.maximum(index - 3, 0))
        for t in range(tiles // 2):
            lanes = slice(2 * LANES * t, 2 * LANES * t + 2 * LANES)
            terms = lax.dot_general(
                taps[...], here[:, lanes], (((1,), (0,)), ((), ())), preferred_element_type=F32
            )
            for a in range(3):
                rows = slice(CP * a, CP * a + CP)
                piece = []
                for b in range(3):
                    first = CP * (3 * a + b)
                    piece.append(terms[first : first + CP] + terms[ROW + first : ROW + first + CP])
                whole[rows, lanes] = second_sum[rows, lanes] + piece[2]
                second_sum[rows, lanes] = first_sum[rows, lanes] + piece[1]
                first_sum[rows, lanes] = piece[0]

    def pair(j, carry):
        step(2 * j, stack_a, stack_b)
        step(2 * j + 1, stack_b, stack_a)
        return carry

    prepare(0, stack_a)
    pair(0, 0)
    wait(rest)
    lax.fori_loop(1, rows_in // 2, pair, 0)
    emit(rows_in - 3)


def conv_scratch(width):
    return [pltpu.VMEM((256, width), BF16)] * 2 + [pltpu.VMEM((3 * CP, width), F32)] * 3


def inside(place, first_x, sizes, width):
    cells_x, cells_y, full_x, full_y = sizes
    x = place[0] * cells_x + first_x + lax.broadcasted_iota(jnp.int32, (CP, width), 1) // NZ
    in_x = (x >= 0) & (x < full_x)

    def at(local_y):
        y = place[1] * cells_y + local_y
        return in_x & ((y >= 0) & (y < full_y))

    return at


def gather(sources, rows, target, first):
    width = sources[0].shape[2]
    count = rows.stop - rows.start
    return [
        (s.at[rows], target.at[slice(first, first + count), :, slice(width * i, width * i + width)])
        for i, s in enumerate(sources)
    ]


def join(sources, rows, target, first):
    width = sources[0].shape[2]
    count = rows.stop - rows.start
    for i, source in enumerate(sources):
        target[first : first + count, :, width * i : width * i + width] = source[rows]


def inner_body(sizes, left, own, right, place, taps, out_ref, rows, *refs):
    count = own.shape[0]
    join((left, own, right), slice(0, count), rows, 0)
    keep = inside(place, -2, sizes, 512)

    def finish(row, tiles):
        values = jnp.concatenate(tiles[1:5], axis=1)
        out_ref[row] = jnp.where(keep(row + 1), gelu_exact(values), 0.0)

    convolve_rows(lambda i: rows[i], count, 768, taps, refs, finish)


def outer_body(sizes, before, left, own, right, after, place, taps, out_ref, rows, *refs):
    count = own.shape[0]
    sides = (left, own, right)
    rows[0:3] = before[...]
    join(sides, slice(0, 2), rows, 3)
    join(sides, slice(count - 2, count), rows, 5)
    rows[7:10] = after[...]
    keep = inside(place, -2, sizes, 512)

    def finish(row, tiles):
        values = jnp.concatenate(tiles[1:5], axis=1)
        local_y = jnp.where(row < 4, row - 2, row + count - 6)
        out_ref[row] = jnp.where(keep(local_y), gelu_exact(values), 0.0)

    convolve_rows(lambda i: rows[i], 10, 768, taps, refs, finish)


def later_body(sizes, inner, outer, place, taps_1, taps_2, out_ref, rows, second, *refs):
    count = inner.shape[0]
    rows[0:3] = outer[0:3]
    rows[3 : 3 + count] = inner[...]
    rows[3 + count :] = outer[5:8]
    keep = inside(place, -2, sizes, 512)

    def finish_second(row, tiles):
        values = jnp.concatenate(tiles, axis=1)
        second[row] = jnp.where(keep(row - 1), gelu_exact(values), 0.0)

    def finish_third(row, tiles):
        out_ref[row] = jnp.concatenate(tiles[1:3], axis=1)

    convolve_rows(lambda i: rows[i], count + 6, 512, taps_1, refs, finish_second)
    convolve_rows(lambda i: second[i], count + 4, 512, taps_2, refs, finish_third)


def last_body(received, third, table, out_ref):
    spectrum = load_payload(received)[:, : third.shape[0] * CP]
    high, low = split(spectrum)

    def dot(left, right):
        return lax.dot_general(left, right, (((0,), (0,)), ((), ())), preferred_element_type=F32)

    spectral = dot(high, table[0]) + dot(low, table[0]) + dot(high, table[1])
    out = gelu_exact(spectral.reshape(third.shape) + third[...])
    channels, cells_x, width = out_ref.shape
    for x in range(cells_x):
        piece = [out[y, :channels, NZ * x : NZ * x + NZ] for y in range(width // NZ)]
        out_ref[:, x, :] = jnp.concatenate(piece, axis=1)


def shift(values, axis, step):
    count = lax.axis_size(axis)
    pairs = [(i, i + step) for i in range(count) if 0 <= i + step < count]
    return lax.ppermute(values, axis, pairs)


def shards(field, mix_weights, kept_z, conv_kernels):
    channels = field.shape[0]
    cells_x = field.shape[1]
    cells_y = field.shape[2] // NZ
    size_x = lax.axis_size("gx")
    size_y = lax.axis_size("gy")
    full_x, full_y = cells_x * size_x, cells_y * size_y
    modes_z = mix_weights.shape[3] * size_x
    kx_local = mix_weights.shape[4] // KY
    modes_x = kx_local * size_y
    place = jnp.stack([lax.axis_index("gx"), lax.axis_index("gy")]).astype(jnp.int32)
    z_in, x_in, y_in, y_out, x_out, z_out = [
        jnp.asarray(t) for t in tables(size_x, size_y, cells_x, cells_y, modes_x, modes_z)
    ]

    sizes = (cells_x, cells_y, full_x, full_y)
    row_scratch = [pltpu.SemaphoreType.DMA((9,)), pltpu.VMEM((2 * ROW, 256), BF16)]
    taps_shape = jax.ShapeDtypeStruct((2 * ROW, 256), BF16)

    grid, sent = call(
        z_in_body,
        (
            jax.ShapeDtypeStruct((cells_y, CP, cells_x * NZ), F32),
            jax.ShapeDtypeStruct((size_x, 24, LANES), F32),
        ),
        field, z_in,
        scratch=[pltpu.VMEM(field.shape, F32), pltpu.VMEM(z_in.shape, BF16), pltpu.SemaphoreType.DMA((2,))],
        hbm=(0, 1), vmem=FULL,
    )
    def make_taps(first, count, kernels):
        body = functools.partial(taps_body, first)
        return call(body, (taps_shape,) * count, kernels, scratch=[pltpu.VMEM((128, 384), F32)])

    conv_kernels, sent = lax.optimization_barrier((conv_kernels, sent))
    taps = make_taps(0, 1, conv_kernels)
    grid, conv_kernels, *taps = lax.optimization_barrier((grid, conv_kernels, *taps))
    left = shift(grid, "gx", 1)
    right = shift(grid, "gx", -1)
    taps = [*taps, *make_taps(1, 2, conv_kernels)]
    received = lax.all_to_all(sent, "gx", 0, 0, tiled=True)
    received, *taps = lax.optimization_barrier((received, *taps))

    sent = call(rows_body, jax.ShapeDtypeStruct((size_y, 24, LANES), F32), received, x_in)

    left, right, _ = lax.optimization_barrier((left, right, sent))
    received = lax.all_to_all(sent, "gy", 0, 0, tiled=True)

    def edge(rows):
        return jnp.concatenate([left[rows], grid[rows], right[rows]], axis=2)

    before = shift(edge(slice(cells_y - 3, cells_y)), "gy", 1)
    after = shift(edge(slice(0, 3)), "gy", -1)
    inner = call(
        lambda *refs: inner_body(sizes, *refs),
        jax.ShapeDtypeStruct((cells_y - 2, CP, 512), F32),
        left, grid, right, place, taps[0],
        scratch=[pltpu.VMEM((cells_y, CP, 768), F32)] + conv_scratch(768),
        smem=(3,), light=False, flops=INNER << 20,
    )
    inner, received = lax.optimization_barrier((inner, received))
    weights = mix_weights.reshape(2, channels * channels, kx_local * KY)
    sent = call(
        mix_body,
        jax.ShapeDtypeStruct((size_y, 24, LANES), F32),
        received, weights, kept_z.reshape(1, -1), place, y_in, y_out,
        scratch=[pltpu.VMEM((cells_y * size_y * kx_local * 2, LANES), F32)]
        + [pltpu.VMEM((LANES, kx_local * KY), F32)] * 2,
        smem=(3,), flops=30 << 30,
    )
    before, after, _ = lax.optimization_barrier((before, after, sent))
    received = lax.all_to_all(sent, "gy", 0, 0, tiled=True)
    outer = call(
        lambda *refs: outer_body(sizes, *refs),
        jax.ShapeDtypeStruct((8, CP, 512), F32),
        before, left, grid, right, after, place, taps[0],
        scratch=[pltpu.VMEM((10, CP, 768), F32)] + conv_scratch(768),
        smem=(5,), flops=4 << 30,
    )
    outer, received = lax.optimization_barrier((outer, received))
    sent = call(rows_body, jax.ShapeDtypeStruct((size_x, 24, LANES), F32), received, x_out)
    outer, sent = lax.optimization_barrier((outer, sent))
    received = lax.all_to_all(sent, "gx", 0, 0, tiled=True)
    third = call(
        lambda *refs: later_body(sizes, *refs),
        jax.ShapeDtypeStruct((cells_y, CP, cells_x * NZ), F32),
        inner, outer, place, taps[1], taps[2],
        scratch=[
            pltpu.VMEM((cells_y + 4, CP, 512), F32),
            pltpu.VMEM((cells_y + 2, CP, 512), F32),
        ]
        + conv_scratch(512),
        smem=(2,), flops=8 << 30,
    )
    return call(
        last_body, jax.ShapeDtypeStruct(field.shape, F32), received, third, z_out,
    )


def solution(mesh):
    placed = (P(None, "gx", "gy"), P(None, None, None, "gx", "gy"), P("gy"), P())
    return jax.shard_map(
        shards, mesh=mesh, in_specs=placed, out_specs=P(None, "gx", "gy"), check_vma=False
    )
```

```python
import math

import jax
import jax.numpy as jnp
import ml_dtypes
import numpy as np
from jax import lax
from jax.experimental import pallas as pl
from jax.experimental.pallas import tpu as pltpu
from jax.sharding import PartitionSpec as P

NZ = 64
KY = 32
INNER = 1024
OUTER = 1024
FULL = 60
CP = 40
LANES = 128
F32 = jnp.float32
BF16 = jnp.bfloat16


def split_table(table):
    high = table.astype(np.float32).astype(ml_dtypes.bfloat16)
    low = (table - high.astype(np.float64)).astype(np.float32).astype(ml_dtypes.bfloat16)
    return np.stack([high, low])


def split(values):
    high = values.astype(BF16)
    return high, (values - high.astype(F32)).astype(BF16)


def product(table, values, dims):
    high, low = split(values)
    numbers = (dims, ((), ()))

    def dot(left, right):
        return lax.dot_general(left, right, numbers, preferred_element_type=F32)

    return dot(table[0], high) + dot(table[0], low) + dot(table[1], high)


def frequencies(count, length):
    index = np.arange(count)
    return np.where(index < count // 2, index, length - count + index)


def tables(size_x, size_y, cells_x, cells_y, modes_x, modes_z):
    full_x, full_y = size_x * cells_x, size_y * cells_y
    scale_in = 1.0 / math.sqrt(full_x * full_y * NZ)
    scale_out = 1.0 / math.sqrt(modes_x * KY * modes_z)
    kx_local = modes_x // size_y
    z = np.arange(NZ)
    k = np.arange(modes_z)
    turn = 2.0 * np.pi * (np.outer(k, z) % NZ) / NZ
    eye_x = np.eye(cells_x)
    parts = np.stack([np.cos(turn), -np.sin(turn)], 1)
    z_in = np.einsum("kpz,xw->kpxwz", parts, eye_x).reshape(modes_z * 2 * cells_x, -1) * scale_in
    weight = np.where(k == 0, 1.0, 2.0)[:, None, None] * scale_out
    z_out = np.einsum("kpz,xw->kpxwz", parts * weight, eye_x).reshape(modes_z * 2 * cells_x, -1)

    def rotation(freq, positions, length):
        angle = 2.0 * np.pi * (np.outer(freq, positions) % length) / length
        cos, sin = np.cos(angle), np.sin(angle)
        return np.stack([np.stack([cos, -sin]), np.stack([sin, cos])])

    plus_x = rotation(frequencies(modes_x, full_x), np.arange(full_x), full_x)
    minus_x = plus_x.transpose(1, 0, 2, 3)
    x_in = minus_x.reshape(2, 2, modes_x, size_x, cells_x).transpose(2, 0, 3, 1, 4)
    x_in = x_in.reshape(modes_x * 2, -1)
    x_out = plus_x.reshape(2, 2, modes_x, size_x, cells_x).transpose(3, 0, 4, 2, 1)
    x_out = x_out.reshape(size_x * 2 * cells_x, -1)
    plus_y = rotation(frequencies(KY, full_y), np.arange(full_y), full_y)
    minus_y = plus_y.transpose(1, 0, 2, 3)
    eye_j = np.eye(kx_local)
    shape = (2, 2, KY, size_y, cells_y)
    y_in = np.einsum("pqlsy,jk->pjlyskq", minus_y.reshape(shape), eye_j)
    y_in = y_in.reshape(2 * kx_local * KY, -1)
    y_out = np.einsum("pqlsy,jk->ysjpqkl", plus_y.reshape(shape), eye_j)
    y_out = y_out.reshape(cells_y * size_y * kx_local * 2, -1)
    z_in_4 = parts.reshape(modes_z * 2, -1) * scale_in
    z_out_4 = (parts * weight).reshape(modes_z * 2, -1)
    x_in_4 = minus_x.reshape(2, 2, modes_x, size_x, cells_x).transpose(4, 2, 0, 3, 1)
    x_in_4 = x_in_4.reshape(cells_x * modes_x * 2, -1)
    x_out_4 = plus_x.reshape(2, 2, modes_x, size_x, cells_x).transpose(4, 3, 0, 2, 1)
    x_out_4 = x_out_4.reshape(cells_x * size_x * 2, -1)
    return [split_table(t) for t in (z_in, x_in, y_in, y_out, x_out, z_out, z_in_4, x_in_4, x_out_4, z_out_4)]


def call(body, out_shape, *args, scratch=(), flops=0, smem=(), hbm=(), out_hbm=(), vmem=24, light=False):
    def spec(index, kept):
        return pl.BlockSpec(memory_space=pl.ANY if index in kept else pltpu.VMEM)

    in_specs = [pl.BlockSpec(memory_space=pltpu.SMEM) if i in smem else spec(i, hbm) for i in range(len(args))]
    size = 0 if light else sum(a.size * a.dtype.itemsize for a in args)
    many = isinstance(out_shape, tuple)
    return pl.pallas_call(
        body,
        out_shape=out_shape,
        in_specs=in_specs,
        out_specs=tuple(spec(i, out_hbm) for i in range(len(out_shape))) if many else spec(0, out_hbm),
        scratch_shapes=list(scratch),
        compiler_params=pltpu.CompilerParams(vmem_limit_bytes=vmem << 20),
        cost_estimate=pl.CostEstimate(flops=flops, bytes_accessed=size, transcendentals=0),
    )(*args)


def copies(pairs, semaphores, first=0):
    started = [pltpu.make_async_copy(a, b, semaphores.at[first + i]) for i, (a, b) in enumerate(pairs)]
    for copy in started:
        copy.start()
    return started


def wait(started):
    for copy in started:
        copy.wait()


MAIN = 32


def store_packed(ref, main, last):
    count = ref.shape[0]
    for tile in range(2):
        block = main[:, LANES * tile : LANES * tile + LANES]
        ref[:, 8 * tile : 8 * tile + 8, :] = block.reshape(count, 8, LANES)
    for dest in range(count):
        ref[dest, 16:18, :] = last[2 * dest : 2 * dest + 2]


def load_packed(ref, last):
    count = ref.shape[0]
    for source in range(count):
        last[2 * source : 2 * source + 2, :] = ref[source, 16:18, :]
    return jnp.concatenate([ref[:, 8 * t : 8 * t + 8, :].reshape(count * 8, LANES) for t in range(2)], axis=1)


def store_payload(ref, rows):
    count = ref.shape[0]
    for tile in range(3):
        width = min(LANES, rows.shape[1] - LANES * tile)
        block = rows[:, LANES * tile : LANES * tile + width]
        ref[:, 8 * tile : 8 * tile + 8, :width] = block.reshape(count, 8, width)
        if width < LANES:
            ref[:, 8 * tile : 8 * tile + 8, width:] = jnp.zeros((count, 8, LANES - width), F32)


def load_payload(ref):
    count = ref.shape[0]
    tiles = [ref[:, 8 * t : 8 * t + 8, :].reshape(count * 8, LANES) for t in range(3)]
    return jnp.concatenate(tiles, axis=1)


def z_in_body(field_hbm, table_hbm, table_4, grid_ref, out_ref, field, table, sems, last):
    arrived = copies([(field_hbm, field), (table_hbm, table)], sems)
    wait(arrived[:1])
    channels, cells_x, width = field.shape
    for x in range(cells_x):
        piece = field[:, x, :]
        piece = jnp.concatenate([piece, jnp.zeros((CP - channels, width), F32)], axis=0)
        for y in range(width // NZ):
            grid_ref[y, :, NZ * x : NZ * x + NZ] = piece[:, NZ * y : NZ * y + NZ]
            spot = 4 * ((width // NZ) * x + y)
            last[spot : spot + 4, :] = piece[MAIN:channels, NZ * y : NZ * y + NZ]
    cells = grid_ref[:, :MAIN, :].reshape(-1, grid_ref.shape[2])
    wait(arrived[1:])
    main = product(table, cells, ((1,), (1,)))
    store_packed(out_ref, main, product(table_4, last[...], ((1,), (1,))))


def x_in_body(received, table, table_4, out_ref, last):
    main = product(table, load_packed(received, last), ((1,), (0,)))
    turned = product(table_4, last[...], ((1,), (0,)))
    rows = main.shape[0]
    rest = turned[:rows, :32]
    for x in range(1, 4):
        rest = rest + turned[rows * x : rows * x + rows, 32 * x : 32 * x + 32]
    store_payload(out_ref, jnp.concatenate([main, rest], axis=1))


def x_out_body(received, table, table_4, out_ref):
    rows = load_payload(received)
    main = product(table, rows[:, :256], ((1,), (0,)))
    turned = product(table_4, rows[:, 256:], ((1,), (0,)))
    count = turned.shape[0] // 4
    last = jnp.concatenate([turned[count * x : count * x + count, :32] for x in range(4)], axis=1)
    store_packed(out_ref, main, last)


def mix_body(received, weights, kept, place, y_in, y_out, out_ref, stacked, s_re, s_im):
    cells_y = received.shape[0]
    rows = load_payload(received)
    block = rows.shape[0]
    for y in range(cells_y):
        own = slice(y * block, (y + 1) * block)
        stacked[own, :MAIN] = rows[:, MAIN * y : MAIN * y + MAIN]
        stacked[own, MAIN : MAIN + 4] = rows[:, MAIN * cells_y + 4 * y : MAIN * cells_y + 4 * y + 4]
        stacked[own, MAIN + 4 :] = jnp.zeros((block, LANES - MAIN - 4), F32)
    modes = product(y_in, stacked[...], ((1,), (0,)))
    count = modes.shape[0] // 2
    s_re[...] = modes[:count].T
    s_im[...] = modes[count:].T
    channels = 36
    pair = 2 * channels
    row = lax.broadcasted_iota(jnp.int32, (8, count), 0)

    def spread(ref, c):
        first = jnp.broadcast_to(ref[c : c + 1, :], (8, count))
        second = jnp.broadcast_to(ref[c + 1 : c + 2, :], (8, count))
        middle = jnp.where(row < 4, first, second)
        return jnp.concatenate([first] * 4 + [middle] + [second] * 4, axis=0)

    total_re = jnp.zeros((pair, count), F32)
    total_im = jnp.zeros((pair, count), F32)
    for c in range(0, channels, 2):
        w_re = weights[0, channels * c : channels * c + pair, :]
        w_im = weights[1, channels * c : channels * c + pair, :]
        f_re, f_im = spread(s_re, c), spread(s_im, c)
        total_re += w_re * f_re - w_im * f_im
        total_im += w_re * f_im + w_im * f_re
    keep = place[0] < kept[...]

    def fold(total):
        total = total[:channels] + total[channels:]
        return jnp.concatenate([jnp.where(keep, total, 0.0), jnp.zeros((CP - channels, count), F32)], axis=0)

    mixed = jnp.concatenate([fold(total_re), fold(total_im)], axis=1)
    back = product(y_out, mixed, ((1,), (1,)))
    pieces = [back[y * block : (y + 1) * block] for y in range(cells_y)]
    lanes = [piece[:, :MAIN] for piece in pieces] + [piece[:, MAIN : MAIN + 4] for piece in pieces]
    lanes = jnp.concatenate(lanes, axis=1)
    store_payload(out_ref, lanes)


def gelu_exact(values):
    return 0.5 * values * (1.0 + lax.erf(values * math.sqrt(0.5)))


ROW = 368


def taps_body(kernels, after, *refs):
    channels = kernels.shape[2]
    *outs, scratch = refs
    for r, out_ref in enumerate(outs):
        scratch[...] = jnp.zeros(scratch.shape, F32)
        for tap in range(27):
            row, lane = CP * (tap % 3), CP * (tap // 3)
            scratch[row : row + channels, lane : lane + channels] = kernels[r, tap]
        high, low = split(scratch[...].T[:ROW])
        out_ref[:ROW, :128] = high
        out_ref[:ROW, 128:] = high
        out_ref[ROW:, :128] = low
        out_ref[ROW:, 128:] = jnp.zeros((ROW, 128), BF16)


def convolve_rows(load_row, rows_in, width, taps, refs, finish, rest=()):
    stack_a, stack_b, first_sum, second_sum, whole = refs
    z_position = lax.broadcasted_iota(jnp.int32, (CP, LANES), 1) % NZ
    has_lower = z_position >= 1
    has_upper = z_position <= NZ - 2
    low_half = lax.broadcasted_iota(jnp.int32, (CP, LANES), 1) < NZ
    tiles = width // LANES

    def prepare(index, stack):
        cells = load_row(index)
        for t in range(tiles):
            piece = cells[:, LANES * t : LANES * t + LANES]
            lower = jnp.where(has_lower, pltpu.roll(piece, 1, 1), 0.0)
            upper = jnp.where(has_upper, pltpu.roll(piece, LANES - 1, 1), 0.0)
            rows = jnp.concatenate([lower, piece, upper, jnp.zeros((8, LANES), F32)], axis=0)
            high, low = split(rows)
            stack[:128, LANES * t : LANES * t + LANES] = high
            stack[128:, LANES * t : LANES * t + LANES] = low

    def emit(row):
        sums = [[whole[CP * a : CP * a + CP, LANES * t : LANES * t + LANES] for t in range(tiles)] for a in range(3)]
        out = []
        for t in range(tiles):
            low_part = sums[0][t]
            if t + 1 < tiles:
                low_part = low_part + sums[2][t + 1]
            high_part = sums[2][t]
            if t > 0:
                high_part = high_part + sums[0][t - 1]
            turned = pltpu.roll(jnp.where(low_half, low_part, high_part), NZ, 1)
            out.append(sums[1][t] + turned)
        finish(row, out)

    def step(index, here, there):
        prepare(jnp.minimum(index + 1, rows_in - 1), there)
        emit(jnp.maximum(index - 3, 0))
        for t in range(tiles // 2):
            lanes = slice(2 * LANES * t, 2 * LANES * t + 2 * LANES)
            terms = lax.dot_general(
                taps[...], here[:, lanes], (((1,), (0,)), ((), ())), preferred_element_type=F32
            )
            for a in range(3):
                rows = slice(CP * a, CP * a + CP)
                piece = []
                for b in range(3):
                    first = CP * (3 * a + b)
                    piece.append(terms[first : first + CP] + terms[ROW + first : ROW + first + CP])
                whole[rows, lanes] = second_sum[rows, lanes] + piece[2]
                second_sum[rows, lanes] = first_sum[rows, lanes] + piece[1]
                first_sum[rows, lanes] = piece[0]

    def pair(j, carry):
        step(2 * j, stack_a, stack_b)
        step(2 * j + 1, stack_b, stack_a)
        return carry

    prepare(0, stack_a)
    pair(0, 0)
    wait(rest)
    lax.fori_loop(1, rows_in // 2, pair, 0)
    emit(rows_in - 3)


def conv_scratch(width):
    return [pltpu.VMEM((256, width), BF16)] * 2 + [pltpu.VMEM((3 * CP, width), F32)] * 3


def inside(place, first_x, sizes, width):
    cells_x, cells_y, full_x, full_y = sizes
    x = place[0] * cells_x + first_x + lax.broadcasted_iota(jnp.int32, (CP, width), 1) // NZ
    in_x = (x >= 0) & (x < full_x)

    def at(local_y):
        y = place[1] * cells_y + local_y
        return in_x & ((y >= 0) & (y < full_y))

    return at


def gather(sources, rows, target, first):
    width = sources[0].shape[2]
    count = rows.stop - rows.start
    return [
        (s.at[rows], target.at[slice(first, first + count), :, slice(width * i, width * i + width)])
        for i, s in enumerate(sources)
    ]


def join(sources, rows, target, first):
    width = sources[0].shape[2]
    count = rows.stop - rows.start
    for i, source in enumerate(sources):
        target[first : first + count, :, width * i : width * i + width] = source[rows]


def inner_body(sizes, left, own, right, place, taps, out_ref, rows, *refs):
    count = own.shape[0]
    join((left, own, right), slice(0, count), rows, 0)
    keep = inside(place, -2, sizes, 512)

    def finish(row, tiles):
        values = jnp.concatenate(tiles[1:5], axis=1)
        out_ref[row] = jnp.where(keep(row + 1), gelu_exact(values), 0.0)

    convolve_rows(lambda i: rows[i], count, 768, taps, refs, finish)


def outer_body(sizes, before, left, own, right, after, place, taps, out_ref, rows, *refs):
    count = own.shape[0]
    sides = (left, own, right)
    rows[0:3] = before[...]
    join(sides, slice(0, 2), rows, 3)
    join(sides, slice(count - 2, count), rows, 5)
    rows[7:10] = after[...]
    keep = inside(place, -2, sizes, 512)

    def finish(row, tiles):
        values = jnp.concatenate(tiles[1:5], axis=1)
        local_y = jnp.where(row < 4, row - 2, row + count - 6)
        out_ref[row] = jnp.where(keep(local_y), gelu_exact(values), 0.0)

    convolve_rows(lambda i: rows[i], 10, 768, taps, refs, finish)


def later_body(sizes, inner, outer, place, taps_1, taps_2, out_ref, rows, second, *refs):
    count = inner.shape[0]
    rows[0:3] = outer[0:3]
    rows[3 : 3 + count] = inner[...]
    rows[3 + count :] = outer[5:8]
    keep = inside(place, -2, sizes, 512)

    def finish_second(row, tiles):
        values = jnp.concatenate(tiles, axis=1)
        second[row] = jnp.where(keep(row - 1), gelu_exact(values), 0.0)

    def finish_third(row, tiles):
        out_ref[row] = jnp.concatenate(tiles[1:3], axis=1)

    convolve_rows(lambda i: rows[i], count + 6, 512, taps_1, refs, finish_second)
    convolve_rows(lambda i: second[i], count + 4, 512, taps_2, refs, finish_third)


def last_body(received, third, table, table_4, out_ref, last, spectral):
    spectrum = load_packed(received, last)
    cells_y = third.shape[0]

    def turn(values, factors):
        high, low = split(values)

        def dot(left, right):
            return lax.dot_general(left, right, (((0,), (0,)), ((), ())), preferred_element_type=F32)

        return dot(high, factors[0]) + dot(low, factors[0]) + dot(high, factors[1])

    spectral[:, :MAIN, :] = turn(spectrum, table).reshape(cells_y, MAIN, -1)
    spectral[:, MAIN:, :] = jnp.zeros((cells_y, CP - MAIN, spectral.shape[2]), F32)
    rest = turn(last[...], table_4)
    for x in range(4):
        for y in range(cells_y):
            spot = 4 * (cells_y * x + y)
            spectral[y, MAIN : MAIN + 4, NZ * x : NZ * x + NZ] = rest[spot : spot + 4]
    out = gelu_exact(spectral[...] + third[...])
    channels, cells_x, width = out_ref.shape
    for x in range(cells_x):
        piece = [out[y, :channels, NZ * x : NZ * x + NZ] for y in range(width // NZ)]
        out_ref[:, x, :] = jnp.concatenate(piece, axis=1)


def shift(values, axis, step):
    count = lax.axis_size(axis)
    pairs = [(i, i + step) for i in range(count) if 0 <= i + step < count]
    return lax.ppermute(values, axis, pairs)


def shards(field, mix_weights, kept_z, conv_kernels):
    channels = field.shape[0]
    cells_x = field.shape[1]
    cells_y = field.shape[2] // NZ
    size_x = lax.axis_size("gx")
    size_y = lax.axis_size("gy")
    full_x, full_y = cells_x * size_x, cells_y * size_y
    modes_z = mix_weights.shape[3] * size_x
    kx_local = mix_weights.shape[4] // KY
    modes_x = kx_local * size_y
    place = jnp.stack([lax.axis_index("gx"), lax.axis_index("gy")]).astype(jnp.int32)
    z_in, x_in, y_in, y_out, x_out, z_out, z_in_4, x_in_4, x_out_4, z_out_4 = [
        jnp.asarray(t) for t in tables(size_x, size_y, cells_x, cells_y, modes_x, modes_z)
    ]

    sizes = (cells_x, cells_y, full_x, full_y)
    taps_shape = jax.ShapeDtypeStruct((2 * ROW, 256), BF16)

    grid, sent = call(
        z_in_body,
        (
            jax.ShapeDtypeStruct((cells_y, CP, cells_x * NZ), F32),
            jax.ShapeDtypeStruct((size_x, 18, LANES), F32),
        ),
        field, z_in, z_in_4,
        scratch=[pltpu.VMEM(field.shape, F32), pltpu.VMEM(z_in.shape, BF16), pltpu.SemaphoreType.DMA((2,)),
                 pltpu.VMEM((LANES, NZ), F32)],
        hbm=(0, 1), vmem=FULL,
    )
    left = shift(grid, "gx", 1)
    right = shift(grid, "gx", -1)
    after, _ = lax.optimization_barrier((place, sent))
    taps = call(
        taps_body, (taps_shape,) * 3, conv_kernels, after, scratch=[pltpu.VMEM((128, 384), F32)], smem=(1,)
    )
    received = lax.all_to_all(sent, "gx", 0, 0, tiled=True)
    received, *taps = lax.optimization_barrier((received, *taps))

    sent = call(
        x_in_body, jax.ShapeDtypeStruct((size_y, 24, LANES), F32), received, x_in, x_in_4,
        scratch=[pltpu.VMEM((2 * size_x, LANES), F32)],
    )

    left, right, _ = lax.optimization_barrier((left, right, sent))
    received = lax.all_to_all(sent, "gy", 0, 0, tiled=True)

    def edge(rows):
        return jnp.concatenate([left[rows], grid[rows], right[rows]], axis=2)

    before = shift(edge(slice(cells_y - 3, cells_y)), "gy", 1)
    after = shift(edge(slice(0, 3)), "gy", -1)
    inner = call(
        lambda *refs: inner_body(sizes, *refs),
        jax.ShapeDtypeStruct((cells_y - 2, CP, 512), F32),
        left, grid, right, place, taps[0],
        scratch=[pltpu.VMEM((cells_y, CP, 768), F32)] + conv_scratch(768),
        smem=(3,), light=False, flops=INNER << 20,
    )
    inner, received = lax.optimization_barrier((inner, received))
    weights = mix_weights.reshape(2, channels * channels, kx_local * KY)
    sent = call(
        mix_body,
        jax.ShapeDtypeStruct((size_y, 24, LANES), F32),
        received, weights, kept_z.reshape(1, -1), place, y_in, y_out,
        scratch=[pltpu.VMEM((cells_y * size_y * kx_local * 2, LANES), F32)]
        + [pltpu.VMEM((LANES, kx_local * KY), F32)] * 2,
        smem=(3,), flops=8 << 30,
    )
    before, after, _ = lax.optimization_barrier((before, after, sent))
    received = lax.all_to_all(sent, "gy", 0, 0, tiled=True)
    outer = call(
        lambda *refs: outer_body(sizes, *refs),
        jax.ShapeDtypeStruct((8, CP, 512), F32),
        before, left, grid, right, after, place, taps[0],
        scratch=[pltpu.VMEM((10, CP, 768), F32)] + conv_scratch(768),
        smem=(5,), flops=OUTER << 20,
    )
    outer, received = lax.optimization_barrier((outer, received))
    sent = call(x_out_body, jax.ShapeDtypeStruct((size_x, 18, LANES), F32), received, x_out, x_out_4)
    outer, sent = lax.optimization_barrier((outer, sent))
    received = lax.all_to_all(sent, "gx", 0, 0, tiled=True)
    third = call(
        lambda *refs: later_body(sizes, *refs),
        jax.ShapeDtypeStruct((cells_y, CP, cells_x * NZ), F32),
        inner, outer, place, taps[1], taps[2],
        scratch=[
            pltpu.VMEM((cells_y + 4, CP, 512), F32),
            pltpu.VMEM((cells_y + 2, CP, 512), F32),
        ]
        + conv_scratch(512),
        smem=(2,), flops=8 << 30,
    )
    return call(
        last_body, jax.ShapeDtypeStruct(field.shape, F32), received, third, z_out, z_out_4,
        scratch=[pltpu.VMEM((2 * size_x, LANES), F32), pltpu.VMEM(third.shape, F32)],
    )


def solution(mesh):
    placed = (P(None, "gx", "gy"), P(None, None, None, "gx", "gy"), P("gy"), P())
    return jax.shard_map(
        shards, mesh=mesh, in_specs=placed, out_specs=P(None, "gx", "gy"), check_vma=False
    )
```

```python
import math

import jax
import jax.numpy as jnp
import ml_dtypes
import numpy as np
from jax import lax
from jax.experimental import pallas as pl
from jax.experimental.pallas import tpu as pltpu
from jax.sharding import PartitionSpec as P

NZ = 64
KY = 32
MIX = 8192
CONV = 12288
FULL = 60
CP = 40
LANES = 128
F32 = jnp.float32
BF16 = jnp.bfloat16


def split_table(table):
    high = table.astype(np.float32).astype(ml_dtypes.bfloat16)
    low = (table - high.astype(np.float64)).astype(np.float32).astype(ml_dtypes.bfloat16)
    return np.stack([high, low])


def split(values):
    high = values.astype(BF16)
    return high, (values - high.astype(F32)).astype(BF16)


def product(table, values, dims):
    high, low = split(values)
    numbers = (dims, ((), ()))

    def dot(left, right):
        return lax.dot_general(left, right, numbers, preferred_element_type=F32)

    return dot(table[0], high) + dot(table[0], low) + dot(table[1], high)


def frequencies(count, length):
    index = np.arange(count)
    return np.where(index < count // 2, index, length - count + index)


def tables(size_x, size_y, cells_x, cells_y, modes_x, modes_z):
    full_x, full_y = size_x * cells_x, size_y * cells_y
    scale_in = 1.0 / math.sqrt(full_x * full_y * NZ)
    scale_out = 1.0 / math.sqrt(modes_x * KY * modes_z)
    kx_local = modes_x // size_y
    z = np.arange(NZ)
    k = np.arange(modes_z)
    turn = 2.0 * np.pi * (np.outer(k, z) % NZ) / NZ
    eye_x = np.eye(cells_x)
    parts = np.stack([np.cos(turn), -np.sin(turn)], 1)
    z_in = np.einsum("kpz,xw->kpxwz", parts, eye_x).reshape(modes_z * 2 * cells_x, -1) * scale_in
    weight = np.where(k == 0, 1.0, 2.0)[:, None, None] * scale_out
    z_out = np.einsum("kpz,xw->kpxwz", parts * weight, eye_x).reshape(modes_z * 2 * cells_x, -1)

    def rotation(freq, positions, length):
        angle = 2.0 * np.pi * (np.outer(freq, positions) % length) / length
        cos, sin = np.cos(angle), np.sin(angle)
        return np.stack([np.stack([cos, -sin]), np.stack([sin, cos])])

    plus_x = rotation(frequencies(modes_x, full_x), np.arange(full_x), full_x)
    minus_x = plus_x.transpose(1, 0, 2, 3)
    x_in = minus_x.reshape(2, 2, modes_x, size_x, cells_x).transpose(2, 0, 3, 1, 4)
    x_in = x_in.reshape(modes_x * 2, -1)
    x_out = plus_x.reshape(2, 2, modes_x, size_x, cells_x).transpose(3, 0, 4, 2, 1)
    x_out = x_out.reshape(size_x * 2 * cells_x, -1)
    plus_y = rotation(frequencies(KY, full_y), np.arange(full_y), full_y)
    minus_y = plus_y.transpose(1, 0, 2, 3)
    eye_j = np.eye(kx_local)
    shape = (2, 2, KY, size_y, cells_y)
    y_in = np.einsum("pqlsy,jk->pjlyskq", minus_y.reshape(shape), eye_j)
    y_in = y_in.reshape(2 * kx_local * KY, -1)
    y_out = np.einsum("pqlsy,jk->ysjpqkl", plus_y.reshape(shape), eye_j)
    y_out = y_out.reshape(cells_y * size_y * kx_local * 2, -1)
    return [split_table(t) for t in (z_in, x_in, y_in, y_out, x_out, z_out)]


def call(body, out_shape, *args, scratch=(), flops=0, smem=(), hbm=(), out_hbm=(), vmem=24, light=False):
    def spec(index, kept):
        return pl.BlockSpec(memory_space=pl.ANY if index in kept else pltpu.VMEM)

    in_specs = [pl.BlockSpec(memory_space=pltpu.SMEM) if i in smem else spec(i, hbm) for i in range(len(args))]
    size = 0 if light else sum(a.size * a.dtype.itemsize for a in args)
    many = isinstance(out_shape, tuple)
    return pl.pallas_call(
        body,
        out_shape=out_shape,
        in_specs=in_specs,
        out_specs=tuple(spec(i, out_hbm) for i in range(len(out_shape))) if many else spec(0, out_hbm),
        scratch_shapes=list(scratch),
        compiler_params=pltpu.CompilerParams(vmem_limit_bytes=vmem << 20),
        cost_estimate=pl.CostEstimate(flops=flops, bytes_accessed=size, transcendentals=0),
    )(*args)


def copies(pairs, semaphores, first=0):
    started = [pltpu.make_async_copy(a, b, semaphores.at[first + i]) for i, (a, b) in enumerate(pairs)]
    for copy in started:
        copy.start()
    return started


def wait(started):
    for copy in started:
        copy.wait()


def store_payload(ref, rows):
    count = ref.shape[0]
    for tile in range(3):
        width = min(LANES, rows.shape[1] - LANES * tile)
        block = rows[:, LANES * tile : LANES * tile + width]
        ref[:, 8 * tile : 8 * tile + 8, :width] = block.reshape(count, 8, width)
        if width < LANES:
            ref[:, 8 * tile : 8 * tile + 8, width:] = jnp.zeros((count, 8, LANES - width), F32)


def load_payload(ref):
    count = ref.shape[0]
    tiles = [ref[:, 8 * t : 8 * t + 8, :].reshape(count * 8, LANES) for t in range(3)]
    return jnp.concatenate(tiles, axis=1)


def z_in_body(field_hbm, table_hbm, grid_ref, out_ref, field, table, sems):
    arrived = copies([(field_hbm, field), (table_hbm, table)], sems)
    wait(arrived[:1])
    channels, cells_x, width = field.shape
    for x in range(cells_x):
        piece = field[:, x, :]
        piece = jnp.concatenate([piece, jnp.zeros((CP - channels, width), F32)], axis=0)
        for y in range(width // NZ):
            grid_ref[y, :, NZ * x : NZ * x + NZ] = piece[:, NZ * y : NZ * y + NZ]
    cells = grid_ref[...].reshape(-1, grid_ref.shape[2])
    wait(arrived[1:])
    store_payload(out_ref, product(table, cells, ((1,), (1,))))


def rows_body(received, table, out_ref):
    rows = product(table, load_payload(received), ((1,), (0,)))
    for tile in range(3):
        block = rows[:, LANES * tile : LANES * tile + LANES]
        out_ref[:, 8 * tile : 8 * tile + 8, :] = block.reshape(out_ref.shape[0], 8, LANES)


def mix_body(received, weights, kept, place, y_in, y_out, out_ref, stacked, s_re, s_im):
    cells_y = received.shape[0]
    rows = load_payload(received)
    block = rows.shape[0]
    for y in range(cells_y):
        stacked[y * block : (y + 1) * block, :CP] = rows[:, CP * y : CP * y + CP]
        stacked[y * block : (y + 1) * block, CP:] = jnp.zeros((block, LANES - CP), F32)
    modes = product(y_in, stacked[...], ((1,), (0,)))
    count = modes.shape[0] // 2
    s_re[...] = modes[:count].T
    s_im[...] = modes[count:].T
    channels = 36
    pair = 2 * channels
    row = lax.broadcasted_iota(jnp.int32, (8, count), 0)

    def spread(ref, c):
        first = jnp.broadcast_to(ref[c : c + 1, :], (8, count))
        second = jnp.broadcast_to(ref[c + 1 : c + 2, :], (8, count))
        middle = jnp.where(row < 4, first, second)
        return jnp.concatenate([first] * 4 + [middle] + [second] * 4, axis=0)

    total_re = jnp.zeros((pair, count), F32)
    total_im = jnp.zeros((pair, count), F32)
    for c in range(0, channels, 2):
        w_re = weights[0, channels * c : channels * c + pair, :]
        w_im = weights[1, channels * c : channels * c + pair, :]
        f_re, f_im = spread(s_re, c), spread(s_im, c)
        total_re += w_re * f_re - w_im * f_im
        total_im += w_re * f_im + w_im * f_re
    keep = place[0] < kept[...]

    def fold(total):
        total = total[:channels] + total[channels:]
        return jnp.concatenate([jnp.where(keep, total, 0.0), jnp.zeros((CP - channels, count), F32)], axis=0)

    mixed = jnp.concatenate([fold(total_re), fold(total_im)], axis=1)
    back = product(y_out, mixed, ((1,), (1,)))
    lanes = jnp.concatenate([back[y * block : (y + 1) * block] for y in range(cells_y)], axis=1)
    store_payload(out_ref, lanes)


def gelu_exact(values):
    return 0.5 * values * (1.0 + lax.erf(values * math.sqrt(0.5)))


ROW = 368


def make_taps(kernels, which, out_ref, scratch):
    channels = kernels.shape[2]
    scratch[...] = jnp.zeros(scratch.shape, F32)
    for tap in range(27):
        row, lane = CP * (tap % 3), CP * (tap // 3)
        scratch[row : row + channels, lane : lane + channels] = kernels[which, tap]
    high, low = split(scratch[...].T[:ROW])
    out_ref[:ROW, :128] = high
    out_ref[:ROW, 128:] = high
    out_ref[ROW:, :128] = low
    out_ref[ROW:, 128:] = jnp.zeros((ROW, 128), BF16)


def convolve_rows(load_row, rows_in, width, taps, refs, finish):
    stack_a, stack_b, first_sum, second_sum, whole = refs
    z_position = lax.broadcasted_iota(jnp.int32, (CP, LANES), 1) % NZ
    has_lower = z_position >= 1
    has_upper = z_position <= NZ - 2
    low_half = lax.broadcasted_iota(jnp.int32, (CP, LANES), 1) < NZ
    tiles = width // LANES

    def prepare(index, stack):
        cells = load_row(index)
        for t in range(tiles):
            piece = cells[:, LANES * t : LANES * t + LANES]
            lower = jnp.where(has_lower, pltpu.roll(piece, 1, 1), 0.0)
            upper = jnp.where(has_upper, pltpu.roll(piece, LANES - 1, 1), 0.0)
            rows = jnp.concatenate([lower, piece, upper, jnp.zeros((8, LANES), F32)], axis=0)
            high, low = split(rows)
            stack[:128, LANES * t : LANES * t + LANES] = high
            stack[128:, LANES * t : LANES * t + LANES] = low

    def emit(row):
        sums = [[whole[CP * a : CP * a + CP, LANES * t : LANES * t + LANES] for t in range(tiles)] for a in range(3)]
        out = []
        for t in range(tiles):
            low_part = sums[0][t]
            if t + 1 < tiles:
                low_part = low_part + sums[2][t + 1]
            high_part = sums[2][t]
            if t > 0:
                high_part = high_part + sums[0][t - 1]
            turned = pltpu.roll(jnp.where(low_half, low_part, high_part), NZ, 1)
            out.append(sums[1][t] + turned)
        finish(row, out)

    def step(index, here, there):
        prepare(jnp.minimum(index + 1, rows_in - 1), there)
        emit(jnp.maximum(index - 3, 0))
        for t in range(tiles // 2):
            lanes = slice(2 * LANES * t, 2 * LANES * t + 2 * LANES)
            terms = lax.dot_general(
                taps[...], here[:, lanes], (((1,), (0,)), ((), ())), preferred_element_type=F32
            )
            for a in range(3):
                rows = slice(CP * a, CP * a + CP)
                piece = []
                for b in range(3):
                    first = CP * (3 * a + b)
                    piece.append(terms[first : first + CP] + terms[ROW + first : ROW + first + CP])
                whole[rows, lanes] = second_sum[rows, lanes] + piece[2]
                second_sum[rows, lanes] = first_sum[rows, lanes] + piece[1]
                first_sum[rows, lanes] = piece[0]

    def pair(j, carry):
        step(2 * j, stack_a, stack_b)
        step(2 * j + 1, stack_b, stack_a)
        return carry

    prepare(0, stack_a)
    lax.fori_loop(0, rows_in // 2, pair, 0)
    emit(rows_in - 3)


def conv_scratch(width):
    return [pltpu.VMEM((256, width), BF16)] * 2 + [pltpu.VMEM((3 * CP, width), F32)] * 3


def inside(place, first_x, sizes, width):
    cells_x, cells_y, full_x, full_y = sizes
    x = place[0] * cells_x + first_x + lax.broadcasted_iota(jnp.int32, (CP, width), 1) // NZ
    in_x = (x >= 0) & (x < full_x)

    def at(local_y):
        y = place[1] * cells_y + local_y
        return in_x & ((y >= 0) & (y < full_y))

    return at


def gather(sources, rows, target, first):
    width = sources[0].shape[2]
    count = rows.stop - rows.start
    return [
        (s.at[rows], target.at[slice(first, first + count), :, slice(width * i, width * i + width)])
        for i, s in enumerate(sources)
    ]


def join(sources, rows, target, first):
    width = sources[0].shape[2]
    count = rows.stop - rows.start
    for i, source in enumerate(sources):
        target[first : first + count, :, width * i : width * i + width] = source[rows]


def convolutions_body(sizes, before, left, own, right, after, place, kernels, out_ref, *refs):
    rows, first, second, table, taps = refs[:5]
    wide, narrow = refs[5:10], refs[10:]
    make_taps(kernels, 0, taps, table)
    count = own.shape[0]
    rows[0:3] = before[...]
    join((left, own, right), slice(0, count), rows, 3)
    rows[3 + count :] = after[...]
    keep = inside(place, -2, sizes, 512)

    def finish_first(row, tiles):
        values = jnp.concatenate(tiles[1:5], axis=1)
        first[row] = jnp.where(keep(row - 2), gelu_exact(values), 0.0)

    def finish_second(row, tiles):
        values = jnp.concatenate(tiles, axis=1)
        second[row] = jnp.where(keep(row - 1), gelu_exact(values), 0.0)

    def finish_third(row, tiles):
        out_ref[row] = jnp.concatenate(tiles[1:3], axis=1)

    convolve_rows(lambda i: rows[i], count + 6, 768, taps, wide, finish_first)
    make_taps(kernels, 1, taps, table)
    convolve_rows(lambda i: first[i], count + 4, 512, taps, narrow, finish_second)
    make_taps(kernels, 2, taps, table)
    convolve_rows(lambda i: second[i], count + 2, 512, taps, narrow, finish_third)


def last_body(received, third, table, out_ref):
    spectrum = load_payload(received)[:, : third.shape[0] * CP]
    high, low = split(spectrum)

    def dot(left, right):
        return lax.dot_general(left, right, (((0,), (0,)), ((), ())), preferred_element_type=F32)

    spectral = dot(high, table[0]) + dot(low, table[0]) + dot(high, table[1])
    out = gelu_exact(spectral.reshape(third.shape) + third[...])
    channels, cells_x, width = out_ref.shape
    for x in range(cells_x):
        piece = [out[y, :channels, NZ * x : NZ * x + NZ] for y in range(width // NZ)]
        out_ref[:, x, :] = jnp.concatenate(piece, axis=1)


def shift(values, axis, step):
    count = lax.axis_size(axis)
    pairs = [(i, i + step) for i in range(count) if 0 <= i + step < count]
    return lax.ppermute(values, axis, pairs)


def shards(field, mix_weights, kept_z, conv_kernels):
    channels = field.shape[0]
    cells_x = field.shape[1]
    cells_y = field.shape[2] // NZ
    size_x = lax.axis_size("gx")
    size_y = lax.axis_size("gy")
    full_x, full_y = cells_x * size_x, cells_y * size_y
    modes_z = mix_weights.shape[3] * size_x
    kx_local = mix_weights.shape[4] // KY
    modes_x = kx_local * size_y
    place = jnp.stack([lax.axis_index("gx"), lax.axis_index("gy")]).astype(jnp.int32)
    z_in, x_in, y_in, y_out, x_out, z_out = [
        jnp.asarray(t) for t in tables(size_x, size_y, cells_x, cells_y, modes_x, modes_z)
    ]

    sizes = (cells_x, cells_y, full_x, full_y)
    grid, sent = call(
        z_in_body,
        (
            jax.ShapeDtypeStruct((cells_y, CP, cells_x * NZ), F32),
            jax.ShapeDtypeStruct((size_x, 24, LANES), F32),
        ),
        field, z_in,
        scratch=[pltpu.VMEM(field.shape, F32), pltpu.VMEM(z_in.shape, BF16), pltpu.SemaphoreType.DMA((2,))],
        hbm=(0, 1), vmem=FULL,
    )
    left = shift(grid, "gx", 1)
    right = shift(grid, "gx", -1)
    received = lax.all_to_all(sent, "gx", 0, 0, tiled=True)

    sent = call(rows_body, jax.ShapeDtypeStruct((size_y, 24, LANES), F32), received, x_in)

    left, right, _ = lax.optimization_barrier((left, right, sent))
    received = lax.all_to_all(sent, "gy", 0, 0, tiled=True)

    def edge(rows):
        return jnp.concatenate([left[rows], grid[rows], right[rows]], axis=2)

    before = shift(edge(slice(cells_y - 3, cells_y)), "gy", 1)
    after = shift(edge(slice(0, 3)), "gy", -1)
    weights = mix_weights.reshape(2, channels * channels, kx_local * KY)
    sent = call(
        mix_body,
        jax.ShapeDtypeStruct((size_y, 24, LANES), F32),
        received, weights, kept_z.reshape(1, -1), place, y_in, y_out,
        scratch=[pltpu.VMEM((cells_y * size_y * kx_local * 2, LANES), F32)]
        + [pltpu.VMEM((LANES, kx_local * KY), F32)] * 2,
        smem=(3,), flops=MIX << 20,
    )
    received = lax.all_to_all(sent, "gy", 0, 0, tiled=True)
    sent = call(rows_body, jax.ShapeDtypeStruct((size_x, 24, LANES), F32), received, x_out)
    before, after, _ = lax.optimization_barrier((before, after, sent))
    received = lax.all_to_all(sent, "gx", 0, 0, tiled=True)
    third = call(
        lambda *refs: convolutions_body(sizes, *refs),
        jax.ShapeDtypeStruct((cells_y, CP, cells_x * NZ), F32),
        before, left, grid, right, after, place, conv_kernels,
        scratch=[
            pltpu.VMEM((cells_y + 6, CP, 768), F32),
            pltpu.VMEM((cells_y + 4, CP, 512), F32),
            pltpu.VMEM((cells_y + 2, CP, 512), F32),
            pltpu.VMEM((128, 384), F32),
            pltpu.VMEM((2 * ROW, 256), BF16),
        ]
        + conv_scratch(768) + conv_scratch(512),
        smem=(5,), flops=CONV << 20,
    )
    return call(
        last_body, jax.ShapeDtypeStruct(field.shape, F32), received, third, z_out,
    )


def solution(mesh):
    placed = (P(None, "gx", "gy"), P(None, None, None, "gx", "gy"), P("gy"), P())
    return jax.shard_map(
        shards, mesh=mesh, in_specs=placed, out_specs=P(None, "gx", "gy"), check_vma=False
    )
```

```python
import math

import jax
import jax.numpy as jnp
import ml_dtypes
import numpy as np
from jax import lax
from jax.experimental import pallas as pl
from jax.experimental.pallas import tpu as pltpu
from jax.sharding import PartitionSpec as P

NZ = 64
KY = 32
MIX = 8192
EARLY = 0
CONV = 12288
FULL = 60
CP = 40
LANES = 128
F32 = jnp.float32
BF16 = jnp.bfloat16


def split_table(table):
    high = table.astype(np.float32).astype(ml_dtypes.bfloat16)
    low = (table - high.astype(np.float64)).astype(np.float32).astype(ml_dtypes.bfloat16)
    return np.stack([high, low])


def split(values):
    high = values.astype(BF16)
    return high, (values - high.astype(F32)).astype(BF16)


def product(table, values, dims):
    high, low = split(values)
    numbers = (dims, ((), ()))

    def dot(left, right):
        return lax.dot_general(left, right, numbers, preferred_element_type=F32)

    return dot(table[0], high) + dot(table[0], low) + dot(table[1], high)


def frequencies(count, length):
    index = np.arange(count)
    return np.where(index < count // 2, index, length - count + index)


def tables(size_x, size_y, cells_x, cells_y, modes_x, modes_z):
    full_x, full_y = size_x * cells_x, size_y * cells_y
    scale_in = 1.0 / math.sqrt(full_x * full_y * NZ)
    scale_out = 1.0 / math.sqrt(modes_x * KY * modes_z)
    kx_local = modes_x // size_y
    z = np.arange(NZ)
    k = np.arange(modes_z)
    turn = 2.0 * np.pi * (np.outer(k, z) % NZ) / NZ
    eye_x = np.eye(cells_x)
    parts = np.stack([np.cos(turn), -np.sin(turn)], 1)
    z_in = np.einsum("kpz,xw->kpxwz", parts, eye_x).reshape(modes_z * 2 * cells_x, -1) * scale_in
    weight = np.where(k == 0, 1.0, 2.0)[:, None, None] * scale_out
    z_out = np.einsum("kpz,xw->kpxwz", parts * weight, eye_x).reshape(modes_z * 2 * cells_x, -1)

    def rotation(freq, positions, length):
        angle = 2.0 * np.pi * (np.outer(freq, positions) % length) / length
        cos, sin = np.cos(angle), np.sin(angle)
        return np.stack([np.stack([cos, -sin]), np.stack([sin, cos])])

    plus_x = rotation(frequencies(modes_x, full_x), np.arange(full_x), full_x)
    minus_x = plus_x.transpose(1, 0, 2, 3)
    x_in = minus_x.reshape(2, 2, modes_x, size_x, cells_x).transpose(2, 0, 3, 1, 4)
    x_in = x_in.reshape(modes_x * 2, -1)
    x_out = plus_x.reshape(2, 2, modes_x, size_x, cells_x).transpose(3, 0, 4, 2, 1)
    x_out = x_out.reshape(size_x * 2 * cells_x, -1)
    plus_y = rotation(frequencies(KY, full_y), np.arange(full_y), full_y)
    minus_y = plus_y.transpose(1, 0, 2, 3)
    eye_j = np.eye(kx_local)
    shape = (2, 2, KY, size_y, cells_y)
    y_in = np.einsum("pqlsy,jk->pjlyskq", minus_y.reshape(shape), eye_j)
    y_in = y_in.reshape(2 * kx_local * KY, -1)
    y_out = np.einsum("pqlsy,jk->ysjpqkl", plus_y.reshape(shape), eye_j)
    y_out = y_out.reshape(cells_y * size_y * kx_local * 2, -1)
    y_tables = np.concatenate(np.split(y_in, 2, axis=1) + [y_out], axis=0)
    return [split_table(t) for t in (z_in, x_in, y_tables, x_out, z_out)]


def call(body, out_shape, *args, scratch=(), flops=0, smem=(), hbm=(), out_hbm=(), vmem=24, light=False):
    def spec(index, kept):
        return pl.BlockSpec(memory_space=pl.ANY if index in kept else pltpu.VMEM)

    in_specs = [pl.BlockSpec(memory_space=pltpu.SMEM) if i in smem else spec(i, hbm) for i in range(len(args))]
    size = 0 if light else sum(a.size * a.dtype.itemsize for a in args)
    many = isinstance(out_shape, tuple)
    return pl.pallas_call(
        body,
        out_shape=out_shape,
        in_specs=in_specs,
        out_specs=tuple(spec(i, out_hbm) for i in range(len(out_shape))) if many else spec(0, out_hbm),
        scratch_shapes=list(scratch),
        compiler_params=pltpu.CompilerParams(vmem_limit_bytes=vmem << 20),
        cost_estimate=pl.CostEstimate(flops=flops, bytes_accessed=size, transcendentals=0),
    )(*args)


def copies(pairs, semaphores, first=0):
    started = [pltpu.make_async_copy(a, b, semaphores.at[first + i]) for i, (a, b) in enumerate(pairs)]
    for copy in started:
        copy.start()
    return started


def wait(started):
    for copy in started:
        copy.wait()


def store_payload(ref, rows):
    count = ref.shape[0]
    for tile in range(3):
        width = min(LANES, rows.shape[1] - LANES * tile)
        block = rows[:, LANES * tile : LANES * tile + width]
        ref[:, 8 * tile : 8 * tile + 8, :width] = block.reshape(count, 8, width)
        if width < LANES:
            ref[:, 8 * tile : 8 * tile + 8, width:] = jnp.zeros((count, 8, LANES - width), F32)


def load_payload(ref):
    count = ref.shape[0]
    tiles = [ref[:, 8 * t : 8 * t + 8, :].reshape(count * 8, LANES) for t in range(3)]
    return jnp.concatenate(tiles, axis=1)


def z_in_body(field_hbm, table_hbm, grid_ref, out_ref, field, table, sems):
    arrived = copies([(field_hbm, field), (table_hbm, table)], sems)
    wait(arrived[:1])
    channels, cells_x, width = field.shape
    for x in range(cells_x):
        piece = field[:, x, :]
        piece = jnp.concatenate([piece, jnp.zeros((CP - channels, width), F32)], axis=0)
        for y in range(width // NZ):
            grid_ref[y, :, NZ * x : NZ * x + NZ] = piece[:, NZ * y : NZ * y + NZ]
    cells = grid_ref[...].reshape(-1, grid_ref.shape[2])
    wait(arrived[1:])
    store_payload(out_ref, product(table, cells, ((1,), (1,))))


def rows_body(received, table, out_ref):
    rows = product(table, load_payload(received), ((1,), (0,)))
    for tile in range(3):
        block = rows[:, LANES * tile : LANES * tile + LANES]
        out_ref[:, 8 * tile : 8 * tile + 8, :] = block.reshape(out_ref.shape[0], 8, LANES)


def mix_body(received, weights, kept, place, y_tables, out_ref, stacked, s_re, s_im):
    cells_y = received.shape[0]
    rows = load_payload(received)
    block = rows.shape[0]
    for y in range(cells_y):
        stacked[y * block : (y + 1) * block, :CP] = rows[:, CP * y : CP * y + CP]
        stacked[y * block : (y + 1) * block, CP:] = jnp.zeros((block, LANES - CP), F32)
    size = y_tables.shape[2]
    modes = 0.0
    for half in range(2):
        span = slice(half * size, half * size + size)
        table = [y_tables[i, span] for i in range(2)]
        modes += product(table, stacked[span], ((1,), (0,)))
    count = modes.shape[0] // 2
    s_re[...] = modes[:count].T
    s_im[...] = modes[count:].T
    channels = 36
    pair = 2 * channels
    row = lax.broadcasted_iota(jnp.int32, (8, count), 0)

    def spread(ref, c):
        first = jnp.broadcast_to(ref[c : c + 1, :], (8, count))
        second = jnp.broadcast_to(ref[c + 1 : c + 2, :], (8, count))
        middle = jnp.where(row < 4, first, second)
        return jnp.concatenate([first] * 4 + [middle] + [second] * 4, axis=0)

    total_re = jnp.zeros((pair, count), F32)
    total_im = jnp.zeros((pair, count), F32)
    for c in range(0, channels, 2):
        w_re = weights[0, channels * c : channels * c + pair, :]
        w_im = weights[1, channels * c : channels * c + pair, :]
        f_re, f_im = spread(s_re, c), spread(s_im, c)
        total_re += w_re * f_re - w_im * f_im
        total_im += w_re * f_im + w_im * f_re
    keep = place[0] < kept[...]

    def fold(total):
        total = total[:channels] + total[channels:]
        return jnp.concatenate([jnp.where(keep, total, 0.0), jnp.zeros((CP - channels, count), F32)], axis=0)

    mixed = jnp.concatenate([fold(total_re), fold(total_im)], axis=1)
    table = [y_tables[i, 2 * size :] for i in range(2)]
    back = product(table, mixed, ((1,), (1,)))
    lanes = jnp.concatenate([back[y * block : (y + 1) * block] for y in range(cells_y)], axis=1)
    store_payload(out_ref, lanes)


def gelu_exact(values):
    return 0.5 * values * (1.0 + lax.erf(values * math.sqrt(0.5)))


ROW = 368


def taps_body(kernels, after, out_ref, scratch):
    channels = kernels.shape[2]
    for r in range(3):
        scratch[...] = jnp.zeros(scratch.shape, F32)
        for tap in range(27):
            row, lane = CP * (tap % 3), CP * (tap // 3)
            scratch[row : row + channels, lane : lane + channels] = kernels[r, tap]
        high, low = split(scratch[...].T[:ROW])
        out_ref[r, :ROW, :128] = high
        out_ref[r, :ROW, 128:] = high
        out_ref[r, ROW:, :128] = low
        out_ref[r, ROW:, 128:] = jnp.zeros((ROW, 128), BF16)


def convolve_rows(load_row, rows_in, width, taps, refs, finish):
    stack_a, stack_b, first_sum, second_sum, whole = refs
    z_position = lax.broadcasted_iota(jnp.int32, (CP, LANES), 1) % NZ
    has_lower = z_position >= 1
    has_upper = z_position <= NZ - 2
    low_half = lax.broadcasted_iota(jnp.int32, (CP, LANES), 1) < NZ
    tiles = width // LANES

    def prepare(index, stack):
        cells = load_row(index)
        for t in range(tiles):
            piece = cells[:, LANES * t : LANES * t + LANES]
            lower = jnp.where(has_lower, pltpu.roll(piece, 1, 1), 0.0)
            upper = jnp.where(has_upper, pltpu.roll(piece, LANES - 1, 1), 0.0)
            rows = jnp.concatenate([lower, piece, upper, jnp.zeros((8, LANES), F32)], axis=0)
            high, low = split(rows)
            stack[:128, LANES * t : LANES * t + LANES] = high
            stack[128:, LANES * t : LANES * t + LANES] = low

    def emit(row):
        sums = [[whole[CP * a : CP * a + CP, LANES * t : LANES * t + LANES] for t in range(tiles)] for a in range(3)]
        out = []
        for t in range(tiles):
            low_part = sums[0][t]
            if t + 1 < tiles:
                low_part = low_part + sums[2][t + 1]
            high_part = sums[2][t]
            if t > 0:
                high_part = high_part + sums[0][t - 1]
            turned = pltpu.roll(jnp.where(low_half, low_part, high_part), NZ, 1)
            out.append(sums[1][t] + turned)
        finish(row, out)

    def step(index, here, there):
        prepare(jnp.minimum(index + 1, rows_in - 1), there)
        emit(jnp.maximum(index - 3, 0))
        for t in range(tiles // 2):
            lanes = slice(2 * LANES * t, 2 * LANES * t + 2 * LANES)
            terms = lax.dot_general(
                taps[...], here[:, lanes], (((1,), (0,)), ((), ())), preferred_element_type=F32
            )
            for a in range(3):
                rows = slice(CP * a, CP * a + CP)
                piece = []
                for b in range(3):
                    first = CP * (3 * a + b)
                    piece.append(terms[first : first + CP] + terms[ROW + first : ROW + first + CP])
                whole[rows, lanes] = second_sum[rows, lanes] + piece[2]
                second_sum[rows, lanes] = first_sum[rows, lanes] + piece[1]
                first_sum[rows, lanes] = piece[0]

    def pair(j, carry):
        step(2 * j, stack_a, stack_b)
        step(2 * j + 1, stack_b, stack_a)
        return carry

    prepare(0, stack_a)
    lax.fori_loop(0, rows_in // 2, pair, 0)
    emit(rows_in - 3)


def conv_scratch(width):
    return [pltpu.VMEM((256, width), BF16)] * 2 + [pltpu.VMEM((3 * CP, width), F32)] * 3


def inside(place, first_x, sizes, width):
    cells_x, cells_y, full_x, full_y = sizes
    x = place[0] * cells_x + first_x + lax.broadcasted_iota(jnp.int32, (CP, width), 1) // NZ
    in_x = (x >= 0) & (x < full_x)

    def at(local_y):
        y = place[1] * cells_y + local_y
        return in_x & ((y >= 0) & (y < full_y))

    return at


def gather(sources, rows, target, first):
    width = sources[0].shape[2]
    count = rows.stop - rows.start
    return [
        (s.at[rows], target.at[slice(first, first + count), :, slice(width * i, width * i + width)])
        for i, s in enumerate(sources)
    ]


def join(sources, rows, target, first):
    width = sources[0].shape[2]
    count = rows.stop - rows.start
    for i, source in enumerate(sources):
        target[first : first + count, :, width * i : width * i + width] = source[rows]


def early_body(sizes, before, left, own, right, place, taps, out_ref, rows, *refs):
    count = own.shape[0]
    half = count // 2 + 1
    rows[0:3] = before[...]
    join((left, own, right), slice(0, half), rows, 3)
    keep = inside(place, -2, sizes, 512)

    def finish(row, tiles):
        values = jnp.concatenate(tiles[1:5], axis=1)
        out_ref[row] = jnp.where(keep(row - 2), gelu_exact(values), 0.0)

    convolve_rows(lambda i: rows[i], half + 3, 768, taps.at[0], refs, finish)


def later_body(sizes, early, left, own, right, after, place, taps, out_ref, *refs):
    rows, first, second = refs[:3]
    wide, narrow = refs[3:8], refs[8:]
    count = own.shape[0]
    half = count // 2 + 1
    join((left, own, right), slice(count - half, count), rows, 0)
    rows[half:] = after[...]
    base = early.shape[0]
    first[:base] = early[...]
    keep = inside(place, -2, sizes, 512)

    def finish_first(row, tiles):
        values = jnp.concatenate(tiles[1:5], axis=1)
        first[base + row] = jnp.where(keep(base + row - 2), gelu_exact(values), 0.0)

    def finish_second(row, tiles):
        values = jnp.concatenate(tiles, axis=1)
        second[row] = jnp.where(keep(row - 1), gelu_exact(values), 0.0)

    def finish_third(row, tiles):
        out_ref[row] = jnp.concatenate(tiles[1:3], axis=1)

    convolve_rows(lambda i: rows[i], half + 3, 768, taps.at[0], wide, finish_first)
    convolve_rows(lambda i: first[i], count + 4, 512, taps.at[1], narrow, finish_second)
    convolve_rows(lambda i: second[i], count + 2, 512, taps.at[2], narrow, finish_third)


def last_body(received, third, table, out_ref):
    spectrum = load_payload(received)[:, : third.shape[0] * CP]
    high, low = split(spectrum)

    def dot(left, right):
        return lax.dot_general(left, right, (((0,), (0,)), ((), ())), preferred_element_type=F32)

    spectral = dot(high, table[0]) + dot(low, table[0]) + dot(high, table[1])
    out = gelu_exact(spectral.reshape(third.shape) + third[...])
    channels, cells_x, width = out_ref.shape
    for x in range(cells_x):
        piece = [out[y, :channels, NZ * x : NZ * x + NZ] for y in range(width // NZ)]
        out_ref[:, x, :] = jnp.concatenate(piece, axis=1)


def shift(values, axis, step):
    count = lax.axis_size(axis)
    pairs = [(i, i + step) for i in range(count) if 0 <= i + step < count]
    return lax.ppermute(values, axis, pairs)


def shards(field, mix_weights, kept_z, conv_kernels):
    channels = field.shape[0]
    cells_x = field.shape[1]
    cells_y = field.shape[2] // NZ
    size_x = lax.axis_size("gx")
    size_y = lax.axis_size("gy")
    full_x, full_y = cells_x * size_x, cells_y * size_y
    modes_z = mix_weights.shape[3] * size_x
    kx_local = mix_weights.shape[4] // KY
    modes_x = kx_local * size_y
    place = jnp.stack([lax.axis_index("gx"), lax.axis_index("gy")]).astype(jnp.int32)
    z_in, x_in, y_tables, x_out, z_out = [
        jnp.asarray(t) for t in tables(size_x, size_y, cells_x, cells_y, modes_x, modes_z)
    ]

    sizes = (cells_x, cells_y, full_x, full_y)
    grid, sent = call(
        z_in_body,
        (
            jax.ShapeDtypeStruct((cells_y, CP, cells_x * NZ), F32),
            jax.ShapeDtypeStruct((size_x, 24, LANES), F32),
        ),
        field, z_in,
        scratch=[pltpu.VMEM(field.shape, F32), pltpu.VMEM(z_in.shape, BF16), pltpu.SemaphoreType.DMA((2,))],
        hbm=(0, 1), vmem=FULL,
    )
    left = shift(grid, "gx", 1)
    right = shift(grid, "gx", -1)
    behind, _ = lax.optimization_barrier((place, sent))
    taps = call(
        taps_body, jax.ShapeDtypeStruct((3, 2 * ROW, 256), BF16), conv_kernels, behind,
        scratch=[pltpu.VMEM((128, 384), F32)], smem=(1,),
    )
    received = lax.all_to_all(sent, "gx", 0, 0, tiled=True)
    received, taps = lax.optimization_barrier((received, taps))

    sent = call(rows_body, jax.ShapeDtypeStruct((size_y, 24, LANES), F32), received, x_in)

    left, right, _ = lax.optimization_barrier((left, right, sent))
    received = lax.all_to_all(sent, "gy", 0, 0, tiled=True)

    def edge(rows):
        return jnp.concatenate([left[rows], grid[rows], right[rows]], axis=2)

    before = shift(edge(slice(cells_y - 3, cells_y)), "gy", 1)
    after = shift(edge(slice(0, 3)), "gy", -1)
    weights = mix_weights.reshape(2, channels * channels, kx_local * KY)
    sent = call(
        mix_body,
        jax.ShapeDtypeStruct((size_y, 24, LANES), F32),
        received, weights, kept_z.reshape(1, -1), place, y_tables,
        scratch=[pltpu.VMEM((cells_y * size_y * kx_local * 2, LANES), F32)]
        + [pltpu.VMEM((LANES, kx_local * KY), F32)] * 2,
        smem=(3,), flops=MIX << 20,
    )
    before, _ = lax.optimization_barrier((before, sent))
    received = lax.all_to_all(sent, "gy", 0, 0, tiled=True)
    half = cells_y // 2 + 1
    early = call(
        lambda *refs: early_body(sizes, *refs),
        jax.ShapeDtypeStruct((half + 1, CP, 512), F32),
        before, left, grid, right, place, taps,
        scratch=[
            pltpu.VMEM((half + 3, CP, 768), F32),
        ]
        + conv_scratch(768),
        smem=(4,), flops=EARLY << 20,
    )
    early, received = lax.optimization_barrier((early, received))
    sent = call(rows_body, jax.ShapeDtypeStruct((size_x, 24, LANES), F32), received, x_out)
    early, after, _ = lax.optimization_barrier((early, after, sent))
    received = lax.all_to_all(sent, "gx", 0, 0, tiled=True)
    third = call(
        lambda *refs: later_body(sizes, *refs),
        jax.ShapeDtypeStruct((cells_y, CP, cells_x * NZ), F32),
        early, left, grid, right, after, place, taps,
        scratch=[
            pltpu.VMEM((half + 3, CP, 768), F32),
            pltpu.VMEM((cells_y + 4, CP, 512), F32),
            pltpu.VMEM((cells_y + 2, CP, 512), F32),
        ]
        + conv_scratch(768) + conv_scratch(512),
        smem=(5,), flops=CONV << 20,
    )
    return call(
        last_body, jax.ShapeDtypeStruct(field.shape, F32), received, third, z_out,
    )


def solution(mesh):
    placed = (P(None, "gx", "gy"), P(None, None, None, "gx", "gy"), P("gy"), P())
    return jax.shard_map(
        shards, mesh=mesh, in_specs=placed, out_specs=P(None, "gx", "gy"), check_vma=False
    )
```

```python
import math

import jax
import jax.numpy as jnp
import ml_dtypes
import numpy as np
from jax import lax
from jax.experimental import pallas as pl
from jax.experimental.pallas import tpu as pltpu
from jax.sharding import PartitionSpec as P

NZ = 64
KY = 32
MIX = 8192
XOUT = 8192
CONV = 12288
FULL = 60
CP = 40
LANES = 128
F32 = jnp.float32
BF16 = jnp.bfloat16


def split_table(table):
    high = table.astype(np.float32).astype(ml_dtypes.bfloat16)
    low = (table - high.astype(np.float64)).astype(np.float32).astype(ml_dtypes.bfloat16)
    return np.stack([high, low])


def split(values):
    high = values.astype(BF16)
    return high, (values - high.astype(F32)).astype(BF16)


def product(table, values, dims):
    high, low = split(values)
    numbers = (dims, ((), ()))

    def dot(left, right):
        return lax.dot_general(left, right, numbers, preferred_element_type=F32)

    return dot(table[0], high) + dot(table[0], low) + dot(table[1], high)


def frequencies(count, length):
    index = np.arange(count)
    return np.where(index < count // 2, index, length - count + index)


def tables(size_x, size_y, cells_x, cells_y, modes_x, modes_z):
    full_x, full_y = size_x * cells_x, size_y * cells_y
    scale_in = 1.0 / math.sqrt(full_x * full_y * NZ)
    scale_out = 1.0 / math.sqrt(modes_x * KY * modes_z)
    kx_local = modes_x // size_y
    z = np.arange(NZ)
    k = np.arange(modes_z)
    turn = 2.0 * np.pi * (np.outer(k, z) % NZ) / NZ
    eye_x = np.eye(cells_x)
    parts = np.stack([np.cos(turn), -np.sin(turn)], 1)
    z_in = np.einsum("kpz,xw->kpxwz", parts, eye_x).reshape(modes_z * 2 * cells_x, -1) * scale_in
    weight = np.where(k == 0, 1.0, 2.0)[:, None, None] * scale_out
    z_out = np.einsum("kpz,xw->kpxwz", parts * weight, eye_x).reshape(modes_z * 2 * cells_x, -1)

    def rotation(freq, positions, length):
        angle = 2.0 * np.pi * (np.outer(freq, positions) % length) / length
        cos, sin = np.cos(angle), np.sin(angle)
        return np.stack([np.stack([cos, -sin]), np.stack([sin, cos])])

    plus_x = rotation(frequencies(modes_x, full_x), np.arange(full_x), full_x)
    minus_x = plus_x.transpose(1, 0, 2, 3)
    x_in = minus_x.reshape(2, 2, modes_x, size_x, cells_x).transpose(2, 0, 3, 1, 4)
    x_in = x_in.reshape(modes_x * 2, -1)
    x_out = plus_x.reshape(2, 2, modes_x, size_x, cells_x).transpose(3, 0, 4, 2, 1)
    x_out = x_out.reshape(size_x * 2 * cells_x, -1)
    plus_y = rotation(frequencies(KY, full_y), np.arange(full_y), full_y)
    minus_y = plus_y.transpose(1, 0, 2, 3)
    eye_j = np.eye(kx_local)
    shape = (2, 2, KY, size_y, cells_y)
    y_in = np.einsum("pqlsy,jk->pjlyskq", minus_y.reshape(shape), eye_j)
    y_in = y_in.reshape(2 * kx_local * KY, -1)
    y_out = np.einsum("pqlsy,jk->ysjpqkl", plus_y.reshape(shape), eye_j)
    y_out = y_out.reshape(cells_y * size_y * kx_local * 2, -1)
    return [split_table(t) for t in (z_in, x_in, y_in, y_out, x_out, z_out)]


def call(body, out_shape, *args, scratch=(), flops=0, smem=(), hbm=(), out_hbm=(), vmem=24, light=False):
    def spec(index, kept):
        return pl.BlockSpec(memory_space=pl.ANY if index in kept else pltpu.VMEM)

    in_specs = [pl.BlockSpec(memory_space=pltpu.SMEM) if i in smem else spec(i, hbm) for i in range(len(args))]
    size = 0 if light else sum(a.size * a.dtype.itemsize for a in args)
    many = isinstance(out_shape, tuple)
    return pl.pallas_call(
        body,
        out_shape=out_shape,
        in_specs=in_specs,
        out_specs=tuple(spec(i, out_hbm) for i in range(len(out_shape))) if many else spec(0, out_hbm),
        scratch_shapes=list(scratch),
        compiler_params=pltpu.CompilerParams(vmem_limit_bytes=vmem << 20),
        cost_estimate=pl.CostEstimate(flops=flops, bytes_accessed=size, transcendentals=0),
    )(*args)


def copies(pairs, semaphores, first=0):
    started = [pltpu.make_async_copy(a, b, semaphores.at[first + i]) for i, (a, b) in enumerate(pairs)]
    for copy in started:
        copy.start()
    return started


def wait(started):
    for copy in started:
        copy.wait()


def store_payload(ref, rows):
    count = ref.shape[0]
    for tile in range(3):
        width = min(LANES, rows.shape[1] - LANES * tile)
        block = rows[:, LANES * tile : LANES * tile + width]
        ref[:, 8 * tile : 8 * tile + 8, :width] = block.reshape(count, 8, width)
        if width < LANES:
            ref[:, 8 * tile : 8 * tile + 8, width:] = jnp.zeros((count, 8, LANES - width), F32)


def load_payload(ref):
    count = ref.shape[0]
    tiles = [ref[:, 8 * t : 8 * t + 8, :].reshape(count * 8, LANES) for t in range(3)]
    return jnp.concatenate(tiles, axis=1)


def z_in_body(field_hbm, table_hbm, grid_ref, out_ref, field, table, sems):
    arrived = copies([(field_hbm, field), (table_hbm, table)], sems)
    wait(arrived[:1])
    channels, cells_x, width = field.shape
    for x in range(cells_x):
        piece = field[:, x, :]
        piece = jnp.concatenate([piece, jnp.zeros((CP - channels, width), F32)], axis=0)
        for y in range(width // NZ):
            grid_ref[y, :, NZ * x : NZ * x + NZ] = piece[:, NZ * y : NZ * y + NZ]
    cells = grid_ref[...].reshape(-1, grid_ref.shape[2])
    wait(arrived[1:])
    store_payload(out_ref, product(table, cells, ((1,), (1,))))


def rows_body(received, table, out_ref):
    rows = product(table, load_payload(received), ((1,), (0,)))
    for tile in range(3):
        block = rows[:, LANES * tile : LANES * tile + LANES]
        out_ref[:, 8 * tile : 8 * tile + 8, :] = block.reshape(out_ref.shape[0], 8, LANES)


def mix_body(received, weights, kept, place, y_in, y_out, out_ref, stacked, s_re, s_im):
    cells_y = received.shape[0]
    rows = load_payload(received)
    block = rows.shape[0]
    for y in range(cells_y):
        stacked[y * block : (y + 1) * block, :CP] = rows[:, CP * y : CP * y + CP]
        stacked[y * block : (y + 1) * block, CP:] = jnp.zeros((block, LANES - CP), F32)
    modes = product(y_in, stacked[...], ((1,), (0,)))
    count = modes.shape[0] // 2
    s_re[...] = modes[:count].T
    s_im[...] = modes[count:].T
    channels = 36
    pair = 2 * channels
    row = lax.broadcasted_iota(jnp.int32, (8, count), 0)

    def spread(ref, c):
        first = jnp.broadcast_to(ref[c : c + 1, :], (8, count))
        second = jnp.broadcast_to(ref[c + 1 : c + 2, :], (8, count))
        middle = jnp.where(row < 4, first, second)
        return jnp.concatenate([first] * 4 + [middle] + [second] * 4, axis=0)

    total_re = jnp.zeros((pair, count), F32)
    total_im = jnp.zeros((pair, count), F32)
    for c in range(0, channels, 2):
        w_re = weights[0, channels * c : channels * c + pair, :]
        w_im = weights[1, channels * c : channels * c + pair, :]
        f_re, f_im = spread(s_re, c), spread(s_im, c)
        total_re += w_re * f_re - w_im * f_im
        total_im += w_re * f_im + w_im * f_re
    keep = place[0] < kept[...]

    def fold(total):
        total = total[:channels] + total[channels:]
        return jnp.concatenate([jnp.where(keep, total, 0.0), jnp.zeros((CP - channels, count), F32)], axis=0)

    mixed = jnp.concatenate([fold(total_re), fold(total_im)], axis=1)
    back = product(y_out, mixed, ((1,), (1,)))
    lanes = jnp.concatenate([back[y * block : (y + 1) * block] for y in range(cells_y)], axis=1)
    store_payload(out_ref, lanes)


def gelu_exact(values):
    return 0.5 * values * (1.0 + lax.erf(values * math.sqrt(0.5)))


ROW = 368


def taps_body(kernels, after, out_ref, scratch):
    channels = kernels.shape[2]
    for r in range(3):
        scratch[...] = jnp.zeros(scratch.shape, F32)
        for tap in range(27):
            row, lane = CP * (tap % 3), CP * (tap // 3)
            scratch[row : row + channels, lane : lane + channels] = kernels[r, tap]
        high, low = split(scratch[...].T[:ROW])
        out_ref[r, :ROW, :128] = high
        out_ref[r, :ROW, 128:] = high
        out_ref[r, ROW:, :128] = low
        out_ref[r, ROW:, 128:] = jnp.zeros((ROW, 128), BF16)


def convolve_rows(load_row, rows_in, width, taps, refs, finish):
    stack_a, stack_b, first_sum, second_sum, whole = refs
    z_position = lax.broadcasted_iota(jnp.int32, (CP, LANES), 1) % NZ
    has_lower = z_position >= 1
    has_upper = z_position <= NZ - 2
    low_half = lax.broadcasted_iota(jnp.int32, (CP, LANES), 1) < NZ
    tiles = width // LANES

    def prepare(index, stack):
        cells = load_row(index)
        for t in range(tiles):
            piece = cells[:, LANES * t : LANES * t + LANES]
            lower = jnp.where(has_lower, pltpu.roll(piece, 1, 1), 0.0)
            upper = jnp.where(has_upper, pltpu.roll(piece, LANES - 1, 1), 0.0)
            rows = jnp.concatenate([lower, piece, upper, jnp.zeros((8, LANES), F32)], axis=0)
            high, low = split(rows)
            stack[:128, LANES * t : LANES * t + LANES] = high
            stack[128:, LANES * t : LANES * t + LANES] = low

    def emit(row):
        sums = [[whole[CP * a : CP * a + CP, LANES * t : LANES * t + LANES] for t in range(tiles)] for a in range(3)]
        out = []
        for t in range(tiles):
            low_part = sums[0][t]
            if t + 1 < tiles:
                low_part = low_part + sums[2][t + 1]
            high_part = sums[2][t]
            if t > 0:
                high_part = high_part + sums[0][t - 1]
            turned = pltpu.roll(jnp.where(low_half, low_part, high_part), NZ, 1)
            out.append(sums[1][t] + turned)
        finish(row, out)

    def step(index, here, there):
        prepare(jnp.minimum(index + 1, rows_in - 1), there)
        emit(jnp.maximum(index - 3, 0))
        for t in range(tiles // 2):
            lanes = slice(2 * LANES * t, 2 * LANES * t + 2 * LANES)
            terms = lax.dot_general(
                taps[...], here[:, lanes], (((1,), (0,)), ((), ())), preferred_element_type=F32
            )
            for a in range(3):
                rows = slice(CP * a, CP * a + CP)
                piece = []
                for b in range(3):
                    first = CP * (3 * a + b)
                    piece.append(terms[first : first + CP] + terms[ROW + first : ROW + first + CP])
                whole[rows, lanes] = second_sum[rows, lanes] + piece[2]
                second_sum[rows, lanes] = first_sum[rows, lanes] + piece[1]
                first_sum[rows, lanes] = piece[0]

    def pair(j, carry):
        step(2 * j, stack_a, stack_b)
        step(2 * j + 1, stack_b, stack_a)
        return carry

    prepare(0, stack_a)
    lax.fori_loop(0, rows_in // 2, pair, 0)
    emit(rows_in - 3)


def conv_scratch(width):
    return [pltpu.VMEM((256, width), BF16)] * 2 + [pltpu.VMEM((3 * CP, width), F32)] * 3


def inside(place, first_x, sizes, width):
    cells_x, cells_y, full_x, full_y = sizes
    x = place[0] * cells_x + first_x + lax.broadcasted_iota(jnp.int32, (CP, width), 1) // NZ
    in_x = (x >= 0) & (x < full_x)

    def at(local_y):
        y = place[1] * cells_y + local_y
        return in_x & ((y >= 0) & (y < full_y))

    return at


def gather(sources, rows, target, first):
    width = sources[0].shape[2]
    count = rows.stop - rows.start
    return [
        (s.at[rows], target.at[slice(first, first + count), :, slice(width * i, width * i + width)])
        for i, s in enumerate(sources)
    ]


def join(sources, rows, target, first):
    width = sources[0].shape[2]
    count = rows.stop - rows.start
    for i, source in enumerate(sources):
        target[first : first + count, :, width * i : width * i + width] = source[rows]


def convolutions_body(sizes, before, left, own, right, after, place, taps, out_ref, *refs):
    rows, first, second = refs[:3]
    wide, narrow = refs[3:8], refs[8:]
    count = own.shape[0]
    rows[0:3] = before[...]
    join((left, own, right), slice(0, count), rows, 3)
    rows[3 + count :] = after[...]
    keep = inside(place, -2, sizes, 512)

    def finish_first(row, tiles):
        values = jnp.concatenate(tiles[1:5], axis=1)
        first[row] = jnp.where(keep(row - 2), gelu_exact(values), 0.0)

    def finish_second(row, tiles):
        values = jnp.concatenate(tiles, axis=1)
        second[row] = jnp.where(keep(row - 1), gelu_exact(values), 0.0)

    def finish_third(row, tiles):
        out_ref[row] = jnp.concatenate(tiles[1:3], axis=1)

    convolve_rows(lambda i: rows[i], count + 6, 768, taps.at[0], wide, finish_first)
    convolve_rows(lambda i: first[i], count + 4, 512, taps.at[1], narrow, finish_second)
    convolve_rows(lambda i: second[i], count + 2, 512, taps.at[2], narrow, finish_third)


def last_body(received, third, table, out_ref):
    spectrum = load_payload(received)[:, : third.shape[0] * CP]
    high, low = split(spectrum)

    def dot(left, right):
        return lax.dot_general(left, right, (((0,), (0,)), ((), ())), preferred_element_type=F32)

    spectral = dot(high, table[0]) + dot(low, table[0]) + dot(high, table[1])
    out = gelu_exact(spectral.reshape(third.shape) + third[...])
    channels, cells_x, width = out_ref.shape
    for x in range(cells_x):
        piece = [out[y, :channels, NZ * x : NZ * x + NZ] for y in range(width // NZ)]
        out_ref[:, x, :] = jnp.concatenate(piece, axis=1)


def shift(values, axis, step):
    count = lax.axis_size(axis)
    pairs = [(i, i + step) for i in range(count) if 0 <= i + step < count]
    return lax.ppermute(values, axis, pairs)


def shards(field, mix_weights, kept_z, conv_kernels):
    channels = field.shape[0]
    cells_x = field.shape[1]
    cells_y = field.shape[2] // NZ
    size_x = lax.axis_size("gx")
    size_y = lax.axis_size("gy")
    full_x, full_y = cells_x * size_x, cells_y * size_y
    modes_z = mix_weights.shape[3] * size_x
    kx_local = mix_weights.shape[4] // KY
    modes_x = kx_local * size_y
    place = jnp.stack([lax.axis_index("gx"), lax.axis_index("gy")]).astype(jnp.int32)
    z_in, x_in, y_in, y_out, x_out, z_out = [
        jnp.asarray(t) for t in tables(size_x, size_y, cells_x, cells_y, modes_x, modes_z)
    ]

    sizes = (cells_x, cells_y, full_x, full_y)
    grid, sent = call(
        z_in_body,
        (
            jax.ShapeDtypeStruct((cells_y, CP, cells_x * NZ), F32),
            jax.ShapeDtypeStruct((size_x, 24, LANES), F32),
        ),
        field, z_in,
        scratch=[pltpu.VMEM(field.shape, F32), pltpu.VMEM(z_in.shape, BF16), pltpu.SemaphoreType.DMA((2,))],
        hbm=(0, 1), vmem=FULL,
    )
    left = shift(grid, "gx", 1)
    right = shift(grid, "gx", -1)
    behind, _ = lax.optimization_barrier((place, sent))
    taps = call(
        taps_body, jax.ShapeDtypeStruct((3, 2 * ROW, 256), BF16), conv_kernels, behind,
        scratch=[pltpu.VMEM((128, 384), F32)], smem=(1,),
    )
    received = lax.all_to_all(sent, "gx", 0, 0, tiled=True)
    received, taps = lax.optimization_barrier((received, taps))

    sent = call(rows_body, jax.ShapeDtypeStruct((size_y, 24, LANES), F32), received, x_in)

    left, right, _ = lax.optimization_barrier((left, right, sent))
    received = lax.all_to_all(sent, "gy", 0, 0, tiled=True)

    def edge(rows):
        return jnp.concatenate([left[rows], grid[rows], right[rows]], axis=2)

    before = shift(edge(slice(cells_y - 3, cells_y)), "gy", 1)
    weights = mix_weights.reshape(2, channels * channels, kx_local * KY)
    sent = call(
        mix_body,
        jax.ShapeDtypeStruct((size_y, 24, LANES), F32),
        received, weights, kept_z.reshape(1, -1), place, y_in, y_out,
        scratch=[pltpu.VMEM((cells_y * size_y * kx_local * 2, LANES), F32)]
        + [pltpu.VMEM((LANES, kx_local * KY), F32)] * 2,
        smem=(3,), flops=MIX << 20,
    )
    left, right, _ = lax.optimization_barrier((left, right, sent))
    after = shift(edge(slice(0, 3)), "gy", -1)
    received = lax.all_to_all(sent, "gy", 0, 0, tiled=True)
    sent = call(
        rows_body, jax.ShapeDtypeStruct((size_x, 24, LANES), F32), received, x_out, flops=XOUT << 20
    )
    before, after, _ = lax.optimization_barrier((before, after, sent))
    received = lax.all_to_all(sent, "gx", 0, 0, tiled=True)
    third = call(
        lambda *refs: convolutions_body(sizes, *refs),
        jax.ShapeDtypeStruct((cells_y, CP, cells_x * NZ), F32),
        before, left, grid, right, after, place, taps,
        scratch=[
            pltpu.VMEM((cells_y + 6, CP, 768), F32),
            pltpu.VMEM((cells_y + 4, CP, 512), F32),
            pltpu.VMEM((cells_y + 2, CP, 512), F32),
        ]
        + conv_scratch(768) + conv_scratch(512),
        smem=(5,), flops=CONV << 20,
    )
    return call(
        last_body, jax.ShapeDtypeStruct(field.shape, F32), received, third, z_out,
    )


def solution(mesh):
    placed = (P(None, "gx", "gy"), P(None, None, None, "gx", "gy"), P("gy"), P())
    return jax.shard_map(
        shards, mesh=mesh, in_specs=placed, out_specs=P(None, "gx", "gy"), check_vma=False
    )
```

```python
import math

import jax
import jax.numpy as jnp
import ml_dtypes
import numpy as np
from jax import lax
from jax.experimental import pallas as pl
from jax.experimental.pallas import tpu as pltpu
from jax.sharding import PartitionSpec as P

NZ = 64
KY = 32
MIX = 8192
XOUT = 8192
CONV = 12288
FULL = 60
CP = 40
LANES = 128
F32 = jnp.float32
BF16 = jnp.bfloat16


def split_table(table):
    high = table.astype(np.float32).astype(ml_dtypes.bfloat16)
    low = (table - high.astype(np.float64)).astype(np.float32).astype(ml_dtypes.bfloat16)
    return np.stack([high, low])


def split(values):
    high = values.astype(BF16)
    return high, (values - high.astype(F32)).astype(BF16)


def product(table, values, dims):
    high, low = split(values)
    numbers = (dims, ((), ()))

    def dot(left, right):
        return lax.dot_general(left, right, numbers, preferred_element_type=F32)

    return dot(table[0], high) + dot(table[0], low) + dot(table[1], high)


def frequencies(count, length):
    index = np.arange(count)
    return np.where(index < count // 2, index, length - count + index)


def tables(size_x, size_y, cells_x, cells_y, modes_x, modes_z):
    full_x, full_y = size_x * cells_x, size_y * cells_y
    scale_in = 1.0 / math.sqrt(full_x * full_y * NZ)
    scale_out = 1.0 / math.sqrt(modes_x * KY * modes_z)
    kx_local = modes_x // size_y
    z = np.arange(NZ)
    k = np.arange(modes_z)
    turn = 2.0 * np.pi * (np.outer(k, z) % NZ) / NZ
    eye_x = np.eye(cells_x)
    parts = np.stack([np.cos(turn), -np.sin(turn)], 1)
    z_in = np.einsum("kpz,xw->kpxwz", parts, eye_x).reshape(modes_z * 2 * cells_x, -1) * scale_in
    weight = np.where(k == 0, 1.0, 2.0)[:, None, None] * scale_out
    z_out = np.einsum("kpz,xw->kpxwz", parts * weight, eye_x).reshape(modes_z * 2 * cells_x, -1)

    def rotation(freq, positions, length):
        angle = 2.0 * np.pi * (np.outer(freq, positions) % length) / length
        cos, sin = np.cos(angle), np.sin(angle)
        return np.stack([np.stack([cos, -sin]), np.stack([sin, cos])])

    plus_x = rotation(frequencies(modes_x, full_x), np.arange(full_x), full_x)
    minus_x = plus_x.transpose(1, 0, 2, 3)
    x_in = minus_x.reshape(2, 2, modes_x, size_x, cells_x).transpose(2, 0, 3, 1, 4)
    x_in = x_in.reshape(modes_x * 2, -1)
    x_out = plus_x.reshape(2, 2, modes_x, size_x, cells_x).transpose(3, 0, 4, 2, 1)
    x_out = x_out.reshape(size_x * 2 * cells_x, -1)
    plus_y = rotation(frequencies(KY, full_y), np.arange(full_y), full_y)
    minus_y = plus_y.transpose(1, 0, 2, 3)
    eye_j = np.eye(kx_local)
    shape = (2, 2, KY, size_y, cells_y)
    y_in = np.einsum("pqlsy,jk->pjlyskq", minus_y.reshape(shape), eye_j)
    y_in = y_in.reshape(2 * kx_local * KY, -1)
    y_out = np.einsum("pqlsy,jk->ysjpqkl", plus_y.reshape(shape), eye_j)
    y_out = y_out.reshape(cells_y * size_y * kx_local * 2, -1)
    return [split_table(t) for t in (z_in, x_in, y_in, y_out, x_out, z_out)]


def call(body, out_shape, *args, scratch=(), flops=0, smem=(), hbm=(), out_hbm=(), vmem=24, light=False):
    def spec(index, kept):
        return pl.BlockSpec(memory_space=pl.ANY if index in kept else pltpu.VMEM)

    in_specs = [pl.BlockSpec(memory_space=pltpu.SMEM) if i in smem else spec(i, hbm) for i in range(len(args))]
    size = 0 if light else sum(a.size * a.dtype.itemsize for a in args)
    many = isinstance(out_shape, tuple)
    return pl.pallas_call(
        body,
        out_shape=out_shape,
        in_specs=in_specs,
        out_specs=tuple(spec(i, out_hbm) for i in range(len(out_shape))) if many else spec(0, out_hbm),
        scratch_shapes=list(scratch),
        compiler_params=pltpu.CompilerParams(vmem_limit_bytes=vmem << 20),
        cost_estimate=pl.CostEstimate(flops=flops, bytes_accessed=size, transcendentals=0),
    )(*args)


def copies(pairs, semaphores, first=0):
    started = [pltpu.make_async_copy(a, b, semaphores.at[first + i]) for i, (a, b) in enumerate(pairs)]
    for copy in started:
        copy.start()
    return started


def wait(started):
    for copy in started:
        copy.wait()


def store_payload(ref, rows):
    count = ref.shape[0]
    for tile in range(3):
        width = min(LANES, rows.shape[1] - LANES * tile)
        block = rows[:, LANES * tile : LANES * tile + width]
        ref[:, 8 * tile : 8 * tile + 8, :width] = block.reshape(count, 8, width)
        if width < LANES:
            ref[:, 8 * tile : 8 * tile + 8, width:] = jnp.zeros((count, 8, LANES - width), F32)


def load_payload(ref):
    count = ref.shape[0]
    tiles = [ref[:, 8 * t : 8 * t + 8, :].reshape(count * 8, LANES) for t in range(3)]
    return jnp.concatenate(tiles, axis=1)


def z_in_body(field_hbm, table_hbm, grid_ref, out_ref, field, table, sems):
    arrived = copies([(field_hbm, field), (table_hbm, table)], sems)
    wait(arrived[:1])
    channels, cells_x, width = field.shape
    for x in range(cells_x):
        piece = field[:, x, :]
        piece = jnp.concatenate([piece, jnp.zeros((CP - channels, width), F32)], axis=0)
        for y in range(width // NZ):
            grid_ref[y, :, NZ * x : NZ * x + NZ] = piece[:, NZ * y : NZ * y + NZ]
    cells = grid_ref[...].reshape(-1, grid_ref.shape[2])
    wait(arrived[1:])
    store_payload(out_ref, product(table, cells, ((1,), (1,))))


def rows_body(received, table, out_ref):
    rows = product(table, load_payload(received), ((1,), (0,)))
    for tile in range(3):
        block = rows[:, LANES * tile : LANES * tile + LANES]
        out_ref[:, 8 * tile : 8 * tile + 8, :] = block.reshape(out_ref.shape[0], 8, LANES)


def mix_body(received, weights, kept, place, y_in, y_out, out_ref, stacked, s_re, s_im):
    cells_y = received.shape[0]
    rows = load_payload(received)
    block = rows.shape[0]
    for y in range(cells_y):
        stacked[y * block : (y + 1) * block, :CP] = rows[:, CP * y : CP * y + CP]
        stacked[y * block : (y + 1) * block, CP:] = jnp.zeros((block, LANES - CP), F32)
    modes = product(y_in, stacked[...], ((1,), (0,)))
    count = modes.shape[0] // 2
    s_re[...] = modes[:count].T
    s_im[...] = modes[count:].T
    channels = 36
    pair = 2 * channels
    row = lax.broadcasted_iota(jnp.int32, (8, count), 0)

    def spread(ref, c):
        first = jnp.broadcast_to(ref[c : c + 1, :], (8, count))
        second = jnp.broadcast_to(ref[c + 1 : c + 2, :], (8, count))
        middle = jnp.where(row < 4, first, second)
        return jnp.concatenate([first] * 4 + [middle] + [second] * 4, axis=0)

    total_re = jnp.zeros((pair, count), F32)
    total_im = jnp.zeros((pair, count), F32)
    for c in range(0, channels, 2):
        w_re = weights[0, channels * c : channels * c + pair, :]
        w_im = weights[1, channels * c : channels * c + pair, :]
        f_re, f_im = spread(s_re, c), spread(s_im, c)
        total_re += w_re * f_re - w_im * f_im
        total_im += w_re * f_im + w_im * f_re
    keep = place[0] < kept[...]

    def fold(total):
        total = total[:channels] + total[channels:]
        return jnp.concatenate([jnp.where(keep, total, 0.0), jnp.zeros((CP - channels, count), F32)], axis=0)

    mixed = jnp.concatenate([fold(total_re), fold(total_im)], axis=1)
    back = product(y_out, mixed, ((1,), (1,)))
    lanes = jnp.concatenate([back[y * block : (y + 1) * block] for y in range(cells_y)], axis=1)
    store_payload(out_ref, lanes)


def gelu_exact(values):
    return 0.5 * values * (1.0 + lax.erf(values * math.sqrt(0.5)))


BLOCK = 112
ROW = 3 * BLOCK


def taps_body(kernels, after, out_ref, scratch):
    channels = kernels.shape[2]
    for r in range(3):
        scratch[...] = jnp.zeros(scratch.shape, F32)
        for tap in range(27):
            shift_x, shift_y, shift_z = tap // 9, tap // 3 % 3, tap % 3
            row, lane = CP * shift_z, BLOCK * shift_y + channels * shift_x
            scratch[row : row + channels, lane : lane + channels] = kernels[r, tap]
        high, low = split(scratch[...].T[:ROW])
        out_ref[r, :ROW, :128] = high
        out_ref[r, :ROW, 128:] = high
        out_ref[r, ROW:, :128] = low
        out_ref[r, ROW:, 128:] = jnp.zeros((ROW, 128), BF16)


def convolve_rows(load_row, rows_in, width, taps, refs, finish):
    stack_a, stack_b, first_sum, second_sum, whole = refs
    z_position = lax.broadcasted_iota(jnp.int32, (CP, LANES), 1) % NZ
    has_lower = z_position >= 1
    has_upper = z_position <= NZ - 2
    low_half = lax.broadcasted_iota(jnp.int32, (CP, LANES), 1) < NZ
    tiles = width // LANES

    def prepare(index, stack):
        cells = load_row(index)
        for t in range(tiles):
            piece = cells[:, LANES * t : LANES * t + LANES]
            lower = jnp.where(has_lower, pltpu.roll(piece, 1, 1), 0.0)
            upper = jnp.where(has_upper, pltpu.roll(piece, LANES - 1, 1), 0.0)
            rows = jnp.concatenate([lower, piece, upper, jnp.zeros((8, LANES), F32)], axis=0)
            high, low = split(rows)
            stack[:128, LANES * t : LANES * t + LANES] = high
            stack[128:, LANES * t : LANES * t + LANES] = low

    def emit(row):
        sums = [[whole[36 * a : 36 * a + CP, LANES * t : LANES * t + LANES] for t in range(tiles)] for a in range(3)]
        out = []
        for t in range(tiles):
            low_part = sums[0][t]
            if t + 1 < tiles:
                low_part = low_part + sums[2][t + 1]
            high_part = sums[2][t]
            if t > 0:
                high_part = high_part + sums[0][t - 1]
            turned = pltpu.roll(jnp.where(low_half, low_part, high_part), NZ, 1)
            out.append(sums[1][t] + turned)
        finish(row, out)

    def step(index, here, there):
        prepare(jnp.minimum(index + 1, rows_in - 1), there)
        emit(jnp.maximum(index - 3, 0))
        for t in range(tiles // 2):
            lanes = slice(2 * LANES * t, 2 * LANES * t + 2 * LANES)
            terms = lax.dot_general(
                taps[...], here[:, lanes], (((1,), (0,)), ((), ())), preferred_element_type=F32
            )
            piece = []
            for b in range(3):
                high = terms[BLOCK * b : BLOCK * b + BLOCK]
                piece.append(high + terms[ROW + BLOCK * b : ROW + BLOCK * b + BLOCK])
            whole[:, lanes] = second_sum[:, lanes] + piece[2]
            second_sum[:, lanes] = first_sum[:, lanes] + piece[1]
            first_sum[:, lanes] = piece[0]

    def pair(j, carry):
        step(2 * j, stack_a, stack_b)
        step(2 * j + 1, stack_b, stack_a)
        return carry

    prepare(0, stack_a)
    lax.fori_loop(0, rows_in // 2, pair, 0)
    emit(rows_in - 3)


def conv_scratch(width):
    return [pltpu.VMEM((256, width), BF16)] * 2 + [pltpu.VMEM((BLOCK, width), F32)] * 3


def inside(place, first_x, sizes, width):
    cells_x, cells_y, full_x, full_y = sizes
    x = place[0] * cells_x + first_x + lax.broadcasted_iota(jnp.int32, (CP, width), 1) // NZ
    in_x = (x >= 0) & (x < full_x)

    def at(local_y):
        y = place[1] * cells_y + local_y
        return in_x & ((y >= 0) & (y < full_y))

    return at


def gather(sources, rows, target, first):
    width = sources[0].shape[2]
    count = rows.stop - rows.start
    return [
        (s.at[rows], target.at[slice(first, first + count), :, slice(width * i, width * i + width)])
        for i, s in enumerate(sources)
    ]


def join(sources, rows, target, first):
    width = sources[0].shape[2]
    count = rows.stop - rows.start
    for i, source in enumerate(sources):
        target[first : first + count, :, width * i : width * i + width] = source[rows]


def convolutions_body(sizes, before, left, own, right, after, place, taps, out_ref, *refs):
    rows, first, second = refs[:3]
    wide, narrow = refs[3:8], refs[8:]
    count = own.shape[0]
    rows[0:3] = before[...]
    join((left, own, right), slice(0, count), rows, 3)
    rows[3 + count :] = after[...]
    keep = inside(place, -2, sizes, 512)

    def finish_first(row, tiles):
        values = jnp.concatenate(tiles[1:5], axis=1)
        first[row] = jnp.where(keep(row - 2), gelu_exact(values), 0.0)

    def finish_second(row, tiles):
        values = jnp.concatenate(tiles, axis=1)
        second[row] = jnp.where(keep(row - 1), gelu_exact(values), 0.0)

    def finish_third(row, tiles):
        out_ref[row] = jnp.concatenate(tiles[1:3], axis=1)

    convolve_rows(lambda i: rows[i], count + 6, 768, taps.at[0], wide, finish_first)
    convolve_rows(lambda i: first[i], count + 4, 512, taps.at[1], narrow, finish_second)
    convolve_rows(lambda i: second[i], count + 2, 512, taps.at[2], narrow, finish_third)


def last_body(received, third, table, out_ref):
    spectrum = load_payload(received)[:, : third.shape[0] * CP]
    high, low = split(spectrum)

    def dot(left, right):
        return lax.dot_general(left, right, (((0,), (0,)), ((), ())), preferred_element_type=F32)

    spectral = dot(high, table[0]) + dot(low, table[0]) + dot(high, table[1])
    out = gelu_exact(spectral.reshape(third.shape) + third[...])
    channels, cells_x, width = out_ref.shape
    for x in range(cells_x):
        piece = [out[y, :channels, NZ * x : NZ * x + NZ] for y in range(width // NZ)]
        out_ref[:, x, :] = jnp.concatenate(piece, axis=1)


def shift(values, axis, step):
    count = lax.axis_size(axis)
    pairs = [(i, i + step) for i in range(count) if 0 <= i + step < count]
    return lax.ppermute(values, axis, pairs)


def shards(field, mix_weights, kept_z, conv_kernels):
    channels = field.shape[0]
    cells_x = field.shape[1]
    cells_y = field.shape[2] // NZ
    size_x = lax.axis_size("gx")
    size_y = lax.axis_size("gy")
    full_x, full_y = cells_x * size_x, cells_y * size_y
    modes_z = mix_weights.shape[3] * size_x
    kx_local = mix_weights.shape[4] // KY
    modes_x = kx_local * size_y
    place = jnp.stack([lax.axis_index("gx"), lax.axis_index("gy")]).astype(jnp.int32)
    z_in, x_in, y_in, y_out, x_out, z_out = [
        jnp.asarray(t) for t in tables(size_x, size_y, cells_x, cells_y, modes_x, modes_z)
    ]

    sizes = (cells_x, cells_y, full_x, full_y)
    grid, sent = call(
        z_in_body,
        (
            jax.ShapeDtypeStruct((cells_y, CP, cells_x * NZ), F32),
            jax.ShapeDtypeStruct((size_x, 24, LANES), F32),
        ),
        field, z_in,
        scratch=[pltpu.VMEM(field.shape, F32), pltpu.VMEM(z_in.shape, BF16), pltpu.SemaphoreType.DMA((2,))],
        hbm=(0, 1), vmem=FULL,
    )
    left = shift(grid, "gx", 1)
    right = shift(grid, "gx", -1)
    behind, _ = lax.optimization_barrier((place, sent))
    taps = call(
        taps_body, jax.ShapeDtypeStruct((3, 2 * ROW, 256), BF16), conv_kernels, behind,
        scratch=[pltpu.VMEM((128, 384), F32)], smem=(1,),
    )
    received = lax.all_to_all(sent, "gx", 0, 0, tiled=True)
    received, taps = lax.optimization_barrier((received, taps))

    sent = call(rows_body, jax.ShapeDtypeStruct((size_y, 24, LANES), F32), received, x_in)

    left, right, _ = lax.optimization_barrier((left, right, sent))
    received = lax.all_to_all(sent, "gy", 0, 0, tiled=True)

    def edge(rows):
        return jnp.concatenate([left[rows], grid[rows], right[rows]], axis=2)

    before = shift(edge(slice(cells_y - 3, cells_y)), "gy", 1)
    weights = mix_weights.reshape(2, channels * channels, kx_local * KY)
    sent = call(
        mix_body,
        jax.ShapeDtypeStruct((size_y, 24, LANES), F32),
        received, weights, kept_z.reshape(1, -1), place, y_in, y_out,
        scratch=[pltpu.VMEM((cells_y * size_y * kx_local * 2, LANES), F32)]
        + [pltpu.VMEM((LANES, kx_local * KY), F32)] * 2,
        smem=(3,), flops=MIX << 20,
    )
    left, right, _ = lax.optimization_barrier((left, right, sent))
    after = shift(edge(slice(0, 3)), "gy", -1)
    received = lax.all_to_all(sent, "gy", 0, 0, tiled=True)
    sent = call(
        rows_body, jax.ShapeDtypeStruct((size_x, 24, LANES), F32), received, x_out, flops=XOUT << 20
    )
    before, after, _ = lax.optimization_barrier((before, after, sent))
    received = lax.all_to_all(sent, "gx", 0, 0, tiled=True)
    third = call(
        lambda *refs: convolutions_body(sizes, *refs),
        jax.ShapeDtypeStruct((cells_y, CP, cells_x * NZ), F32),
        before, left, grid, right, after, place, taps,
        scratch=[
            pltpu.VMEM((cells_y + 6, CP, 768), F32),
            pltpu.VMEM((cells_y + 4, CP, 512), F32),
            pltpu.VMEM((cells_y + 2, CP, 512), F32),
        ]
        + conv_scratch(768) + conv_scratch(512),
        smem=(5,), flops=CONV << 20,
    )
    return call(
        last_body, jax.ShapeDtypeStruct(field.shape, F32), received, third, z_out,
    )


def solution(mesh):
    placed = (P(None, "gx", "gy"), P(None, None, None, "gx", "gy"), P("gy"), P())
    return jax.shard_map(
        shards, mesh=mesh, in_specs=placed, out_specs=P(None, "gx", "gy"), check_vma=False
    )
```

```python
import math

import jax
import jax.numpy as jnp
import ml_dtypes
import numpy as np
from jax import lax
from jax.experimental import pallas as pl
from jax.experimental.pallas import tpu as pltpu
from jax.sharding import PartitionSpec as P

NZ = 64
KY = 32
MIX = 8192
XOUT = 8192
CONV = 12288
FULL = 60
CP = 40
LANES = 128
F32 = jnp.float32
BF16 = jnp.bfloat16


def split_table(table):
    high = table.astype(np.float32).astype(ml_dtypes.bfloat16)
    low = (table - high.astype(np.float64)).astype(np.float32).astype(ml_dtypes.bfloat16)
    return np.stack([high, low])


def split(values):
    high = values.astype(BF16)
    return high, (values - high.astype(F32)).astype(BF16)


def product(table, values, dims):
    high, low = split(values)
    numbers = (dims, ((), ()))

    def dot(left, right):
        return lax.dot_general(left, right, numbers, preferred_element_type=F32)

    return dot(table[0], high) + dot(table[0], low) + dot(table[1], high)


def frequencies(count, length):
    index = np.arange(count)
    return np.where(index < count // 2, index, length - count + index)


def tables(size_x, size_y, cells_x, cells_y, modes_x, modes_z):
    full_x, full_y = size_x * cells_x, size_y * cells_y
    scale_in = 1.0 / math.sqrt(full_x * full_y * NZ)
    scale_out = 1.0 / math.sqrt(modes_x * KY * modes_z)
    kx_local = modes_x // size_y
    z = np.arange(NZ)
    k = np.arange(modes_z)
    turn = 2.0 * np.pi * (np.outer(k, z) % NZ) / NZ
    eye_x = np.eye(cells_x)
    parts = np.stack([np.cos(turn), -np.sin(turn)], 1)
    z_in = np.einsum("kpz,xw->kpxwz", parts, eye_x).reshape(modes_z * 2 * cells_x, -1) * scale_in
    weight = np.where(k == 0, 1.0, 2.0)[:, None, None] * scale_out
    z_out = np.einsum("kpz,xw->kpxwz", parts * weight, eye_x).reshape(modes_z * 2 * cells_x, -1)

    def rotation(freq, positions, length):
        angle = 2.0 * np.pi * (np.outer(freq, positions) % length) / length
        cos, sin = np.cos(angle), np.sin(angle)
        return np.stack([np.stack([cos, -sin]), np.stack([sin, cos])])

    plus_x = rotation(frequencies(modes_x, full_x), np.arange(full_x), full_x)
    minus_x = plus_x.transpose(1, 0, 2, 3)
    x_in = minus_x.reshape(2, 2, modes_x, size_x, cells_x).transpose(2, 0, 3, 1, 4)
    x_in = x_in.reshape(modes_x * 2, -1)
    x_out = plus_x.reshape(2, 2, modes_x, size_x, cells_x).transpose(3, 0, 4, 2, 1)
    x_out = x_out.reshape(size_x * 2 * cells_x, -1)
    plus_y = rotation(frequencies(KY, full_y), np.arange(full_y), full_y)
    minus_y = plus_y.transpose(1, 0, 2, 3)
    eye_j = np.eye(kx_local)
    shape = (2, 2, KY, size_y, cells_y)
    y_in = np.einsum("pqlsy,jk->pjlyskq", minus_y.reshape(shape), eye_j)
    y_in = y_in.reshape(2 * kx_local * KY, -1)
    y_out = np.einsum("pqlsy,jk->ysjpqkl", plus_y.reshape(shape), eye_j)
    y_out = y_out.reshape(cells_y * size_y * kx_local * 2, -1)
    return [split_table(t) for t in (z_in, x_in, y_in, y_out, x_out, z_out)]


def call(body, out_shape, *args, scratch=(), flops=0, smem=(), hbm=(), out_hbm=(), vmem=24, light=False):
    def spec(index, kept):
        return pl.BlockSpec(memory_space=pl.ANY if index in kept else pltpu.VMEM)

    in_specs = [pl.BlockSpec(memory_space=pltpu.SMEM) if i in smem else spec(i, hbm) for i in range(len(args))]
    size = 0 if light else sum(a.size * a.dtype.itemsize for a in args)
    many = isinstance(out_shape, tuple)
    return pl.pallas_call(
        body,
        out_shape=out_shape,
        in_specs=in_specs,
        out_specs=tuple(spec(i, out_hbm) for i in range(len(out_shape))) if many else spec(0, out_hbm),
        scratch_shapes=list(scratch),
        compiler_params=pltpu.CompilerParams(vmem_limit_bytes=vmem << 20),
        cost_estimate=pl.CostEstimate(flops=flops, bytes_accessed=size, transcendentals=0),
    )(*args)


def copies(pairs, semaphores, first=0):
    started = [pltpu.make_async_copy(a, b, semaphores.at[first + i]) for i, (a, b) in enumerate(pairs)]
    for copy in started:
        copy.start()
    return started


def wait(started):
    for copy in started:
        copy.wait()


def store_payload(ref, rows):
    count = ref.shape[0]
    for tile in range(3):
        width = min(LANES, rows.shape[1] - LANES * tile)
        block = rows[:, LANES * tile : LANES * tile + width]
        ref[:, 8 * tile : 8 * tile + 8, :width] = block.reshape(count, 8, width)
        if width < LANES:
            ref[:, 8 * tile : 8 * tile + 8, width:] = jnp.zeros((count, 8, LANES - width), F32)


def load_payload(ref):
    count = ref.shape[0]
    tiles = [ref[:, 8 * t : 8 * t + 8, :].reshape(count * 8, LANES) for t in range(3)]
    return jnp.concatenate(tiles, axis=1)


def z_in_body(field_hbm, table_hbm, grid_ref, out_ref, field, table, sems):
    arrived = copies([(field_hbm, field), (table_hbm, table)], sems)
    wait(arrived[:1])
    channels, cells_x, width = field.shape
    for x in range(cells_x):
        piece = field[:, x, :]
        piece = jnp.concatenate([piece, jnp.zeros((CP - channels, width), F32)], axis=0)
        for y in range(width // NZ):
            grid_ref[y, :, NZ * x : NZ * x + NZ] = piece[:, NZ * y : NZ * y + NZ]
    cells = grid_ref[...].reshape(-1, grid_ref.shape[2])
    wait(arrived[1:])
    store_payload(out_ref, product(table, cells, ((1,), (1,))))


def rows_body(received, table, out_ref):
    rows = product(table, load_payload(received), ((1,), (0,)))
    for tile in range(3):
        block = rows[:, LANES * tile : LANES * tile + LANES]
        out_ref[:, 8 * tile : 8 * tile + 8, :] = block.reshape(out_ref.shape[0], 8, LANES)


def mix_body(received_hbm, weights_hbm, kept, place, y_in_hbm, y_out_hbm, out_ref, stacked, s_re, s_im, *refs):
    received, weights, y_in, y_out, sems = refs
    arrived = copies(
        [(received_hbm, received)]
        + [(y_in_hbm.at[i], y_in.at[i]) for i in range(2)]
        + [(weights_hbm.at[i], weights.at[i]) for i in range(2)]
        + [(y_out_hbm.at[i], y_out.at[i]) for i in range(2)],
        sems,
    )
    wait(arrived[:1])
    cells_y = received.shape[0]
    rows = load_payload(received)
    block = rows.shape[0]
    for y in range(cells_y):
        stacked[y * block : (y + 1) * block, :CP] = rows[:, CP * y : CP * y + CP]
        stacked[y * block : (y + 1) * block, CP:] = jnp.zeros((block, LANES - CP), F32)
    wait(arrived[1:3])
    modes = product(y_in, stacked[...], ((1,), (0,)))
    count = modes.shape[0] // 2
    s_re[...] = modes[:count].T
    s_im[...] = modes[count:].T
    channels = 36
    pair = 2 * channels
    row = lax.broadcasted_iota(jnp.int32, (8, count), 0)

    def spread(ref, c):
        first = jnp.broadcast_to(ref[c : c + 1, :], (8, count))
        second = jnp.broadcast_to(ref[c + 1 : c + 2, :], (8, count))
        middle = jnp.where(row < 4, first, second)
        return jnp.concatenate([first] * 4 + [middle] + [second] * 4, axis=0)

    wait(arrived[3:5])
    total_re = jnp.zeros((pair, count), F32)
    total_im = jnp.zeros((pair, count), F32)
    for c in range(0, channels, 2):
        w_re = weights[0, channels * c : channels * c + pair, :]
        w_im = weights[1, channels * c : channels * c + pair, :]
        f_re, f_im = spread(s_re, c), spread(s_im, c)
        total_re += w_re * f_re - w_im * f_im
        total_im += w_re * f_im + w_im * f_re
    keep = place[0] < kept[...]

    def fold(total):
        total = total[:channels] + total[channels:]
        return jnp.concatenate([jnp.where(keep, total, 0.0), jnp.zeros((CP - channels, count), F32)], axis=0)

    mixed = jnp.concatenate([fold(total_re), fold(total_im)], axis=1)
    wait(arrived[5:])
    back = product(y_out, mixed, ((1,), (1,)))
    lanes = jnp.concatenate([back[y * block : (y + 1) * block] for y in range(cells_y)], axis=1)
    store_payload(out_ref, lanes)


def gelu_exact(values):
    return 0.5 * values * (1.0 + lax.erf(values * math.sqrt(0.5)))


BLOCK = 112
ROW = 3 * BLOCK


def taps_body(kernels, after, out_ref, scratch):
    channels = kernels.shape[2]
    for r in range(3):
        scratch[...] = jnp.zeros(scratch.shape, F32)
        for tap in range(27):
            shift_x, shift_y, shift_z = tap // 9, tap // 3 % 3, tap % 3
            row, lane = CP * shift_z, BLOCK * shift_y + channels * shift_x
            scratch[row : row + channels, lane : lane + channels] = kernels[r, tap]
        high, low = split(scratch[...].T[:ROW])
        out_ref[r, :ROW, :128] = high
        out_ref[r, :ROW, 128:] = high
        out_ref[r, ROW:, :128] = low
        out_ref[r, ROW:, 128:] = jnp.zeros((ROW, 128), BF16)


def convolve_rows(load_row, rows_in, width, taps, refs, finish):
    stack_a, stack_b, first_sum, second_sum, whole = refs
    z_position = lax.broadcasted_iota(jnp.int32, (CP, LANES), 1) % NZ
    has_lower = z_position >= 1
    has_upper = z_position <= NZ - 2
    low_half = lax.broadcasted_iota(jnp.int32, (CP, LANES), 1) < NZ
    tiles = width // LANES

    def prepare(index, stack):
        cells = load_row(index)
        for t in range(tiles):
            piece = cells[:, LANES * t : LANES * t + LANES]
            lower = jnp.where(has_lower, pltpu.roll(piece, 1, 1), 0.0)
            upper = jnp.where(has_upper, pltpu.roll(piece, LANES - 1, 1), 0.0)
            rows = jnp.concatenate([lower, piece, upper, jnp.zeros((8, LANES), F32)], axis=0)
            high, low = split(rows)
            stack[:128, LANES * t : LANES * t + LANES] = high
            stack[128:, LANES * t : LANES * t + LANES] = low

    def emit(row):
        sums = [[whole[36 * a : 36 * a + CP, LANES * t : LANES * t + LANES] for t in range(tiles)] for a in range(3)]
        out = []
        for t in range(tiles):
            low_part = sums[0][t]
            if t + 1 < tiles:
                low_part = low_part + sums[2][t + 1]
            high_part = sums[2][t]
            if t > 0:
                high_part = high_part + sums[0][t - 1]
            turned = pltpu.roll(jnp.where(low_half, low_part, high_part), NZ, 1)
            out.append(sums[1][t] + turned)
        finish(row, out)

    def step(index, here, there):
        prepare(jnp.minimum(index + 1, rows_in - 1), there)
        emit(jnp.maximum(index - 3, 0))
        for t in range(tiles // 2):
            lanes = slice(2 * LANES * t, 2 * LANES * t + 2 * LANES)
            terms = lax.dot_general(
                taps[...], here[:, lanes], (((1,), (0,)), ((), ())), preferred_element_type=F32
            )
            piece = []
            for b in range(3):
                high = terms[BLOCK * b : BLOCK * b + BLOCK]
                piece.append(high + terms[ROW + BLOCK * b : ROW + BLOCK * b + BLOCK])
            whole[:, lanes] = second_sum[:, lanes] + piece[2]
            second_sum[:, lanes] = first_sum[:, lanes] + piece[1]
            first_sum[:, lanes] = piece[0]

    def pair(j, carry):
        step(2 * j, stack_a, stack_b)
        step(2 * j + 1, stack_b, stack_a)
        return carry

    prepare(0, stack_a)
    lax.fori_loop(0, rows_in // 2, pair, 0)
    emit(rows_in - 3)


def conv_scratch(width):
    return [pltpu.VMEM((256, width), BF16)] * 2 + [pltpu.VMEM((BLOCK, width), F32)] * 3


def inside(place, first_x, sizes, width):
    cells_x, cells_y, full_x, full_y = sizes
    x = place[0] * cells_x + first_x + lax.broadcasted_iota(jnp.int32, (CP, width), 1) // NZ
    in_x = (x >= 0) & (x < full_x)

    def at(local_y):
        y = place[1] * cells_y + local_y
        return in_x & ((y >= 0) & (y < full_y))

    return at


def gather(sources, rows, target, first):
    width = sources[0].shape[2]
    count = rows.stop - rows.start
    return [
        (s.at[rows], target.at[slice(first, first + count), :, slice(width * i, width * i + width)])
        for i, s in enumerate(sources)
    ]


def join(sources, rows, target, first):
    width = sources[0].shape[2]
    count = rows.stop - rows.start
    for i, source in enumerate(sources):
        target[first : first + count, :, width * i : width * i + width] = source[rows]


def convolutions_body(sizes, before, left, own, right, after, place, taps, out_ref, *refs):
    rows, first, second = refs[:3]
    wide, narrow = refs[3:8], refs[8:]
    count = own.shape[0]
    rows[0:3] = before[...]
    join((left, own, right), slice(0, count), rows, 3)
    rows[3 + count :] = after[...]
    keep = inside(place, -2, sizes, 512)

    def finish_first(row, tiles):
        values = jnp.concatenate(tiles[1:5], axis=1)
        first[row] = jnp.where(keep(row - 2), gelu_exact(values), 0.0)

    def finish_second(row, tiles):
        values = jnp.concatenate(tiles, axis=1)
        second[row] = jnp.where(keep(row - 1), gelu_exact(values), 0.0)

    def finish_third(row, tiles):
        out_ref[row] = jnp.concatenate(tiles[1:3], axis=1)

    convolve_rows(lambda i: rows[i], count + 6, 768, taps.at[0], wide, finish_first)
    convolve_rows(lambda i: first[i], count + 4, 512, taps.at[1], narrow, finish_second)
    convolve_rows(lambda i: second[i], count + 2, 512, taps.at[2], narrow, finish_third)


def last_body(received, third, table, out_ref):
    spectrum = load_payload(received)[:, : third.shape[0] * CP]
    high, low = split(spectrum)

    def dot(left, right):
        return lax.dot_general(left, right, (((0,), (0,)), ((), ())), preferred_element_type=F32)

    spectral = dot(high, table[0]) + dot(low, table[0]) + dot(high, table[1])
    out = gelu_exact(spectral.reshape(third.shape) + third[...])
    channels, cells_x, width = out_ref.shape
    for x in range(cells_x):
        piece = [out[y, :channels, NZ * x : NZ * x + NZ] for y in range(width // NZ)]
        out_ref[:, x, :] = jnp.concatenate(piece, axis=1)


def shift(values, axis, step):
    count = lax.axis_size(axis)
    pairs = [(i, i + step) for i in range(count) if 0 <= i + step < count]
    return lax.ppermute(values, axis, pairs)


def shards(field, mix_weights, kept_z, conv_kernels):
    channels = field.shape[0]
    cells_x = field.shape[1]
    cells_y = field.shape[2] // NZ
    size_x = lax.axis_size("gx")
    size_y = lax.axis_size("gy")
    full_x, full_y = cells_x * size_x, cells_y * size_y
    modes_z = mix_weights.shape[3] * size_x
    kx_local = mix_weights.shape[4] // KY
    modes_x = kx_local * size_y
    place = jnp.stack([lax.axis_index("gx"), lax.axis_index("gy")]).astype(jnp.int32)
    z_in, x_in, y_in, y_out, x_out, z_out = [
        jnp.asarray(t) for t in tables(size_x, size_y, cells_x, cells_y, modes_x, modes_z)
    ]

    sizes = (cells_x, cells_y, full_x, full_y)
    grid, sent = call(
        z_in_body,
        (
            jax.ShapeDtypeStruct((cells_y, CP, cells_x * NZ), F32),
            jax.ShapeDtypeStruct((size_x, 24, LANES), F32),
        ),
        field, z_in,
        scratch=[pltpu.VMEM(field.shape, F32), pltpu.VMEM(z_in.shape, BF16), pltpu.SemaphoreType.DMA((2,))],
        hbm=(0, 1), vmem=FULL,
    )
    left = shift(grid, "gx", 1)
    right = shift(grid, "gx", -1)
    behind, _ = lax.optimization_barrier((place, sent))
    taps = call(
        taps_body, jax.ShapeDtypeStruct((3, 2 * ROW, 256), BF16), conv_kernels, behind,
        scratch=[pltpu.VMEM((128, 384), F32)], smem=(1,),
    )
    received = lax.all_to_all(sent, "gx", 0, 0, tiled=True)
    received, taps = lax.optimization_barrier((received, taps))

    sent = call(rows_body, jax.ShapeDtypeStruct((size_y, 24, LANES), F32), received, x_in)

    left, right, _ = lax.optimization_barrier((left, right, sent))
    received = lax.all_to_all(sent, "gy", 0, 0, tiled=True)

    def edge(rows):
        return jnp.concatenate([left[rows], grid[rows], right[rows]], axis=2)

    before = shift(edge(slice(cells_y - 3, cells_y)), "gy", 1)
    weights = mix_weights.reshape(2, channels * channels, kx_local * KY)
    sent = call(
        mix_body,
        jax.ShapeDtypeStruct((size_y, 24, LANES), F32),
        received, weights, kept_z.reshape(1, -1), place, y_in, y_out,
        scratch=[pltpu.VMEM((cells_y * size_y * kx_local * 2, LANES), F32)]
        + [pltpu.VMEM((LANES, kx_local * KY), F32)] * 2
        + [pltpu.VMEM(a.shape, a.dtype) for a in (received, weights, y_in, y_out)]
        + [pltpu.SemaphoreType.DMA((7,))],
        smem=(3,), hbm=(0, 1, 4, 5), vmem=FULL, flops=MIX << 20,
    )
    left, right, _ = lax.optimization_barrier((left, right, sent))
    after = shift(edge(slice(0, 3)), "gy", -1)
    received = lax.all_to_all(sent, "gy", 0, 0, tiled=True)
    sent = call(
        rows_body, jax.ShapeDtypeStruct((size_x, 24, LANES), F32), received, x_out, flops=XOUT << 20
    )
    before, after, _ = lax.optimization_barrier((before, after, sent))
    received = lax.all_to_all(sent, "gx", 0, 0, tiled=True)
    third = call(
        lambda *refs: convolutions_body(sizes, *refs),
        jax.ShapeDtypeStruct((cells_y, CP, cells_x * NZ), F32),
        before, left, grid, right, after, place, taps,
        scratch=[
            pltpu.VMEM((cells_y + 6, CP, 768), F32),
            pltpu.VMEM((cells_y + 4, CP, 512), F32),
            pltpu.VMEM((cells_y + 2, CP, 512), F32),
        ]
        + conv_scratch(768) + conv_scratch(512),
        smem=(5,), flops=CONV << 20,
    )
    return call(
        last_body, jax.ShapeDtypeStruct(field.shape, F32), received, third, z_out,
    )


def solution(mesh):
    placed = (P(None, "gx", "gy"), P(None, None, None, "gx", "gy"), P("gy"), P())
    return jax.shard_map(
        shards, mesh=mesh, in_specs=placed, out_specs=P(None, "gx", "gy"), check_vma=False
    )
```

```python
import math

import jax
import jax.numpy as jnp
import ml_dtypes
import numpy as np
from jax import lax
from jax.experimental import pallas as pl
from jax.experimental.pallas import tpu as pltpu
from jax.sharding import PartitionSpec as P

NZ = 64
KY = 32
MIX = 8192
XOUT = 8192
CONV = 12288
FULL = 60
CP = 40
LANES = 128
F32 = jnp.float32
BF16 = jnp.bfloat16


def split_table(table):
    high = table.astype(np.float32).astype(ml_dtypes.bfloat16)
    low = (table - high.astype(np.float64)).astype(np.float32).astype(ml_dtypes.bfloat16)
    return np.stack([high, low])


def split(values):
    high = values.astype(BF16)
    return high, (values - high.astype(F32)).astype(BF16)


def product(table, values, dims):
    high, low = split(values)
    numbers = (dims, ((), ()))

    def dot(left, right):
        return lax.dot_general(left, right, numbers, preferred_element_type=F32)

    return dot(table[0], high) + dot(table[0], low) + dot(table[1], high)


def frequencies(count, length):
    index = np.arange(count)
    return np.where(index < count // 2, index, length - count + index)


def tables(size_x, size_y, cells_x, cells_y, modes_x, modes_z):
    full_x, full_y = size_x * cells_x, size_y * cells_y
    scale_in = 1.0 / math.sqrt(full_x * full_y * NZ)
    scale_out = 1.0 / math.sqrt(modes_x * KY * modes_z)
    kx_local = modes_x // size_y
    z = np.arange(NZ)
    k = np.arange(modes_z)
    turn = 2.0 * np.pi * (np.outer(k, z) % NZ) / NZ
    eye_x = np.eye(cells_x)
    parts = np.stack([np.cos(turn), -np.sin(turn)], 1)
    z_in = np.einsum("kpz,xw->kpxwz", parts, eye_x).reshape(modes_z * 2 * cells_x, -1) * scale_in
    weight = np.where(k == 0, 1.0, 2.0)[:, None, None] * scale_out
    z_out = np.einsum("kpz,xw->kpxwz", parts * weight, eye_x).reshape(modes_z * 2 * cells_x, -1)

    def rotation(freq, positions, length):
        angle = 2.0 * np.pi * (np.outer(freq, positions) % length) / length
        cos, sin = np.cos(angle), np.sin(angle)
        return np.stack([np.stack([cos, -sin]), np.stack([sin, cos])])

    plus_x = rotation(frequencies(modes_x, full_x), np.arange(full_x), full_x)
    minus_x = plus_x.transpose(1, 0, 2, 3)
    x_in = minus_x.reshape(2, 2, modes_x, size_x, cells_x).transpose(2, 0, 3, 1, 4)
    x_in = x_in.reshape(modes_x * 2, -1)
    x_out = plus_x.reshape(2, 2, modes_x, size_x, cells_x).transpose(3, 0, 4, 2, 1)
    x_out = x_out.reshape(size_x * 2 * cells_x, -1)
    plus_y = rotation(frequencies(KY, full_y), np.arange(full_y), full_y)
    minus_y = plus_y.transpose(1, 0, 2, 3)
    eye_j = np.eye(kx_local)
    shape = (2, 2, KY, size_y, cells_y)
    y_in = np.einsum("pqlsy,jk->pjlyskq", minus_y.reshape(shape), eye_j)
    y_in = y_in.reshape(2 * kx_local * KY, -1)
    y_out = np.einsum("pqlsy,jk->ysjpqkl", plus_y.reshape(shape), eye_j)
    y_out = y_out.reshape(cells_y * size_y * kx_local * 2, -1)
    return [split_table(t) for t in (z_in, x_in, y_in, y_out, x_out, z_out)]


def call(body, out_shape, *args, scratch=(), flops=0, smem=(), hbm=(), out_hbm=(), vmem=24, light=False):
    def spec(index, kept):
        return pl.BlockSpec(memory_space=pl.ANY if index in kept else pltpu.VMEM)

    in_specs = [pl.BlockSpec(memory_space=pltpu.SMEM) if i in smem else spec(i, hbm) for i in range(len(args))]
    size = 0 if light else sum(a.size * a.dtype.itemsize for a in args)
    many = isinstance(out_shape, tuple)
    return pl.pallas_call(
        body,
        out_shape=out_shape,
        in_specs=in_specs,
        out_specs=tuple(spec(i, out_hbm) for i in range(len(out_shape))) if many else spec(0, out_hbm),
        scratch_shapes=list(scratch),
        compiler_params=pltpu.CompilerParams(vmem_limit_bytes=vmem << 20),
        cost_estimate=pl.CostEstimate(flops=flops, bytes_accessed=size, transcendentals=0),
    )(*args)


def copies(pairs, semaphores, first=0):
    started = [pltpu.make_async_copy(a, b, semaphores.at[first + i]) for i, (a, b) in enumerate(pairs)]
    for copy in started:
        copy.start()
    return started


def wait(started):
    for copy in started:
        copy.wait()


def store_payload(ref, rows):
    count = ref.shape[0]
    for tile in range(3):
        width = min(LANES, rows.shape[1] - LANES * tile)
        block = rows[:, LANES * tile : LANES * tile + width]
        ref[:, 8 * tile : 8 * tile + 8, :width] = block.reshape(count, 8, width)
        if width < LANES:
            ref[:, 8 * tile : 8 * tile + 8, width:] = jnp.zeros((count, 8, LANES - width), F32)


def load_payload(ref):
    count = ref.shape[0]
    tiles = [ref[:, 8 * t : 8 * t + 8, :].reshape(count * 8, LANES) for t in range(3)]
    return jnp.concatenate(tiles, axis=1)


def z_in_body(field_hbm, table_hbm, grid_ref, out_ref, field, table, sems):
    arrived = copies([(field_hbm, field), (table_hbm, table)], sems)
    wait(arrived[:1])
    channels, cells_x, width = field.shape
    for x in range(cells_x):
        piece = field[:, x, :]
        piece = jnp.concatenate([piece, jnp.zeros((CP - channels, width), F32)], axis=0)
        for y in range(width // NZ):
            grid_ref[y, :, NZ * x : NZ * x + NZ] = piece[:, NZ * y : NZ * y + NZ]
    cells = grid_ref[...].reshape(-1, grid_ref.shape[2])
    wait(arrived[1:])
    store_payload(out_ref, product(table, cells, ((1,), (1,))))


def rows_body(received, table, out_ref):
    rows = product(table, load_payload(received), ((1,), (0,)))
    for tile in range(3):
        block = rows[:, LANES * tile : LANES * tile + LANES]
        out_ref[:, 8 * tile : 8 * tile + 8, :] = block.reshape(out_ref.shape[0], 8, LANES)


def mix_body(received_hbm, weights_hbm, kept, place, y_in_hbm, y_out_hbm, out_ref, stacked, s_re, s_im, *refs):
    received, weights, y_in, y_out, sems = refs
    arrived = copies(
        [(received_hbm, received)]
        + [(y_in_hbm.at[i], y_in.at[i]) for i in range(2)]
        + [(weights_hbm.at[i], weights.at[i]) for i in range(2)]
        + [(y_out_hbm.at[i], y_out.at[i]) for i in range(2)],
        sems,
    )
    wait(arrived[:1])
    cells_y = received.shape[0]
    rows = load_payload(received)
    block = rows.shape[0]
    for y in range(cells_y):
        stacked[y * block : (y + 1) * block, :CP] = rows[:, CP * y : CP * y + CP]
        stacked[y * block : (y + 1) * block, CP:] = jnp.zeros((block, LANES - CP), F32)
    wait(arrived[1:3])
    modes = product(y_in, stacked[...], ((1,), (0,)))
    count = modes.shape[0] // 2
    s_re[...] = modes[:count].T
    s_im[...] = modes[count:].T
    channels = 36
    pair = 2 * channels
    row = lax.broadcasted_iota(jnp.int32, (8, count), 0)

    def spread(ref, c):
        first = jnp.broadcast_to(ref[c : c + 1, :], (8, count))
        second = jnp.broadcast_to(ref[c + 1 : c + 2, :], (8, count))
        middle = jnp.where(row < 4, first, second)
        return jnp.concatenate([first] * 4 + [middle] + [second] * 4, axis=0)

    wait(arrived[3:5])
    total_re = jnp.zeros((pair, count), F32)
    total_im = jnp.zeros((pair, count), F32)
    for c in range(0, channels, 2):
        w_re = weights[0, channels * c : channels * c + pair, :]
        w_im = weights[1, channels * c : channels * c + pair, :]
        f_re, f_im = spread(s_re, c), spread(s_im, c)
        total_re += w_re * f_re - w_im * f_im
        total_im += w_re * f_im + w_im * f_re
    keep = place[0] < kept[...]

    def fold(total):
        total = total[:channels] + total[channels:]
        return jnp.concatenate([jnp.where(keep, total, 0.0), jnp.zeros((CP - channels, count), F32)], axis=0)

    mixed = jnp.concatenate([fold(total_re), fold(total_im)], axis=1)
    wait(arrived[5:])
    back = product(y_out, mixed, ((1,), (1,)))
    lanes = jnp.concatenate([back[y * block : (y + 1) * block] for y in range(cells_y)], axis=1)
    store_payload(out_ref, lanes)


def gelu_exact(values):
    return 0.5 * values * (1.0 + lax.erf(values * math.sqrt(0.5)))


BLOCK = 112
ROW = 3 * BLOCK


def taps_body(kernels, after, out_ref, scratch):
    channels = kernels.shape[2]
    for r in range(3):
        scratch[...] = jnp.zeros(scratch.shape, F32)
        for tap in range(27):
            shift_x, shift_y, shift_z = tap // 9, tap // 3 % 3, tap % 3
            row, lane = CP * shift_z, BLOCK * shift_y + channels * shift_x
            scratch[row : row + channels, lane : lane + channels] = kernels[r, tap]
        high, low = split(scratch[...].T[:ROW])
        out_ref[r, :ROW, :128] = high
        out_ref[r, :ROW, 128:] = high
        out_ref[r, ROW:, :128] = low
        out_ref[r, ROW:, 128:] = jnp.zeros((ROW, 128), BF16)


def convolve_rows(load_row, rows_in, width, taps, refs, finish, late=()):
    stack_a, stack_b, first_sum, second_sum, whole = refs
    z_position = lax.broadcasted_iota(jnp.int32, (CP, LANES), 1) % NZ
    has_lower = z_position >= 1
    has_upper = z_position <= NZ - 2
    low_half = lax.broadcasted_iota(jnp.int32, (CP, LANES), 1) < NZ
    tiles = width // LANES

    def prepare(index, stack):
        cells = load_row(index)
        for t in range(tiles):
            piece = cells[:, LANES * t : LANES * t + LANES]
            lower = jnp.where(has_lower, pltpu.roll(piece, 1, 1), 0.0)
            upper = jnp.where(has_upper, pltpu.roll(piece, LANES - 1, 1), 0.0)
            rows = jnp.concatenate([lower, piece, upper, jnp.zeros((8, LANES), F32)], axis=0)
            high, low = split(rows)
            stack[:128, LANES * t : LANES * t + LANES] = high
            stack[128:, LANES * t : LANES * t + LANES] = low

    def emit(row):
        sums = [[whole[36 * a : 36 * a + CP, LANES * t : LANES * t + LANES] for t in range(tiles)] for a in range(3)]
        out = []
        for t in range(tiles):
            low_part = sums[0][t]
            if t + 1 < tiles:
                low_part = low_part + sums[2][t + 1]
            high_part = sums[2][t]
            if t > 0:
                high_part = high_part + sums[0][t - 1]
            turned = pltpu.roll(jnp.where(low_half, low_part, high_part), NZ, 1)
            out.append(sums[1][t] + turned)
        finish(row, out)

    def step(index, here, there):
        prepare(jnp.minimum(index + 1, rows_in - 1), there)
        emit(jnp.maximum(index - 3, 0))
        for t in range(tiles // 2):
            lanes = slice(2 * LANES * t, 2 * LANES * t + 2 * LANES)
            terms = lax.dot_general(
                taps[...], here[:, lanes], (((1,), (0,)), ((), ())), preferred_element_type=F32
            )
            piece = []
            for b in range(3):
                high = terms[BLOCK * b : BLOCK * b + BLOCK]
                piece.append(high + terms[ROW + BLOCK * b : ROW + BLOCK * b + BLOCK])
            whole[:, lanes] = second_sum[:, lanes] + piece[2]
            second_sum[:, lanes] = first_sum[:, lanes] + piece[1]
            first_sum[:, lanes] = piece[0]

    def pair(j, carry):
        step(2 * j, stack_a, stack_b)
        step(2 * j + 1, stack_b, stack_a)
        return carry

    prepare(0, stack_a)
    middle = (rows_in - 4) // 2 if late else 0
    if late:
        lax.fori_loop(0, middle, pair, 0)
        wait(late)
    lax.fori_loop(middle, rows_in // 2, pair, 0)
    emit(rows_in - 3)


def conv_scratch(width):
    return [pltpu.VMEM((256, width), BF16)] * 2 + [pltpu.VMEM((BLOCK, width), F32)] * 3


def inside(place, first_x, sizes, width):
    cells_x, cells_y, full_x, full_y = sizes
    x = place[0] * cells_x + first_x + lax.broadcasted_iota(jnp.int32, (CP, width), 1) // NZ
    in_x = (x >= 0) & (x < full_x)

    def at(local_y):
        y = place[1] * cells_y + local_y
        return in_x & ((y >= 0) & (y < full_y))

    return at


def gather(sources, rows, target, first):
    width = sources[0].shape[2]
    count = rows.stop - rows.start
    return [
        (s.at[rows], target.at[slice(first, first + count), :, slice(width * i, width * i + width)])
        for i, s in enumerate(sources)
    ]


def join(sources, rows, target, first):
    width = sources[0].shape[2]
    count = rows.stop - rows.start
    for i, source in enumerate(sources):
        target[first : first + count, :, width * i : width * i + width] = source[rows]


def convolutions_body(sizes, before, left, own, right, after, place, taps, out_ref, *refs):
    rows, first, second, sems = refs[:4]
    wide, narrow = refs[4:9], refs[9:]
    count = own.shape[0]
    late = copies([(after, rows.at[3 + count : 6 + count])], sems)
    rows[0:3] = before[...]
    join((left, own, right), slice(0, count), rows, 3)
    keep = inside(place, -2, sizes, 512)

    def finish_first(row, tiles):
        values = jnp.concatenate(tiles[1:5], axis=1)
        first[row] = jnp.where(keep(row - 2), gelu_exact(values), 0.0)

    def finish_second(row, tiles):
        values = jnp.concatenate(tiles, axis=1)
        second[row] = jnp.where(keep(row - 1), gelu_exact(values), 0.0)

    def finish_third(row, tiles):
        out_ref[row] = jnp.concatenate(tiles[1:3], axis=1)

    convolve_rows(lambda i: rows[i], count + 6, 768, taps.at[0], wide, finish_first, late)
    convolve_rows(lambda i: first[i], count + 4, 512, taps.at[1], narrow, finish_second)
    convolve_rows(lambda i: second[i], count + 2, 512, taps.at[2], narrow, finish_third)


def last_body(received, third, table, out_ref):
    spectrum = load_payload(received)[:, : third.shape[0] * CP]
    high, low = split(spectrum)

    def dot(left, right):
        return lax.dot_general(left, right, (((0,), (0,)), ((), ())), preferred_element_type=F32)

    spectral = dot(high, table[0]) + dot(low, table[0]) + dot(high, table[1])
    out = gelu_exact(spectral.reshape(third.shape) + third[...])
    channels, cells_x, width = out_ref.shape
    for x in range(cells_x):
        piece = [out[y, :channels, NZ * x : NZ * x + NZ] for y in range(width // NZ)]
        out_ref[:, x, :] = jnp.concatenate(piece, axis=1)


def shift(values, axis, step):
    count = lax.axis_size(axis)
    pairs = [(i, i + step) for i in range(count) if 0 <= i + step < count]
    return lax.ppermute(values, axis, pairs)


def shards(field, mix_weights, kept_z, conv_kernels):
    channels = field.shape[0]
    cells_x = field.shape[1]
    cells_y = field.shape[2] // NZ
    size_x = lax.axis_size("gx")
    size_y = lax.axis_size("gy")
    full_x, full_y = cells_x * size_x, cells_y * size_y
    modes_z = mix_weights.shape[3] * size_x
    kx_local = mix_weights.shape[4] // KY
    modes_x = kx_local * size_y
    place = jnp.stack([lax.axis_index("gx"), lax.axis_index("gy")]).astype(jnp.int32)
    z_in, x_in, y_in, y_out, x_out, z_out = [
        jnp.asarray(t) for t in tables(size_x, size_y, cells_x, cells_y, modes_x, modes_z)
    ]

    sizes = (cells_x, cells_y, full_x, full_y)
    grid, sent = call(
        z_in_body,
        (
            jax.ShapeDtypeStruct((cells_y, CP, cells_x * NZ), F32),
            jax.ShapeDtypeStruct((size_x, 24, LANES), F32),
        ),
        field, z_in,
        scratch=[pltpu.VMEM(field.shape, F32), pltpu.VMEM(z_in.shape, BF16), pltpu.SemaphoreType.DMA((2,))],
        hbm=(0, 1), vmem=FULL,
    )
    left = shift(grid, "gx", 1)
    right = shift(grid, "gx", -1)
    behind, _ = lax.optimization_barrier((place, sent))
    taps = call(
        taps_body, jax.ShapeDtypeStruct((3, 2 * ROW, 256), BF16), conv_kernels, behind,
        scratch=[pltpu.VMEM((128, 384), F32)], smem=(1,),
    )
    received = lax.all_to_all(sent, "gx", 0, 0, tiled=True)
    received, taps = lax.optimization_barrier((received, taps))

    sent = call(rows_body, jax.ShapeDtypeStruct((size_y, 24, LANES), F32), received, x_in)

    left, right, _ = lax.optimization_barrier((left, right, sent))
    received = lax.all_to_all(sent, "gy", 0, 0, tiled=True)

    def edge(rows):
        return jnp.concatenate([left[rows], grid[rows], right[rows]], axis=2)

    before = shift(edge(slice(cells_y - 3, cells_y)), "gy", 1)
    weights = mix_weights.reshape(2, channels * channels, kx_local * KY)
    sent = call(
        mix_body,
        jax.ShapeDtypeStruct((size_y, 24, LANES), F32),
        received, weights, kept_z.reshape(1, -1), place, y_in, y_out,
        scratch=[pltpu.VMEM((cells_y * size_y * kx_local * 2, LANES), F32)]
        + [pltpu.VMEM((LANES, kx_local * KY), F32)] * 2
        + [pltpu.VMEM(a.shape, a.dtype) for a in (received, weights, y_in, y_out)]
        + [pltpu.SemaphoreType.DMA((7,))],
        smem=(3,), hbm=(0, 1, 4, 5), vmem=FULL, flops=MIX << 20,
    )
    left, right, _ = lax.optimization_barrier((left, right, sent))
    after = shift(edge(slice(0, 3)), "gy", -1)
    received = lax.all_to_all(sent, "gy", 0, 0, tiled=True)
    sent = call(
        rows_body, jax.ShapeDtypeStruct((size_x, 24, LANES), F32), received, x_out, flops=XOUT << 20
    )
    before, after, _ = lax.optimization_barrier((before, after, sent))
    received = lax.all_to_all(sent, "gx", 0, 0, tiled=True)
    third = call(
        lambda *refs: convolutions_body(sizes, *refs),
        jax.ShapeDtypeStruct((cells_y, CP, cells_x * NZ), F32),
        before, left, grid, right, after, place, taps,
        scratch=[
            pltpu.VMEM((cells_y + 6, CP, 768), F32),
            pltpu.VMEM((cells_y + 4, CP, 512), F32),
            pltpu.VMEM((cells_y + 2, CP, 512), F32),
            pltpu.SemaphoreType.DMA((1,)),
        ]
        + conv_scratch(768) + conv_scratch(512),
        smem=(5,), hbm=(4,), flops=CONV << 20,
    )
    return call(
        last_body, jax.ShapeDtypeStruct(field.shape, F32), received, third, z_out,
    )


def solution(mesh):
    placed = (P(None, "gx", "gy"), P(None, None, None, "gx", "gy"), P("gy"), P())
    return jax.shard_map(
        shards, mesh=mesh, in_specs=placed, out_specs=P(None, "gx", "gy"), check_vma=False
    )
```
